32 devices in a mesh: fsdp: 4 (over y, core), dp: 8 (over z, x).
Axes of the slice: x: 2, y: 2, z: 4, core: 2. Of those that a mesh axis runs over, the one named last changes fastest.
Arguments:
- tokens: bfloat16 [8, 2048, 768], P('fsdp', 'dp'), may hold values from -6 to 6
- segments: int32 [8, 2048], P('fsdp'), may hold values from 0 to 2, never falling along the last dimension, each value on 1 to 2000 neighbouring positions
- ln1_gain: bfloat16 [768], P('fsdp'), may hold values from 0.5 to 1.5
- ln1_bias: bfloat16 [768], P('fsdp'), may hold values from -1.75 to 1.75
- w_query: bfloat16 [768, 768], P('fsdp'), may hold values from -0.21875 to 0.21875
- w_key: bfloat16 [768, 768], P('fsdp'), may hold values from -0.21875 to 0.21875
- w_value: bfloat16 [768, 768], P('fsdp'), may hold values from -0.21875 to 0.21875
- shift_taps: bfloat16 [64, 768], P(None, 'fsdp'), may hold values from -0.75 to 0.75
- ssm_rate: bfloat16 [12, 32], P('fsdp'), may hold values from 0.0009994507 to 0.099609375
- ssm_freq: bfloat16 [12, 32], P('fsdp'), may hold values from -0.29882812 to 0.29882812
- ssm_coef: bfloat16 [2, 12, 32], P(None, 'fsdp'), may hold values from -0.01171875 to 0.01171875
- ssm_skip: bfloat16 [12], P('fsdp'), may hold values from -0.625 to 0.625
- w_out: bfloat16 [768, 768], P('fsdp'), may hold values from -0.21875 to 0.21875
- ln2_gain: bfloat16 [768], P('fsdp'), may hold values from 0.5 to 1.5
- ln2_bias: bfloat16 [768], P('fsdp'), may hold values from -1.75 to 1.75
- w_up: bfloat16 [768, 3072], P('fsdp'), may hold values from -0.21875 to 0.21875
- w_down: bfloat16 [3072, 768], P('fsdp'), may hold values from -0.109375 to 0.109375
- cotangent: bfloat16 [8, 2048, 768], P('fsdp', 'dp'), may hold values from -6 to 6
Outputs:
- output: bfloat16 [8, 2048, 768], P('fsdp', 'dp')
- input_grad: bfloat16 [8, 2048, 768], P('fsdp', 'dp')
- ln1_gain_grad: float32 [768], P('fsdp')
- ln1_bias_grad: float32 [768], P('fsdp')
- w_query_grad: float32 [768, 768], P('fsdp')
- w_key_grad: float32 [768, 768], P('fsdp')
- w_value_grad: float32 [768, 768], P('fsdp')
- shift_taps_grad: float32 [64, 768], P(None, 'fsdp')
- ssm_rate_grad: float32 [12, 32], P('fsdp')
- ssm_freq_grad: float32 [12, 32], P('fsdp')
- ssm_coef_grad: float32 [2, 12, 32], P(None, 'fsdp')
- ssm_skip_grad: float32 [12], P('fsdp')
- w_out_grad: float32 [768, 768], P('fsdp')
- ln2_gain_grad: float32 [768], P('fsdp')
- ln2_bias_grad: float32 [768], P('fsdp')
- w_up_grad: float32 [768, 3072], P('fsdp')
- w_down_grad: float32 [3072, 768], P('fsdp')
The draws below stay inside these ranges and needn't reach their ends.
Inputs may be any that keep to these rules, and one draw needn't show every extreme that they name: `segments`: along each row the document numbers never fall; each document has 1 to 2000 tokens and some document in each row exactly 2000.
All inputs are finite; a program needn't handle non-finite values.
Results may differ from the reference program's by a relative error of at most 0.014.
Values may be sent and summed in bfloat16 or wider, within the bound.
No kernel may reach another device: no remote copies, remote signals or barrier semaphores. Data moves between devices by JAX's collectives and lax.ppermute only.
A program may use at most 256 MiB of HBM per device.

```python
import math
import jax
import jax.numpy as jnp
import numpy as np
from jax import lax

D = 768
FF = 3072
HEADS = 12
MODES = 32
SHIFT = 64
TOK = 256
DOC_MAX = 2000
HOPS = 8
KW = 2304
LEN = 2048
BATCH = 8
DOCS = 3


def shard_levels(stream_key, extent, pieces, smallest, largest):
    def one(dim, parts):
        steps = jax.random.uniform(jax.random.fold_in(jax.random.fold_in(stream_key, 6), dim), (parts,), jnp.float32, smallest / len(pieces), largest / len(pieces))
        return jnp.repeat(jnp.exp(steps), extent[dim] // parts).reshape((-1,) + (1,) * (len(extent) - dim - 1))

    gain = one(*pieces[0])
    for cut in pieces[1:]:
        gain = gain * one(*cut)
    return gain


def profile(amount, total, limit, lean):
    loads = [(1 << 20) // math.isqrt(grade ** lean) + 1 for grade in range(2, amount + 1)]
    rest, given = total - limit - (amount - 1), [1] * (amount - 1)
    while rest > 0:
        movable = [i for i in range(amount - 1) if given[i] < limit]
        whole, budget = sum([loads[i] for i in movable]), rest
        for i in movable:
            more = min(limit - given[i], max(1, budget * loads[i] // whole), rest)
            given[i] = given[i] + more
            rest = rest - more
    return np.array([limit] + given)


def ragged(key, amount, total, most, skew):
    if amount == 2:
        one = jax.random.randint(key, (), max(1, total - most), min(most, total - 1) + 1)
        return jnp.stack([one, total - one])
    lengths = jnp.asarray(profile(amount, total, most, skew), jnp.int32)
    pairs = (amount - 1) // 2
    donor, sink = lengths[1:1 + 2 * pairs:2], lengths[2:2 + 2 * pairs:2]
    room = jnp.minimum(donor - 1, most - sink)
    passed = jax.random.randint(jax.random.fold_in(key, 1), (pairs,), 0, 1 << 20) % (room + 1)
    lengths = lengths.at[1:1 + 2 * pairs:2].set(donor - passed).at[2:2 + 2 * pairs:2].set(sink + passed)
    return lengths[jax.random.permutation(jax.random.fold_in(key, 2), amount)]


def scatter_about(own_key, dims, deviation, limit, pieces=(), dtype=jnp.bfloat16):
    drawn = jax.random.normal(own_key, dims, jnp.float32) * deviation
    if len(pieces) > 0:
        drawn = shard_levels(own_key, dims, pieces, -0.22, 0.18) * drawn
    return jnp.clip(drawn, min=-limit, max=limit).astype(dtype)


def setup_inputs(seed: int = 0) -> dict:
    arg_keys = jax.random.split(jax.random.key(seed), 19)
    tokens = scatter_about(arg_keys[0], (BATCH, LEN, D), 1.0, 6.0, ((0, 4), (1, 8)))
    segments = jax.vmap(lambda own: jnp.searchsorted(jnp.cumsum(ragged(own, DOCS, LEN, DOC_MAX, 1)), jnp.arange(LEN), side="right"))(jax.random.split(arg_keys[1], BATCH)).reshape((BATCH, LEN)).astype(jnp.int32)
    ln1_gain = jnp.clip(1.0 + 0.1 * jax.random.normal(arg_keys[2], (D,), jnp.float32), 0.5, 1.5).astype(jnp.bfloat16)
    ln1_bias = scatter_about(arg_keys[3], (D,), 0.3, 1.75, ((0, 4),))
    w_query = scatter_about(arg_keys[4], (D, D), D ** -0.5, 0.21875, ((0, 4),))
    w_key = scatter_about(arg_keys[5], (D, D), D ** -0.5, 0.21875, ((0, 4),))
    w_value = scatter_about(arg_keys[6], (D, D), D ** -0.5, 0.21875, ((0, 4),))
    shift_taps = scatter_about(arg_keys[7], (SHIFT, D), SHIFT ** -0.5, 0.75, ((1, 4),))
    ssm_rate = jnp.clip(jnp.exp(math.log(0.099609375) - 4.6018058 * jax.random.uniform(arg_keys[8], (HEADS, MODES), jnp.float32) ** shard_levels(arg_keys[8], (HEADS, MODES), ((0, 4),), -0.2, 0.2)), 0.0009994507, 0.099609375).astype(jnp.bfloat16)
    ssm_freq = jnp.clip(jax.random.uniform(arg_keys[9], (HEADS, MODES), jnp.float32, -0.29882812, 0.29882812) * shard_levels(arg_keys[9], (HEADS, MODES), ((0, 4),), -0.4, 0.0), -0.29882812, 0.29882812).astype(jnp.bfloat16)
    ssm_coef = scatter_about(arg_keys[10], (2, HEADS, MODES), 0.002, 0.01171875, ((1, 4),))
    ssm_skip = scatter_about(arg_keys[11], (HEADS,), 0.1, 0.625, ((0, 4),))
    w_out = scatter_about(arg_keys[12], (D, D), D ** -0.5, 0.21875, ((0, 4),))
    ln2_gain = jnp.clip(1.0 + 0.1 * jax.random.normal(arg_keys[13], (D,), jnp.float32), 0.5, 1.5).astype(jnp.bfloat16)
    ln2_bias = scatter_about(arg_keys[14], (D,), 0.3, 1.75, ((0, 4),))
    w_up = scatter_about(arg_keys[15], (D, FF), D ** -0.5, 0.21875, ((0, 4),))
    w_down = scatter_about(arg_keys[16], (FF, D), FF ** -0.5, 0.109375, ((0, 4),))
    cotangent = scatter_about(arg_keys[17], (BATCH, LEN, D), 1.0, 6.0, ((0, 4), (1, 8)))
    return {"tokens": tokens, "segments": segments, "ln1_gain": ln1_gain, "ln1_bias": ln1_bias, "w_query": w_query, "w_key": w_key, "w_value": w_value, "shift_taps": shift_taps, "ssm_rate": ssm_rate, "ssm_freq": ssm_freq, "ssm_coef": ssm_coef, "ssm_skip": ssm_skip, "w_out": w_out, "ln2_gain": ln2_gain, "ln2_bias": ln2_bias, "w_up": w_up, "w_down": w_down, "cotangent": cotangent}


@jax.custom_vjp
def low(v):
    return lax.optimization_barrier(v.astype(jnp.bfloat16)).astype(jnp.float32)

@jax.custom_vjp
def low_back(v):
    return v

def low_keep(v):
    return (low(v), None)

def low_pass(kept, grad):
    return (grad,)

def back_keep(v):
    return (v, None)

def back_low(kept, grad):
    return (low(grad),)
low.defvjp(low_keep, low_pass)
low_back.defvjp(back_keep, back_low)
highest = lax.Precision.HIGHEST
epsilon = 1e-05

def layer_norm(inputs, scales, offsets):
    row_mean = lax.optimization_barrier(jnp.mean(inputs, axis=-1, keepdims=True))
    centered = inputs - row_mean
    spread = lax.optimization_barrier(jnp.mean(centered * centered, axis=-1, keepdims=True))
    return centered * lax.rsqrt(spread + epsilon) * scales + offsets

def matmul(left, right):
    return jnp.dot(left, right, precision=highest, preferred_element_type=jnp.float32)

def kernel_table(decay_rate, frequency, coefficients, skip_gain):
    lag_values = jnp.arange(KW).astype(jnp.float32)
    decays = jnp.exp(-decay_rate[:, :, None] * lag_values)
    angles = frequency[:, :, None] * lag_values
    oscillation = coefficients[0][:, :, None] * jnp.cos(angles) - coefficients[1][:, :, None] * jnp.sin(angles)
    first_lag = (jnp.arange(KW) == 0).astype(jnp.float32)
    return lax.optimization_barrier(jnp.sum(decays * oscillation, axis=1)) + skip_gain[:, None] * first_lag

def one_sequence(inputs, seg_row, params):
    gain_one, bias_one, query_w, key_w, value_w, taps_w, decay_rate, frequency, coefficients, skip_gain, out_w, gain_two, bias_two, up_w, down_w = params
    heads = decay_rate.shape[0]
    head_size = D // heads
    block_count = LEN // TOK
    act_one = low(layer_norm(inputs, gain_one, bias_one))
    queries = low_back(low(matmul(act_one, query_w)))
    key_rows = low(low_back(matmul(act_one, key_w)))
    values = low(low_back(matmul(act_one, value_w)))
    key_pad = jnp.concatenate([jnp.zeros((SHIFT - 1, D), jnp.float32), key_rows], axis=0)
    seg_short = jnp.concatenate([jnp.full((SHIFT - 1,), -1, jnp.int32), seg_row], axis=0)

    def shift_block(block_index):
        offset = (block_index * TOK).astype(jnp.int32)
        window = lax.dynamic_slice_in_dim(key_pad, offset, TOK + SHIFT - 1, 0)
        seg_window = lax.dynamic_slice_in_dim(seg_short, offset, TOK + SHIFT - 1, 0)
        seg_now = seg_window[SHIFT - 1:]
        running = jnp.zeros((TOK, D), jnp.float32)
        for tap_lag in range(SHIFT):
            first_row = SHIFT - 1 - tap_lag
            same_doc = seg_window[first_row:first_row + TOK] == seg_now
            running = running + jnp.where(same_doc[:, None], window[first_row:first_row + TOK], 0.0) * taps_w[tap_lag]
        return running
    blocks = jnp.arange(block_count).astype(jnp.int32)
    shifted = low(lax.map(jax.checkpoint(shift_block), blocks).reshape(LEN, D))
    reach_rows = HOPS * TOK
    key_wide = jnp.concatenate([jnp.zeros((reach_rows, D), jnp.float32), shifted], axis=0)
    value_wide = jnp.concatenate([jnp.zeros((reach_rows, D), jnp.float32), values], axis=0)
    seg_wide = jnp.concatenate([jnp.full((reach_rows,), -1, jnp.int32), seg_row], axis=0)
    kernel_rows = kernel_table(decay_rate, frequency, coefficients, skip_gain)
    lag_index = lax.broadcasted_iota(jnp.int32, (TOK, KW), 0) + reach_rows - lax.broadcasted_iota(jnp.int32, (TOK, KW), 1)
    kernel_mat = jnp.take(kernel_rows, jnp.clip(lag_index, 0, KW - 1), axis=1)

    def mix_block(block_index):
        offset = (block_index * TOK).astype(jnp.int32)
        q_block = lax.dynamic_slice_in_dim(queries, offset, TOK, 0).reshape(TOK, heads, head_size)
        k_block = lax.dynamic_slice_in_dim(key_wide, offset, KW, 0).reshape(KW, heads, head_size)
        v_block = lax.dynamic_slice_in_dim(value_wide, offset, KW, 0).reshape(KW, heads, head_size)
        seg_keys = lax.dynamic_slice_in_dim(seg_wide, offset, KW, 0)
        seg_now = lax.dynamic_slice_in_dim(seg_row, offset, TOK, 0)
        live_mask = (seg_now[:, None] == seg_keys[None, :]) & (lag_index >= 0)
        scores = low_back(jnp.einsum('thd,uhd->htu', q_block, k_block, precision=highest))
        weights = low(jnp.where(live_mask[None], scores * kernel_mat, 0.0))
        return jnp.einsum('htu,uhe->the', weights, v_block, precision=highest).reshape(TOK, D)
    mixed = low(low_back(lax.map(jax.checkpoint(mix_block), blocks).reshape(LEN, D)))
    resid = inputs + low_back(matmul(mixed, out_w))
    act_two = low(layer_norm(resid, gain_two, bias_two))
    hidden = low(jax.nn.gelu(low_back(matmul(act_two, up_w)), approximate=True))
    return resid + matmul(hidden, down_w)

def reference(tokens, segments, ln1_gain, ln1_bias, w_query, w_key, w_value, shift_taps, ssm_rate, ssm_freq, ssm_coef, ssm_skip, w_out, ln2_gain, ln2_bias, w_up, w_down, cotangent):
    params = tuple((p.astype(jnp.float32) for p in (ln1_gain, ln1_bias, w_query, w_key, w_value, shift_taps, ssm_rate, ssm_freq, ssm_coef, ssm_skip, w_out, ln2_gain, ln2_bias, w_up, w_down)))
    inputs = tokens.astype(jnp.float32)

    def forward(inputs, *weights):

        def one_pair(seq_pair):
            return one_sequence(seq_pair[0], seq_pair[1], weights)
        return lax.map(jax.checkpoint(one_pair), (inputs, segments))
    result, pullback = jax.vjp(forward, inputs, *params)
    gradients = pullback(cotangent.astype(jnp.float32))
    return (result.astype(jnp.bfloat16), gradients[0].astype(jnp.bfloat16), gradients[1], gradients[2], gradients[3], gradients[4], gradients[5], gradients[6], gradients[7], gradients[8], gradients[9], gradients[10], gradients[11], gradients[12], gradients[13], gradients[14], gradients[15])
```

```python
import functools

import jax
import jax.numpy as jnp
import numpy as np
from jax import lax
from jax.experimental import pallas as pl
from jax.experimental.pallas import tpu as pltpu
from jax.sharding import PartitionSpec as P

SHIFT = 64
HOPS = 8
TILE = 256
HALO = 64
EPS = 1e-05
BF = jnp.bfloat16
F32 = jnp.float32
VMEM_BYTES = 56 * 1024 * 1024


def vmem():
    return pl.BlockSpec(memory_space=pltpu.VMEM)


def smem():
    return pl.BlockSpec(memory_space=pltpu.SMEM)


def params():
    return pltpu.CompilerParams(vmem_limit_bytes=VMEM_BYTES)


def mm(left, right):
    return lax.dot_general(left, right, (((1,), (0,)), ((), ())), preferred_element_type=F32)


def mm_nt(left, right):
    return lax.dot_general(left, right, (((1,), (1,)), ((), ())), preferred_element_type=F32)


def lane_tiles(width):
    return [(base, min(128, width - base)) for base in range(0, width, 128)]


def fill_ext(ext_ref, first_row, rows, source_ref, width):
    for index, (base, size) in enumerate(lane_tiles(width)):
        if size < 128:
            ext_ref[index, pl.ds(first_row, rows), :] = jnp.zeros((rows, 128), F32)
        ext_ref[index, pl.ds(first_row, rows), 0:size] = source_ref[:, base : base + size].astype(F32)


def shift_fwd_kernel(seg_s, k_ref, halo_ref, taps_ref, segcol_ref, out_ref, ext, seg_b):
    rows, width = k_ref.shape
    fill_ext(ext, 0, HALO, halo_ref, width)
    fill_ext(ext, HALO, rows, k_ref, width)
    seg_b[...] = jnp.broadcast_to(segcol_ref[...], seg_b.shape)
    for index, (base, size) in enumerate(lane_tiles(width)):

        def tap_row(lag):
            return taps_ref[index, lag : lag + 1, :]

        def body(tile, carry):
            start = pl.multiple_of(tile * 64, 64)

            def plain():
                total = jnp.zeros((64, 128), F32)
                for lag in range(SHIFT):
                    total = total + ext[index, pl.ds(start + HALO - lag, 64), :] * tap_row(lag)
                return total

            def masked():
                total = jnp.zeros((64, 128), F32)
                now = seg_b[pl.ds(start + HALO, 64), :]
                for lag in range(SHIFT):
                    same = seg_b[pl.ds(start + HALO - lag, 64), :] == now
                    part = ext[index, pl.ds(start + HALO - lag, 64), :] * tap_row(lag)
                    total = total + jnp.where(same, part, 0.0)
                return total

            total = lax.cond(seg_s[start + 1] == seg_s[start + HALO + 63], plain, masked)
            out_ref[pl.ds(start, 64), base : base + size] = total[:, 0:size].astype(BF)
            return carry

        lax.fori_loop(0, rows // 64, body, 0)


def shift_fwd(seg_full, k_own, k_halo, taps):
    rows, width = k_own.shape
    tiles = len(lane_tiles(width))
    return pl.pallas_call(
        shift_fwd_kernel,
        out_shape=jax.ShapeDtypeStruct((rows, width), BF),
        in_specs=[smem(), vmem(), vmem(), vmem(), vmem()],
        out_specs=vmem(),
        scratch_shapes=[
            pltpu.VMEM((tiles, HALO + rows, 128), F32),
            pltpu.VMEM((HALO + rows, 128), jnp.int32),
        ],
        compiler_params=params(),
        name="shift_fwd",
    )(seg_full, k_own, k_halo, taps, seg_full[: HALO + rows, None])


def shift_bwd_kernel(
    seg_s, k_ref, halo_ref, g_ref, ghalo_ref, taps_ref, segcol_ref, gk_ref, tg_ref, ext, gext, seg_b, acc
):
    rows, width = k_ref.shape
    fill_ext(ext, 0, HALO, halo_ref, width)
    fill_ext(ext, HALO, rows, k_ref, width)
    fill_ext(gext, 0, rows, g_ref, width)
    fill_ext(gext, rows, HALO, ghalo_ref, width)
    seg_b[...] = jnp.broadcast_to(segcol_ref[...], seg_b.shape)
    acc[...] = jnp.zeros_like(acc)
    for index, (base, size) in enumerate(lane_tiles(width)):

        def tap_row(lag):
            return taps_ref[index, lag : lag + 1, :]

        def fold(part):
            total = part[0:8]
            for piece in range(1, 8):
                total = total + part[8 * piece : 8 * piece + 8]
            return total

        def body(tile, carry):
            start = pl.multiple_of(tile * 64, 64)

            def plain():
                total = jnp.zeros((64, 128), F32)
                for lag in range(SHIFT):
                    total = total + gext[index, pl.ds(start + lag, 64), :] * tap_row(lag)
                return total

            def masked():
                total = jnp.zeros((64, 128), F32)
                now = seg_b[pl.ds(start + HALO, 64), :]
                for lag in range(SHIFT):
                    same = seg_b[pl.ds(start + HALO + lag, 64), :] == now
                    part = gext[index, pl.ds(start + lag, 64), :] * tap_row(lag)
                    total = total + jnp.where(same, part, 0.0)
                return total

            total = lax.cond(seg_s[start + HALO] == seg_s[start + HALO + 126], plain, masked)
            gk_ref[pl.ds(start, 64), base : base + size] = total[:, 0:size].astype(BF)
            grad = gext[index, pl.ds(start, 64), :]
            clear = seg_s[start + 1] == seg_s[start + HALO + 63]

            @pl.when(clear)
            def _():
                for lag in range(SHIFT):
                    part = ext[index, pl.ds(start + HALO - lag, 64), :] * grad
                    acc[index, lag] = acc[index, lag] + fold(part)

            @pl.when(jnp.logical_not(clear))
            def _():
                now = seg_b[pl.ds(start + HALO, 64), :]
                for lag in range(SHIFT):
                    same = seg_b[pl.ds(start + HALO - lag, 64), :] == now
                    part = ext[index, pl.ds(start + HALO - lag, 64), :] * grad
                    acc[index, lag] = acc[index, lag] + fold(jnp.where(same, part, 0.0))

            return carry

        lax.fori_loop(0, rows // 64, body, 0)
        tg_ref[:, base : base + size] = jnp.sum(acc[index], axis=1)[:, 0:size]


def shift_bwd(seg_full, k_own, k_halo, grad, grad_halo, taps):
    rows, width = k_own.shape
    tiles = len(lane_tiles(width))
    return pl.pallas_call(
        shift_bwd_kernel,
        out_shape=(jax.ShapeDtypeStruct((rows, width), BF), jax.ShapeDtypeStruct((SHIFT, width), F32)),
        in_specs=[smem()] + [vmem()] * 6,
        out_specs=(vmem(), vmem()),
        scratch_shapes=[
            pltpu.VMEM((tiles, HALO + rows, 128), F32),
            pltpu.VMEM((tiles, HALO + rows, 128), F32),
            pltpu.VMEM((2 * HALO + rows, 128), jnp.int32),
            pltpu.VMEM((tiles, SHIFT, 8, 128), F32),
        ],
        compiler_params=params(),
        name="shift_bwd",
    )(seg_full, k_own, k_halo, grad, grad_halo, taps, seg_full[:, None])


def tile_table(query_blocks, key_blocks, unroll):
    offset = key_blocks - query_blocks
    pairs = []
    for distance in range(HOPS + 1):
        for row in range(query_blocks):
            if row + offset - distance >= 0:
                pairs.append((row, row + offset - distance))
    assert len(pairs) % unroll == 0
    return np.array(pairs, np.int32)


def build_bands(bands, row):
    length = row.shape[1]
    skewed = pltpu.roll(jnp.broadcast_to(row, (8, length)), 0, 1, stride=1, stride_axis=0)
    for step in range(16):
        bands[step] = pltpu.roll(skewed, 8 * step, 1) if step else skewed


def read_band(bands, first, second):
    upper = bands[:, :, pl.ds(first, TILE)].reshape(128, TILE)
    lower = bands[:, :, pl.ds(second, TILE)].reshape(128, TILE)
    return jnp.concatenate([upper, lower], axis=0)


def split_heads(dest, source, heads, size):
    for head in range(heads):
        dest[head] = source[:, head * size : (head + 1) * size]


UNROLL_F = 4
UNROLL_B = 2


def mix_fwd_kernel(tab, q_ref, k_ref, v_ref, row_ref, segq_ref, segk_ref, y_ref, qh, kh, vh, yacc, bands, seg_b):
    heads, length = row_ref.shape[0], row_ref.shape[2]
    size = q_ref.shape[1] // heads
    offset = (k_ref.shape[0] - q_ref.shape[0]) // TILE
    tiles = tab.shape[0]
    split_heads(qh, q_ref, heads, size)
    split_heads(kh, k_ref, heads, size)
    split_heads(vh, v_ref, heads, size)
    seg_b[...] = jnp.broadcast_to(segq_ref[...], seg_b.shape)
    yacc[...] = jnp.zeros_like(yacc)

    def head_body(head, carry):
        build_bands(bands, row_ref[head])

        def body(step, carry):
            for unrolled in range(UNROLL_F):
                row = tab[step * UNROLL_F + unrolled, 0]
                col = tab[step * UNROLL_F + unrolled, 1]
                rows = pl.ds(pl.multiple_of(row * TILE, TILE), TILE)
                cols = pl.ds(pl.multiple_of(col * TILE, TILE), TILE)
                base = pl.multiple_of((length - TILE) - TILE * (row + offset - col), TILE)
                kern = read_band(bands, base, pl.multiple_of(base - 128, 128))
                score = mm_nt(qh[head, rows, :], kh[head, cols, :])
                seg_now = seg_b[rows, :]
                live = jnp.concatenate([seg_now, seg_now], axis=1) == segk_ref[col]
                weight = jnp.where(live, score * kern, 0.0).astype(BF)
                yacc[head, rows, :] += mm(weight, vh[head, cols, :])
            return carry

        lax.fori_loop(0, tiles // UNROLL_F, body, 0)
        return carry

    lax.fori_loop(0, heads, head_body, 0)
    for head in range(heads):
        y_ref[:, head * size : (head + 1) * size] = yacc[head].astype(BF)


def mix_fwd(q, k_win, v_win, kern_desc, seg_q, seg_k):
    rows, width = q.shape
    wide = k_win.shape[0]
    heads, _, length = kern_desc.shape
    size = width // heads
    table = tile_table(rows // TILE, wide // TILE, UNROLL_F)
    return pl.pallas_call(
        mix_fwd_kernel,
        out_shape=jax.ShapeDtypeStruct((rows, width), BF),
        in_specs=[smem()] + [vmem()] * 6,
        out_specs=vmem(),
        scratch_shapes=[
            pltpu.VMEM((heads, rows, size), BF),
            pltpu.VMEM((heads, wide, size), BF),
            pltpu.VMEM((heads, wide, size), BF),
            pltpu.VMEM((heads, rows, size), F32),
            pltpu.VMEM((16, 8, length), F32),
            pltpu.VMEM((rows, 128), jnp.int32),
        ],
        compiler_params=params(),
        name="mix_fwd",
    )(table, q, k_win, v_win, kern_desc, seg_q[:, None], seg_k.reshape(wide // TILE, 1, TILE))


def mix_bwd_kernel(
    tab, q_ref, k_ref, v_ref, g_ref, row_ref, segq_ref, segk_ref, gq_ref, gk_ref, gv_ref, gkern_ref,
    qh, kh, vh, gh, kt, gqt, gkacc, gvacc, bands, gbands, seg_b,
):
    heads, length = row_ref.shape[0], row_ref.shape[2]
    size = q_ref.shape[1] // heads
    query_blocks, key_blocks = q_ref.shape[0] // TILE, k_ref.shape[0] // TILE
    offset = key_blocks - query_blocks
    tiles = tab.shape[0]
    split_heads(qh, q_ref, heads, size)
    split_heads(kh, k_ref, heads, size)
    split_heads(vh, v_ref, heads, size)
    split_heads(gh, g_ref, heads, size)
    for head in range(heads):
        for block in range(key_blocks):
            kt[head, block] = kh[head, block * TILE : (block + 1) * TILE, :].T
    seg_b[...] = jnp.broadcast_to(segk_ref[...], seg_b.shape)
    gqt[...] = jnp.zeros_like(gqt)
    gkacc[...] = jnp.zeros_like(gkacc)
    gvacc[...] = jnp.zeros_like(gvacc)

    def head_body(head, carry):
        build_bands(bands, row_ref[head])
        gbands[...] = jnp.zeros_like(gbands)

        def body(step, carry):
            for unrolled in range(UNROLL_B):
                row = tab[step * UNROLL_B + unrolled, 0]
                col = tab[step * UNROLL_B + unrolled, 1]
                rows = pl.ds(pl.multiple_of(row * TILE, TILE), TILE)
                cols = pl.ds(pl.multiple_of(col * TILE, TILE), TILE)
                first = pl.multiple_of(TILE + TILE * (row + offset - col), TILE)
                second = pl.multiple_of(first - 128, 128)
                kern = read_band(bands, first, second)
                q_now, g_now = qh[head, rows, :], gh[head, rows, :]
                score = mm_nt(kh[head, cols, :], q_now)
                grad = mm_nt(vh[head, cols, :], g_now)
                seg_now = seg_b[cols, :]
                live = jnp.concatenate([seg_now, seg_now], axis=1) == segq_ref[row]
                grad = jnp.where(live, grad, 0.0)
                weight = jnp.where(live, score * kern, 0.0).astype(BF)
                gscore = (grad * kern).astype(BF)
                both = grad * score
                gbands[:, :, pl.ds(first, TILE)] += both[0:128].reshape(16, 8, TILE)
                gbands[:, :, pl.ds(second, TILE)] += both[128:256].reshape(16, 8, TILE)
                gkacc[head, cols, :] += mm(gscore, q_now)
                gvacc[head, cols, :] += mm(weight, g_now)
                gqt[head, row] += mm(kt[head, col], gscore)
            return carry

        lax.fori_loop(0, tiles // UNROLL_B, body, 0)
        total = gbands[0]
        for step in range(1, 16):
            total = total + pltpu.roll(gbands[step], length - 8 * step, 1)
        line = total[0:1]
        for sub in range(1, 8):
            line = line + pltpu.roll(total, length - sub, 1)[sub : sub + 1]
        gkern_ref[head] = line
        return carry

    lax.fori_loop(0, heads, head_body, 0)
    for head in range(heads):
        lanes = slice(head * size, (head + 1) * size)
        for block in range(query_blocks):
            gq_ref[block * TILE : (block + 1) * TILE, lanes] = gqt[head, block].T.astype(BF)
        gk_ref[:, lanes] = gkacc[head]
        gv_ref[:, lanes] = gvacc[head].astype(gv_ref.dtype)


def mix_bwd(q, k_win, v_win, grad, kern_asc, seg_q, seg_k):
    rows, width = q.shape
    wide = k_win.shape[0]
    heads, _, length = kern_asc.shape
    size = width // heads
    table = tile_table(rows // TILE, wide // TILE, UNROLL_B)
    return pl.pallas_call(
        mix_bwd_kernel,
        out_shape=(
            jax.ShapeDtypeStruct((rows, width), BF),
            jax.ShapeDtypeStruct((wide, width), F32),
            jax.ShapeDtypeStruct((wide, width), BF if wide == rows else F32),
            jax.ShapeDtypeStruct((heads, 1, length), F32),
        ),
        in_specs=[smem()] + [vmem()] * 7,
        out_specs=(vmem(),) * 4,
        scratch_shapes=[
            pltpu.VMEM((heads, rows, size), BF),
            pltpu.VMEM((heads, wide, size), BF),
            pltpu.VMEM((heads, wide, size), BF),
            pltpu.VMEM((heads, rows, size), BF),
            pltpu.VMEM((heads, wide // TILE, size, TILE), BF),
            pltpu.VMEM((heads, rows // TILE, size, TILE), F32),
            pltpu.VMEM((heads, wide, size), F32),
            pltpu.VMEM((heads, wide, size), F32),
            pltpu.VMEM((16, 8, length), F32),
            pltpu.VMEM((16, 8, length), F32),
            pltpu.VMEM((wide, 128), jnp.int32),
        ],
        compiler_params=params(),
        name="mix_bwd",
    )(table, q, k_win, v_win, grad, kern_asc, seg_q.reshape(rows // TILE, 1, TILE), seg_k[:, None])


def xor_permute(value, axis, mask):
    count = lax.axis_size(axis)
    return lax.ppermute(value, axis, [(source, source ^ mask) for source in range(count)])


def gather_fsdp(shard):
    me = lax.axis_index("fsdp")
    across = xor_permute(shard, "fsdp", 2)
    beside = xor_permute(shard, "fsdp", 1)
    both = xor_permute(across, "fsdp", 1)
    full = jnp.zeros((4,) + shard.shape, shard.dtype)
    zero = (0,) * shard.ndim
    for mask, part in ((0, shard), (1, beside), (2, across), (3, both)):
        full = lax.dynamic_update_slice(full, part[None], (me ^ mask,) + zero)
    return full


def reduce_grad(partial, groups):
    me = lax.axis_index("fsdp")
    high, low = me // 2, me % 2
    rows, cols = partial.shape[1:]
    pairs = partial.reshape(2, 2, rows, cols)
    keep = lax.dynamic_index_in_dim(pairs, low, 1, keepdims=False)
    send = lax.dynamic_index_in_dim(pairs, 1 - low, 1, keepdims=False).astype(BF)
    total = keep + xor_permute(send, "fsdp", 1).astype(F32)
    keep = lax.dynamic_index_in_dim(total, high, 0, keepdims=False)
    send = lax.dynamic_index_in_dim(total, 1 - high, 0, keepdims=False).astype(BF)
    total = keep + xor_permute(send, "fsdp", 2).astype(F32)
    count = lax.axis_size("dp")
    split = total.astype(BF).reshape(count, rows // count, cols)
    owned = jnp.sum(lax.all_to_all(split, "dp", 0, 0).astype(F32), axis=0).astype(BF)
    spread = jnp.broadcast_to(owned[None], (count,) + owned.shape)
    return lax.all_to_all(spread, "dp", 0, 0).reshape(rows, cols).astype(F32)


def layer_norm(inputs, scales, offsets):
    row_mean = jnp.mean(inputs, axis=-1, keepdims=True)
    centered = inputs - row_mean
    spread = jnp.mean(centered * centered, axis=-1, keepdims=True)
    return centered * lax.rsqrt(spread + EPS) * scales + offsets


def kernel_rows(rate, freq, coef, skip, lags, reach):
    lag = lags.astype(F32)
    inside = (lags >= 0) & (lags < reach)
    clipped = jnp.where(inside, lag, 0.0)
    decay = jnp.exp(-rate[:, :, None] * clipped)
    angle = freq[:, :, None] * clipped
    wave = coef[0][:, :, None] * jnp.cos(angle) - coef[1][:, :, None] * jnp.sin(angle)
    first = (lags == 0).astype(F32)
    return jnp.where(inside, jnp.sum(decay * wave, axis=1) + skip[:, None] * first, 0.0)


def shards(
    tokens, segments, ln1_gain, ln1_bias, w_query, w_key, w_value, shift_taps, ssm_rate, ssm_freq,
    ssm_coef, ssm_skip, w_out, ln2_gain, ln2_bias, w_up, w_down, cotangent,
):
    seqs, rows, width = tokens.shape
    fsdp = lax.axis_size("fsdp")
    dp = lax.axis_size("dp")
    run = HOPS
    assert dp % run == 0 and rows == TILE and fsdp == 4
    me = lax.axis_index("dp")
    chunk, inner = me // run, me % run
    group_count = run // seqs
    share = width // group_count
    seq, group = inner // group_count, inner % group_count
    span = run * rows
    multi = dp > run
    groups = [list(range(base, base + run)) for base in range(0, dp, run)] if multi else None
    reach = HOPS * rows + rows

    def exchange(value):
        return lax.all_to_all(value, "dp", 0, 0, axis_index_groups=groups)

    def to_runs(value):
        split = value.reshape(seqs, rows, group_count, share).transpose(0, 2, 1, 3)
        return exchange(split.reshape(run, rows, share)).reshape(span, share)

    def from_runs(value):
        back = exchange(value.reshape(run, rows, share)).reshape(seqs, group_count, rows, share)
        return back.transpose(0, 2, 1, 3).reshape(seqs * rows, width)

    def from_prev(value):
        if not multi:
            return jnp.zeros_like(value)
        return lax.ppermute(value, "dp", [(src, src + run) for src in range(dp - run)])

    def from_next(value):
        if not multi:
            return jnp.zeros_like(value)
        return lax.ppermute(value, "dp", [(src + run, src) for src in range(dp - run)])

    small_parts = (ln1_gain, ln1_bias, shift_taps, ssm_rate, ssm_freq, ssm_coef, ssm_skip, ln2_gain, ln2_bias)
    flat = jnp.concatenate([part.reshape(-1) for part in small_parts])
    padded = -(-flat.shape[0] // 1024) * 1024
    flat = jnp.pad(flat, (0, padded - flat.shape[0])).reshape(padded // 128, 128)
    small = gather_fsdp(flat).reshape(fsdp, padded)
    pieces, at = [], 0
    for part in small_parts:
        pieces.append(small[:, at : at + part.size])
        at += part.size
    gain_one, bias_one, gain_two, bias_two = (
        pieces[index].reshape(width).astype(F32) for index in (0, 1, 7, 8)
    )

    def mine(piece, shape):
        return lax.dynamic_index_in_dim(piece, group, 0, keepdims=False).reshape(shape).astype(F32)

    heads = ssm_rate.shape[0]
    taps = mine(pieces[2], shift_taps.shape)
    rate = mine(pieces[3], ssm_rate.shape)
    freq = mine(pieces[4], ssm_freq.shape)
    coef = mine(pieces[5], ssm_coef.shape)
    skip = mine(pieces[6], ssm_skip.shape)
    assert fsdp == group_count
    query_w = gather_fsdp(w_query).reshape(width, width)
    key_w = gather_fsdp(w_key).reshape(width, width)
    value_w = gather_fsdp(w_value).reshape(width, width)
    out_w = gather_fsdp(w_out).reshape(width, width)
    up_w = gather_fsdp(w_up).reshape(width, -1)
    down_w = gather_fsdp(w_down).reshape(-1, width)
    hidden_size = up_w.shape[1]

    length = reach + TILE
    lag_up = jnp.arange(length) - TILE
    lag_down = reach - jnp.arange(length)
    kern_asc, kern_pull = jax.vjp(
        lambda *leaves: kernel_rows(*leaves, lag_up, reach), rate, freq, coef, skip
    )
    kern_desc = kernel_rows(rate, freq, coef, skip, lag_down, reach)

    seg_row = lax.dynamic_index_in_dim(segments, seq, 0, keepdims=False)
    seg_wide = jnp.concatenate(
        [jnp.full((span,), -1, jnp.int32), seg_row, jnp.full((HALO,), -2, jnp.int32)]
    )
    seg_full = lax.dynamic_slice_in_dim(seg_wide, chunk * span + span - HALO, span + 2 * HALO, 0)
    seg_q = seg_full[HALO : HALO + span]
    seg_k = lax.dynamic_slice_in_dim(seg_wide, chunk * span, 2 * span, 0) if multi else seg_q

    taps_tiles = jnp.pad(taps, ((0, 0), (0, -share % 128)))
    taps_tiles = taps_tiles.reshape(SHIFT, -1, 128).transpose(1, 0, 2)

    inputs = tokens.reshape(seqs * rows, width).astype(F32)
    normed, norm_one_pull = jax.vjp(layer_norm, inputs, gain_one, bias_one)
    act_one = normed.astype(BF)
    k_own = to_runs(mm(act_one, key_w).astype(BF))
    q_own = to_runs(mm(act_one, query_w).astype(BF))
    v_own = to_runs(mm(act_one, value_w).astype(BF))
    k_halo = from_prev(k_own[span - HALO :])
    ks_own = shift_fwd(seg_full, k_own, k_halo, taps_tiles)
    if multi:
        ks_win = jnp.concatenate([from_prev(ks_own), ks_own], axis=0)
        v_win = jnp.concatenate([from_prev(v_own), v_own], axis=0)
    else:
        ks_win, v_win = ks_own, v_own
    y_own = mix_fwd(q_own, ks_win, v_win, kern_desc[:, None, :], seg_q, seg_k)
    mixed = from_runs(y_own)
    resid = inputs + mm(mixed, out_w)
    normed_two, norm_two_pull = jax.vjp(layer_norm, resid, gain_two, bias_two)
    act_two = normed_two.astype(BF)
    gelu_rows, gelu_pull = jax.vjp(lambda entries: jax.nn.gelu(entries, approximate=True), mm(act_two, up_w))
    hidden = gelu_rows.astype(BF)
    output = (resid + mm(hidden, down_w)).astype(BF)

    def tn(left, right):
        return lax.dot_general(left, right, (((0,), (0,)), ((), ())), preferred_element_type=F32)

    cot = cotangent.reshape(seqs * rows, width)
    down_grad = tn(hidden, cot)
    up_grad_rows = gelu_pull(mm_nt(cot, down_w))[0].astype(BF)
    up_grad = tn(act_two, up_grad_rows)
    resid_part, gain_two_grad, bias_two_grad = norm_two_pull(mm_nt(up_grad_rows, up_w))
    resid_grad = cot.astype(F32) + resid_part
    resid_low = resid_grad.astype(BF)
    out_grad = tn(mixed, resid_low)
    gy_own = to_runs(mm_nt(resid_low, out_w).astype(BF))
    gq_own, gks_win, gv_win, gkern = mix_bwd(
        q_own, ks_win, v_win, gy_own, kern_asc[:, None, :], seg_q, seg_k
    )
    if multi:
        gks_own = gks_win[span:] + from_next(gks_win[:span].astype(BF)).astype(F32)
        gv_own = (gv_win[span:] + from_next(gv_win[:span].astype(BF)).astype(F32)).astype(BF)
        gks_halo = from_next(gks_own[:HALO].astype(BF)).astype(F32)
    else:
        gks_own, gv_own = gks_win, gv_win
        gks_halo = jnp.zeros((HALO, share), F32)
    gk_own, taps_grad = shift_bwd(seg_full, k_own, k_halo, gks_own, gks_halo, taps_tiles)
    rate_grad, freq_grad, coef_grad, skip_grad = kern_pull(gkern[:, 0, :])
    gq = from_runs(gq_own)
    gv = from_runs(gv_own)
    gk = from_runs(gk_own)
    query_grad, key_grad, value_grad = tn(act_one, gq), tn(act_one, gk), tn(act_one, gv)
    act_one_grad = mm_nt(gq, query_w) + mm_nt(gk, key_w) + mm_nt(gv, value_w)
    input_part, gain_one_grad, bias_one_grad = norm_one_pull(act_one_grad)
    input_grad = (resid_grad + input_part).astype(BF)

    big = [
        reduce_grad(grad.reshape(fsdp, grad.shape[0] // fsdp, grad.shape[1]), groups)
        for grad in (query_grad, key_grad, value_grad, out_grad, up_grad, down_grad)
    ]
    by_shard = jnp.concatenate(
        [
            grad.reshape(fsdp, width // fsdp)
            for grad in (gain_one_grad, bias_one_grad, gain_two_grad, bias_two_grad)
        ],
        axis=1,
    )
    by_group = jnp.concatenate(
        [grad.reshape(-1) for grad in (taps_grad, rate_grad, freq_grad, coef_grad, skip_grad)]
    )
    slots = (jnp.arange(group_count) == group)[:, None]
    packed = jnp.concatenate([by_shard, jnp.where(slots, by_group[None], 0.0)], axis=1)
    summed = lax.psum(packed, ("fsdp", "dp"))
    owned = lax.dynamic_index_in_dim(summed, lax.axis_index("fsdp"), 0, keepdims=False)
    shapes = [ln1_gain.shape, ln1_bias.shape, ln2_gain.shape, ln2_bias.shape, shift_taps.shape]
    shapes += [ssm_rate.shape, ssm_freq.shape, ssm_coef.shape, ssm_skip.shape]
    little, at = [], 0
    for shape in shapes:
        count = int(np.prod(shape))
        little.append(owned[at : at + count].reshape(shape))
        at += count
    return (
        output.reshape(seqs, rows, width),
        input_grad.reshape(seqs, rows, width),
        little[0],
        little[1],
        big[0],
        big[1],
        big[2],
        little[4],
        little[5],
        little[6],
        little[7],
        little[8],
        big[3],
        little[2],
        little[3],
        big[4],
        big[5],
    )


def solution(mesh):
    return jax.shard_map(
        shards,
        mesh=mesh,
        in_specs=(
            P("fsdp", "dp", None),
            P("fsdp", None),
            P("fsdp"),
            P("fsdp"),
            P("fsdp", None),
            P("fsdp", None),
            P("fsdp", None),
            P(None, "fsdp"),
            P("fsdp", None),
            P("fsdp", None),
            P(None, "fsdp", None),
            P("fsdp"),
            P("fsdp", None),
            P("fsdp"),
            P("fsdp"),
            P("fsdp", None),
            P("fsdp", None),
            P("fsdp", "dp", None),
        ),
        out_specs=(
            P("fsdp", "dp", None),
            P("fsdp", "dp", None),
            P("fsdp"),
            P("fsdp"),
            P("fsdp", None),
            P("fsdp", None),
            P("fsdp", None),
            P(None, "fsdp"),
            P("fsdp", None),
            P("fsdp", None),
            P(None, "fsdp", None),
            P("fsdp"),
            P("fsdp", None),
            P("fsdp"),
            P("fsdp"),
            P("fsdp", None),
            P("fsdp", None),
        ),
        check_vma=False,
    )
```

```python
import jax
import jax.numpy as jnp
import numpy as np
from jax import lax
from jax.experimental import pallas as pl
from jax.experimental.pallas import tpu as pltpu
from jax.sharding import PartitionSpec as P

SHIFT = 64
HOPS = 8
TILE = 256
HALO = 64
EPS = 1e-05
BF = jnp.bfloat16
F32 = jnp.float32
VMEM_BYTES = 56 * 1024 * 1024


def vmem():
    return pl.BlockSpec(memory_space=pltpu.VMEM)


def smem():
    return pl.BlockSpec(memory_space=pltpu.SMEM)


def hbm():
    return pl.BlockSpec(memory_space=pl.ANY)


def params():
    return pltpu.CompilerParams(vmem_limit_bytes=VMEM_BYTES)


def cost(micros, moved):
    return pl.CostEstimate(flops=int(micros * 1.0e9), bytes_accessed=int(moved), transcendentals=0)


def mm(left, right):
    return lax.dot_general(left, right, (((1,), (0,)), ((), ())), preferred_element_type=F32)


def mm_nt(left, right):
    return lax.dot_general(left, right, (((1,), (1,)), ((), ())), preferred_element_type=F32)


def tn(left, right):
    return lax.dot_general(left, right, (((0,), (0,)), ((), ())), preferred_element_type=F32)


def lane_tiles(width):
    return [(base, min(128, width - base)) for base in range(0, width, 128)]


def fill_ext(ext_ref, first_row, rows, source_ref, width):
    for index, (base, size) in enumerate(lane_tiles(width)):
        if size < 128:
            ext_ref[index, pl.ds(first_row, rows), :] = jnp.zeros((rows, 128), F32)
        ext_ref[index, pl.ds(first_row, rows), 0:size] = source_ref[:, base : base + size].astype(F32)


def fill_ext_t(ext_ref, first_row, source_ref):
    count, width, rows = source_ref.shape
    for index, (base, size) in enumerate(lane_tiles(width)):
        for block in range(count):
            part = source_ref[block, base : base + size, :].astype(F32).T
            if size < 128:
                part = jnp.concatenate([part, jnp.zeros((rows, 128 - size), F32)], axis=1)
            ext_ref[index, pl.ds(first_row + block * rows, rows), :] = part


def shift_fwd_kernel(seg_s, k_ref, halo_ref, taps_ref, segcol_ref, out_ref, ext, seg_b):
    width = k_ref.shape[1]
    rows = k_ref.shape[0] * k_ref.shape[2]
    fill_ext(ext, 0, HALO, halo_ref, width)
    fill_ext_t(ext, HALO, k_ref)
    seg_b[...] = jnp.broadcast_to(segcol_ref[...], seg_b.shape)
    for index, (base, size) in enumerate(lane_tiles(width)):

        def tap_row(lag):
            return taps_ref[index, lag : lag + 1, :]

        def body(tile, carry):
            start = pl.multiple_of(tile * 64, 64)

            def plain():
                total = jnp.zeros((64, 128), F32)
                for lag in range(SHIFT):
                    total = total + ext[index, pl.ds(start + HALO - lag, 64), :] * tap_row(lag)
                return total

            def masked():
                total = jnp.zeros((64, 128), F32)
                now = seg_b[pl.ds(start + HALO, 64), :]
                for lag in range(SHIFT):
                    same = seg_b[pl.ds(start + HALO - lag, 64), :] == now
                    part = ext[index, pl.ds(start + HALO - lag, 64), :] * tap_row(lag)
                    total = total + jnp.where(same, part, 0.0)
                return total

            total = lax.cond(seg_s[start + 1] == seg_s[start + HALO + 63], plain, masked)
            out_ref[pl.ds(start, 64), base : base + size] = total[:, 0:size].astype(BF)
            return carry

        lax.fori_loop(0, rows // 64, body, 0)


def shift_fwd(seg_full, k_own, k_halo, taps):
    width = k_own.shape[1]
    rows = k_own.shape[0] * k_own.shape[2]
    tiles = len(lane_tiles(width))
    return pl.pallas_call(
        shift_fwd_kernel,
        out_shape=jax.ShapeDtypeStruct((rows, width), BF),
        in_specs=[smem(), vmem(), vmem(), vmem(), vmem()],
        out_specs=vmem(),
        scratch_shapes=[
            pltpu.VMEM((tiles, HALO + rows, 128), F32),
            pltpu.VMEM((HALO + rows, 128), jnp.int32),
        ],
        compiler_params=params(),
        cost_estimate=cost(12, 2 << 20),
        name="shift_fwd",
    )(seg_full, k_own, k_halo, taps, seg_full[: HALO + rows, None])


def shift_bwd_kernel(
    seg_s, k_ref, halo_ref, g_ref, ghalo_ref, taps_ref, segcol_ref, gk_ref, tg_ref, ext, gext, seg_b, acc, gk_rows
):
    width = k_ref.shape[1]
    rows = k_ref.shape[0] * k_ref.shape[2]
    fill_ext(ext, 0, HALO, halo_ref, width)
    fill_ext_t(ext, HALO, k_ref)
    fill_ext(gext, 0, rows, g_ref, width)
    fill_ext(gext, rows, HALO, ghalo_ref, width)
    seg_b[...] = jnp.broadcast_to(segcol_ref[...], seg_b.shape)
    acc[...] = jnp.zeros_like(acc)
    for index, (base, size) in enumerate(lane_tiles(width)):

        def tap_row(lag):
            return taps_ref[index, lag : lag + 1, :]

        def fold(part):
            total = part[0:8]
            for piece in range(1, 8):
                total = total + part[8 * piece : 8 * piece + 8]
            return total

        def body(tile, carry):
            start = pl.multiple_of(tile * 64, 64)

            def plain():
                total = jnp.zeros((64, 128), F32)
                for lag in range(SHIFT):
                    total = total + gext[index, pl.ds(start + lag, 64), :] * tap_row(lag)
                return total

            def masked():
                total = jnp.zeros((64, 128), F32)
                now = seg_b[pl.ds(start + HALO, 64), :]
                for lag in range(SHIFT):
                    same = seg_b[pl.ds(start + HALO + lag, 64), :] == now
                    part = gext[index, pl.ds(start + lag, 64), :] * tap_row(lag)
                    total = total + jnp.where(same, part, 0.0)
                return total

            total = lax.cond(seg_s[start + HALO] == seg_s[start + HALO + 126], plain, masked)
            gk_rows[index, pl.ds(start, 64), :] = total
            grad = gext[index, pl.ds(start, 64), :]
            clear = seg_s[start + 1] == seg_s[start + HALO + 63]

            @pl.when(clear)
            def _():
                for lag in range(SHIFT):
                    part = ext[index, pl.ds(start + HALO - lag, 64), :] * grad
                    acc[index, lag] = acc[index, lag] + fold(part)

            @pl.when(jnp.logical_not(clear))
            def _():
                now = seg_b[pl.ds(start + HALO, 64), :]
                for lag in range(SHIFT):
                    same = seg_b[pl.ds(start + HALO - lag, 64), :] == now
                    part = ext[index, pl.ds(start + HALO - lag, 64), :] * grad
                    acc[index, lag] = acc[index, lag] + fold(jnp.where(same, part, 0.0))

            return carry

        lax.fori_loop(0, rows // 64, body, 0)
        tg_ref[:, base : base + size] = jnp.sum(acc[index], axis=1)[:, 0:size]
        for block in range(k_ref.shape[0]):
            turned = gk_rows[index, block * TILE : (block + 1) * TILE, :].T
            gk_ref[block, base : base + size, :] = turned[0:size].astype(BF)


def shift_bwd(seg_full, k_own, k_halo, grad, grad_halo, taps):
    count, width, _ = k_own.shape
    rows = count * TILE
    tiles = len(lane_tiles(width))
    return pl.pallas_call(
        shift_bwd_kernel,
        out_shape=(
            jax.ShapeDtypeStruct(k_own.shape, BF),
            jax.ShapeDtypeStruct((SHIFT, width), F32),
        ),
        in_specs=[smem()] + [vmem()] * 6,
        out_specs=(vmem(), vmem()),
        scratch_shapes=[
            pltpu.VMEM((tiles, HALO + rows, 128), F32),
            pltpu.VMEM((tiles, HALO + rows, 128), F32),
            pltpu.VMEM((2 * HALO + rows, 128), jnp.int32),
            pltpu.VMEM((tiles, SHIFT, 8, 128), F32),
            pltpu.VMEM((tiles, rows, 128), F32),
        ],
        compiler_params=params(),
        cost_estimate=cost(25, 4 << 20),
        name="shift_bwd",
    )(seg_full, k_own, k_halo, grad, grad_halo, taps, seg_full[:, None])


def tile_table(query_blocks, key_blocks, unroll):
    offset = key_blocks - query_blocks
    pairs = []
    for distance in range(HOPS + 1):
        for row in range(query_blocks):
            if row + offset - distance >= 0:
                pairs.append((row, row + offset - distance))
    assert len(pairs) % unroll == 0
    return np.array(pairs, np.int32)


def build_bands(bands, row):
    length = row.shape[1]
    skewed = pltpu.roll(jnp.broadcast_to(row, (8, length)), 0, 1, stride=1, stride_axis=0)
    for step in range(16):
        bands[step] = pltpu.roll(skewed, 8 * step, 1) if step else skewed


def read_band(bands, first, second):
    upper = bands[:, :, pl.ds(first, TILE)].reshape(128, TILE)
    lower = bands[:, :, pl.ds(second, TILE)].reshape(128, TILE)
    return jnp.concatenate([upper, lower], axis=0)


UNROLL_F = 4
UNROLL_B = 2


def head_rows(dest, source, heads, size):
    for head in range(heads):
        dest[head] = source[:, head * size : (head + 1) * size]


def head_turn(dest, source, heads, size):
    for head in range(heads):
        for block in range(source.shape[0]):
            part = source[block, head * size : (head + 1) * size, :].astype(F32)
            dest[head, block * TILE : (block + 1) * TILE, :] = part.T.astype(dest.dtype)


def mix_fwd_kernel(tab, q_ref, k_ref, v_ref, row_ref, segq_ref, segk_ref, y_ref, kh, yacc, bands, seg_b):
    heads, length = row_ref.shape[0], row_ref.shape[2]
    size = q_ref.shape[1] // heads
    offset = v_ref.shape[0] - q_ref.shape[0]
    tiles = tab.shape[0]
    head_rows(kh, k_ref, heads, size)
    seg_b[...] = jnp.broadcast_to(segk_ref[...], seg_b.shape)
    yacc[...] = jnp.zeros_like(yacc)

    def head_body(head, carry):
        build_bands(bands, row_ref[head])
        own = pl.ds(pl.multiple_of(head * size, size), size)

        def body(step, carry):
            for unrolled in range(UNROLL_F):
                row = tab[step * UNROLL_F + unrolled, 0]
                col = tab[step * UNROLL_F + unrolled, 1]
                cols = pl.ds(pl.multiple_of(col * TILE, TILE), TILE)
                first = pl.multiple_of(TILE + TILE * (row + offset - col), TILE)
                kern = read_band(bands, first, pl.multiple_of(first - 128, 128))
                score = mm(kh[head, cols, :], q_ref[row, own, :])
                seg_now = seg_b[cols, :]
                live = jnp.concatenate([seg_now, seg_now], axis=1) == segq_ref[row]
                weight = jnp.where(live, score * kern, 0.0).astype(BF)
                yacc[row, own, :] += mm(v_ref[col, own, :], weight)
            return carry

        lax.fori_loop(0, tiles // UNROLL_F, body, 0)
        return carry

    lax.fori_loop(0, heads, head_body, 0)
    y_ref[...] = yacc[...].astype(BF)


def mix_fwd(q, k_win, v_win, kern_asc, seg_q, seg_k):
    blocks, width, _ = q.shape
    wide = k_win.shape[0]
    heads, _, length = kern_asc.shape
    size = width // heads
    table = tile_table(blocks, wide // TILE, UNROLL_F)
    return pl.pallas_call(
        mix_fwd_kernel,
        out_shape=jax.ShapeDtypeStruct(q.shape, BF),
        in_specs=[smem()] + [vmem()] * 6,
        out_specs=vmem(),
        scratch_shapes=[
            pltpu.VMEM((heads, wide, size), BF),
            pltpu.VMEM(q.shape, F32),
            pltpu.VMEM((16, 8, length), F32),
            pltpu.VMEM((wide, 128), jnp.int32),
        ],
        compiler_params=params(),
        cost_estimate=cost(20, 4 << 20),
        name="mix_fwd",
    )(table, q, k_win, v_win, kern_asc, seg_q.reshape(blocks, 1, TILE), seg_k[:, None])


def mix_bwd_kernel(
    tab, q_ref, k_ref, v_ref, g_ref, row_ref, segq_ref, segk_ref, gq_ref, gk_ref, gv_ref, gkern_ref,
    qh, kh, vh, gh, kt, gqt, gkacc, gvacc, bands, gbands, seg_b,
):
    heads, length = row_ref.shape[0], row_ref.shape[2]
    size = q_ref.shape[1] // heads
    query_blocks, key_blocks = q_ref.shape[0], v_ref.shape[0]
    offset = key_blocks - query_blocks
    tiles = tab.shape[0]
    head_turn(qh, q_ref, heads, size)
    head_rows(kh, k_ref, heads, size)
    head_turn(vh, v_ref, heads, size)
    head_turn(gh, g_ref, heads, size)
    for head in range(heads):
        for block in range(key_blocks):
            part = kh[head, block * TILE : (block + 1) * TILE, :].astype(F32)
            kt[block, head * size : (head + 1) * size, :] = part.T.astype(BF)
    seg_b[...] = jnp.broadcast_to(segk_ref[...], seg_b.shape)
    gqt[...] = jnp.zeros_like(gqt)
    gkacc[...] = jnp.zeros_like(gkacc)
    gvacc[...] = jnp.zeros_like(gvacc)

    def head_body(head, carry):
        build_bands(bands, row_ref[head])
        gbands[...] = jnp.zeros_like(gbands)
        own = pl.ds(pl.multiple_of(head * size, size), size)

        def body(step, carry):
            for unrolled in range(UNROLL_B):
                row = tab[step * UNROLL_B + unrolled, 0]
                col = tab[step * UNROLL_B + unrolled, 1]
                rows = pl.ds(pl.multiple_of(row * TILE, TILE), TILE)
                cols = pl.ds(pl.multiple_of(col * TILE, TILE), TILE)
                first = pl.multiple_of(TILE + TILE * (row + offset - col), TILE)
                second = pl.multiple_of(first - 128, 128)
                kern = read_band(bands, first, second)
                score = mm(kh[head, cols, :], q_ref[row, own, :])
                grad = mm(vh[head, cols, :], g_ref[row, own, :])
                seg_now = seg_b[cols, :]
                live = jnp.concatenate([seg_now, seg_now], axis=1) == segq_ref[row]
                grad = jnp.where(live, grad, 0.0)
                weight = jnp.where(live, score * kern, 0.0).astype(BF)
                gscore = (grad * kern).astype(BF)
                both = grad * score
                gbands[:, :, pl.ds(first, TILE)] += both[0:128].reshape(16, 8, TILE)
                gbands[:, :, pl.ds(second, TILE)] += both[128:256].reshape(16, 8, TILE)
                gkacc[head, cols, :] += mm(gscore, qh[head, rows, :])
                gvacc[head, cols, :] += mm(weight, gh[head, rows, :])
                gqt[row, own, :] += mm(kt[col, own, :], gscore)
            return carry

        lax.fori_loop(0, tiles // UNROLL_B, body, 0)
        total = gbands[0]
        for step in range(1, 16):
            total = total + pltpu.roll(gbands[step], length - 8 * step, 1)
        line = total[0:1]
        for sub in range(1, 8):
            line = line + pltpu.roll(total, length - sub, 1)[sub : sub + 1]
        gkern_ref[head] = line
        return carry

    lax.fori_loop(0, heads, head_body, 0)
    gq_ref[...] = gqt[...].astype(BF)
    for head in range(heads):
        gk_ref[:, head * size : (head + 1) * size] = gkacc[head]
        for block in range(key_blocks):
            part = gvacc[head, block * TILE : (block + 1) * TILE, :].T
            gv_ref[block, head * size : (head + 1) * size, :] = part.astype(gv_ref.dtype)


def mix_bwd(q, k_win, v_win, grad, kern_asc, seg_q, seg_k):
    blocks, width, _ = q.shape
    wide = k_win.shape[0]
    heads, _, length = kern_asc.shape
    size = width // heads
    rows = blocks * TILE
    table = tile_table(blocks, wide // TILE, UNROLL_B)
    return pl.pallas_call(
        mix_bwd_kernel,
        out_shape=(
            jax.ShapeDtypeStruct(q.shape, BF),
            jax.ShapeDtypeStruct((wide, width), F32),
            jax.ShapeDtypeStruct(v_win.shape, BF if wide == rows else F32),
            jax.ShapeDtypeStruct((heads, 1, length), F32),
        ),
        in_specs=[smem()] + [vmem()] * 7,
        out_specs=(vmem(),) * 4,
        scratch_shapes=[
            pltpu.VMEM((heads, rows, size), BF),
            pltpu.VMEM((heads, wide, size), BF),
            pltpu.VMEM((heads, wide, size), BF),
            pltpu.VMEM((heads, rows, size), BF),
            pltpu.VMEM(v_win.shape, BF),
            pltpu.VMEM(q.shape, F32),
            pltpu.VMEM((heads, wide, size), F32),
            pltpu.VMEM((heads, wide, size), F32),
            pltpu.VMEM((16, 8, length), F32),
            pltpu.VMEM((16, 8, length), F32),
            pltpu.VMEM((wide, 128), jnp.int32),
        ],
        compiler_params=params(),
        cost_estimate=cost(45, 8 << 20),
        name="mix_bwd",
    )(table, q, k_win, v_win, grad, kern_asc, seg_q.reshape(blocks, 1, TILE), seg_k[:, None])


def load_pieces(me, pieces, full, sem, base):
    rows = pieces[0].shape[0]
    copies = []
    for mask, piece in enumerate(pieces):
        place = pl.ds(pl.multiple_of((me ^ mask) * rows, 64), rows)
        copies.append(pltpu.make_async_copy(piece, full.at[place], sem.at[base + mask]))
    for copy in copies:
        copy.start()

    def wait():
        for copy in copies:
            copy.wait()

    return wait


def normal_stats(value):
    center = value - jnp.mean(value, axis=-1, keepdims=True)
    scale = lax.rsqrt(jnp.mean(center * center, axis=-1, keepdims=True) + EPS)
    return center * scale, scale


def normal_grad(grad, hat, scale, gain):
    lead = grad * gain
    first = jnp.mean(lead, axis=-1, keepdims=True)
    second = jnp.mean(lead * hat, axis=-1, keepdims=True)
    return scale * (lead - first - hat * second)


def to_blocks(dest, turned, seqs, groups):
    share = turned.shape[0] // groups
    for seq in range(seqs):
        for group in range(groups):
            dest[seq * groups + group] = turned[
                group * share : (group + 1) * share, seq * TILE : (seq + 1) * TILE
            ]


def from_blocks(dest, blocks, seqs, groups):
    for seq in range(seqs):
        whole = jnp.concatenate([blocks[seq * groups + group] for group in range(groups)], axis=0)
        dest[seq * TILE : (seq + 1) * TILE, :] = whole.astype(F32).T.astype(BF)


def turn(value):
    return value.astype(F32).T.astype(BF)


def key_kernel(me_ref, x_ref, gain_ref, bias_ref, w0, w1, w2, w3, act_ref, out_ref, full, sem):
    wait = load_pieces(me_ref[0], (w0, w1, w2, w3), full, sem, 0)
    groups = full.shape[0] // out_ref.shape[1]
    seqs = x_ref.shape[0] // TILE
    hat, _ = normal_stats(x_ref[...].astype(F32))
    act_ref[...] = (hat * gain_ref[...] + bias_ref[...]).astype(BF)
    wait()
    to_blocks(out_ref, mm(act_ref[...], full[...]).T.astype(BF), seqs, groups)


def key_call(me, x, gain, bias, pieces, blocks):
    tokens, width = x.shape
    return pl.pallas_call(
        key_kernel,
        out_shape=(
            jax.ShapeDtypeStruct((tokens, width), BF),
            jax.ShapeDtypeStruct(blocks, BF),
        ),
        in_specs=[smem()] + [vmem()] * 3 + [hbm()] * 4,
        out_specs=(vmem(), vmem()),
        scratch_shapes=[pltpu.VMEM((width, width), BF), pltpu.SemaphoreType.DMA((4,))],
        compiler_params=params(),
        cost_estimate=cost(4, 4 << 20),
        name="key_call",
    )(me, x, gain, bias, *pieces)


def query_value_kernel(me_ref, act_ref, q0, q1, q2, q3, v0, v1, v2, v3, q_ref, v_ref, qfull, vfull, sem):
    wait_q = load_pieces(me_ref[0], (q0, q1, q2, q3), qfull, sem, 0)
    wait_v = load_pieces(me_ref[0], (v0, v1, v2, v3), vfull, sem, 4)
    groups = qfull.shape[0] // q_ref.shape[1]
    seqs = act_ref.shape[0] // TILE
    wait_q()
    to_blocks(q_ref, mm(act_ref[...], qfull[...]).T.astype(BF), seqs, groups)
    wait_v()
    to_blocks(v_ref, mm(act_ref[...], vfull[...]).T.astype(BF), seqs, groups)


def query_value_call(me, act, q_pieces, v_pieces, blocks):
    width = act.shape[1]
    return pl.pallas_call(
        query_value_kernel,
        out_shape=(jax.ShapeDtypeStruct(blocks, BF),) * 2,
        in_specs=[smem(), vmem()] + [hbm()] * 8,
        out_specs=(vmem(), vmem()),
        scratch_shapes=[
            pltpu.VMEM((width, width), BF),
            pltpu.VMEM((width, width), BF),
            pltpu.SemaphoreType.DMA((8,)),
        ],
        compiler_params=params(),
        cost_estimate=cost(5, 5 << 20),
        name="query_value_call",
    )(me, act, *q_pieces, *v_pieces)


GELU_A = 0.7978845608028654
GELU_B = 0.044715


def middle_kernel(
    me_ref, y_ref, x_ref, gain_ref, bias_ref, cot_ref, o0, o1, o2, o3, u0, u1, u2, u3, d0, d1, d2, d3,
    resid_ref, act_ref, hidden_ref, gz_ref, gr_ref, gy_ref, gln_ref,
    ofull, ufull, dfull, mixed, hat, gb, sem,
):
    me = me_ref[0]
    wait_o = load_pieces(me, (o0, o1, o2, o3), ofull, sem, 0)
    wait_u = load_pieces(me, (u0, u1, u2, u3), ufull, sem, 4)
    wait_d = load_pieces(me, (d0, d1, d2, d3), dfull, sem, 8)
    tokens, width = x_ref.shape
    groups = width // y_ref.shape[1]
    seqs = tokens // TILE
    chunk = width
    chunks = ufull.shape[1] // chunk
    from_blocks(mixed, y_ref, seqs, groups)
    wait_o()
    resid_ref[...] = x_ref[...].astype(F32) + mm(mixed[...], ofull[...])
    normed, scale = normal_stats(resid_ref[...])
    hat[...] = normed
    act_ref[...] = (normed * gain_ref[...] + bias_ref[...]).astype(BF)
    gb[...] = jnp.zeros_like(gb)
    wait_u()
    wait_d()

    def body(step, carry):
        rows = pl.ds(pl.multiple_of((step % seqs) * TILE, TILE), TILE)
        cols = pl.ds(pl.multiple_of((step // seqs) * chunk, chunk), chunk)
        z = mm(act_ref[rows, :], ufull[:, cols])
        dh = mm_nt(cot_ref[rows, :], dfull[cols, :])
        square = z * z
        t = jnp.tanh(GELU_A * z * (1.0 + GELU_B * square))
        half = 0.5 * (1.0 + t)
        hidden_ref[rows, cols] = (z * half).astype(BF)
        slope = half + 0.5 * z * (1.0 - t * t) * (GELU_A * (1.0 + 3.0 * GELU_B * square))
        gz = (slope * dh).astype(BF)
        gz_ref[rows, cols] = gz
        gb[rows, :] += mm_nt(gz, ufull[:, cols])
        return carry

    lax.fori_loop(0, seqs * chunks, body, 0)
    gln_ref[0:1, :] = jnp.sum(gb[...] * hat[...], axis=0, keepdims=True)
    gln_ref[1:2, :] = jnp.sum(gb[...], axis=0, keepdims=True)
    gr_ref[...] = cot_ref[...].astype(F32) + normal_grad(gb[...], hat[...], scale, gain_ref[...])
    to_blocks(gy_ref, mm_nt(ofull[...], gr_ref[...].astype(BF)).astype(BF), seqs, groups)


def middle_call(me, y, x, gain, bias, cot, o_pieces, u_pieces, d_pieces):
    tokens, width = x.shape
    hidden = u_pieces[0].shape[1]
    return pl.pallas_call(
        middle_kernel,
        out_shape=(
            jax.ShapeDtypeStruct((tokens, width), F32),
            jax.ShapeDtypeStruct((tokens, width), BF),
            jax.ShapeDtypeStruct((tokens, hidden), BF),
            jax.ShapeDtypeStruct((tokens, hidden), BF),
            jax.ShapeDtypeStruct((tokens, width), F32),
            jax.ShapeDtypeStruct(y.shape, BF),
            jax.ShapeDtypeStruct((2, width), F32),
        ),
        in_specs=[smem()] + [vmem()] * 5 + [hbm()] * 12,
        out_specs=(vmem(),) * 7,
        scratch_shapes=[
            pltpu.VMEM((width, width), BF),
            pltpu.VMEM((width, hidden), BF),
            pltpu.VMEM((hidden, width), BF),
            pltpu.VMEM((tokens, width), BF),
            pltpu.VMEM((tokens, width), F32),
            pltpu.VMEM((tokens, width), F32),
            pltpu.SemaphoreType.DMA((12,)),
        ],
        compiler_params=params(),
        cost_estimate=cost(15, 24 << 20),
        name="middle_call",
    )(me, y, x, gain, bias, cot, *o_pieces, *u_pieces, *d_pieces)


def ffn_grads_kernel(
    me_ref, y_ref, resid_ref, act_ref, hidden_ref, gz_ref, gr_ref, cot_ref, d0, d1, d2, d3,
    out_ref, keep_ref, send_ref, dfull, act_t, low, sem,
):
    me = me_ref[0]
    wait_d = load_pieces(me, (d0, d1, d2, d3), dfull, sem, 0)
    tokens, width = resid_ref.shape
    hidden = hidden_ref.shape[1]
    groups = width // y_ref.shape[1]
    share = width // groups
    wide = hidden // groups
    seqs = tokens // TILE
    act_t[...] = turn(act_ref[...])
    low[...] = gr_ref[...].astype(BF)
    blocks = hidden // width
    for slot in range(2):
        for dest, mask in ((keep_ref, 2 * slot), (send_ref, 2 * slot + 1)):
            owner = me ^ mask
            part = hidden_ref[:, pl.ds(pl.multiple_of(owner * wide, wide), wide)]
            dest[slot, 0:wide, :] = mm(turn(part), cot_ref[...]).astype(dest.dtype)
            part = act_t[pl.ds(pl.multiple_of(owner * share, share), share), :]
            for block in range(blocks):
                base = wide + block * share
                value = mm(part, gz_ref[:, block * width : (block + 1) * width])
                dest[slot, base : base + share, :] = value.astype(dest.dtype)
            base = wide + blocks * share
            value = mm(y_ref[owner], low[0:TILE, :])
            for seq in range(1, seqs):
                value = value + mm(y_ref[seq * groups + owner], low[seq * TILE : (seq + 1) * TILE, :])
            dest[slot, base : base + share, :] = value.astype(dest.dtype)
    wait_d()
    out_ref[...] = (resid_ref[...] + mm(hidden_ref[...], dfull[...])).astype(BF)


def ffn_grads_call(me, y, resid, act, hidden, gz, gr, cot, d_pieces):
    tokens, width = resid.shape
    wide = hidden.shape[1]
    groups = width // y.shape[1]
    rows = wide // groups + (wide // width + 1) * (width // groups)
    return pl.pallas_call(
        ffn_grads_kernel,
        out_shape=(
            jax.ShapeDtypeStruct((tokens, width), BF),
            jax.ShapeDtypeStruct((2, rows, width), F32),
            jax.ShapeDtypeStruct((2, rows, width), BF),
        ),
        in_specs=[smem()] + [vmem()] * 7 + [hbm()] * 4,
        out_specs=(vmem(),) * 3,
        scratch_shapes=[
            pltpu.VMEM((wide, width), BF),
            pltpu.VMEM((width, tokens), BF),
            pltpu.VMEM((tokens, width), BF),
            pltpu.SemaphoreType.DMA((4,)),
        ],
        compiler_params=params(),
        cost_estimate=cost(15, 32 << 20),
        name="ffn_grads_call",
    )(me, y, resid, act, hidden, gz, gr, cot, *d_pieces)


def input_grads(me, act_t, grad, share, base, keep_ref, send_ref):
    for slot in range(2):
        for dest, mask in ((keep_ref, 2 * slot), (send_ref, 2 * slot + 1)):
            part = act_t[pl.ds(pl.multiple_of((me ^ mask) * share, share), share), :]
            dest[slot, base : base + share, :] = mm(part, grad).astype(dest.dtype)


def qv_grads_kernel(
    me_ref, gq_ref, gv_ref, act_ref, q0, q1, q2, q3, v0, v1, v2, v3,
    keep_ref, send_ref, ga_ref, qfull, vfull, act_t, rows, sem,
):
    me = me_ref[0]
    wait_q = load_pieces(me, (q0, q1, q2, q3), qfull, sem, 0)
    wait_v = load_pieces(me, (v0, v1, v2, v3), vfull, sem, 4)
    tokens, width = act_ref.shape
    share = gq_ref.shape[1]
    groups = width // share
    seqs = tokens // TILE
    act_t[...] = turn(act_ref[...])
    from_blocks(rows, gq_ref, seqs, groups)
    input_grads(me, act_t, rows[...], share, 0, keep_ref, send_ref)
    wait_q()
    ga_ref[...] = mm_nt(rows[...], qfull[...])
    from_blocks(rows, gv_ref, seqs, groups)
    input_grads(me, act_t, rows[...], share, share, keep_ref, send_ref)
    wait_v()
    ga_ref[...] += mm_nt(rows[...], vfull[...])


def qv_grads_call(me, gq, gv, act, q_pieces, v_pieces):
    tokens, width = act.shape
    share = gq.shape[1]
    return pl.pallas_call(
        qv_grads_kernel,
        out_shape=(
            jax.ShapeDtypeStruct((2, 2 * share, width), F32),
            jax.ShapeDtypeStruct((2, 2 * share, width), BF),
            jax.ShapeDtypeStruct((tokens, width), F32),
        ),
        in_specs=[smem()] + [vmem()] * 3 + [hbm()] * 8,
        out_specs=(vmem(),) * 3,
        scratch_shapes=[
            pltpu.VMEM((width, width), BF),
            pltpu.VMEM((width, width), BF),
            pltpu.VMEM((width, tokens), BF),
            pltpu.VMEM((tokens, width), BF),
            pltpu.SemaphoreType.DMA((8,)),
        ],
        compiler_params=params(),
        cost_estimate=cost(8, 12 << 20),
        name="qv_grads_call",
    )(me, gq, gv, act, *q_pieces, *v_pieces)


def last_kernel(
    me_ref, gk_ref, act_ref, ga_ref, x_ref, gr_ref, gain_ref, k0, k1, k2, k3,
    keep_ref, send_ref, gx_ref, gln_ref, kfull, act_t, rows, sem,
):
    me = me_ref[0]
    wait_k = load_pieces(me, (k0, k1, k2, k3), kfull, sem, 0)
    tokens, width = act_ref.shape
    share = gk_ref.shape[1]
    act_t[...] = turn(act_ref[...])
    from_blocks(rows, gk_ref, tokens // TILE, width // share)
    input_grads(me, act_t, rows[...], share, 0, keep_ref, send_ref)
    wait_k()
    ga = ga_ref[...] + mm_nt(rows[...], kfull[...])
    hat, scale = normal_stats(x_ref[...].astype(F32))
    gln_ref[0:1, :] = jnp.sum(ga * hat, axis=0, keepdims=True)
    gln_ref[1:2, :] = jnp.sum(ga, axis=0, keepdims=True)
    gx_ref[...] = (gr_ref[...] + normal_grad(ga, hat, scale, gain_ref[...])).astype(BF)


def last_call(me, gk, act, ga, x, gr, gain, k_pieces):
    tokens, width = act.shape
    share = gk.shape[1]
    return pl.pallas_call(
        last_kernel,
        out_shape=(
            jax.ShapeDtypeStruct((2, share, width), F32),
            jax.ShapeDtypeStruct((2, share, width), BF),
            jax.ShapeDtypeStruct((tokens, width), BF),
            jax.ShapeDtypeStruct((2, width), F32),
        ),
        in_specs=[smem()] + [vmem()] * 6 + [hbm()] * 4,
        out_specs=(vmem(),) * 4,
        scratch_shapes=[
            pltpu.VMEM((width, width), BF),
            pltpu.VMEM((width, tokens), BF),
            pltpu.VMEM((tokens, width), BF),
            pltpu.SemaphoreType.DMA((4,)),
        ],
        compiler_params=params(),
        cost_estimate=cost(6, 8 << 20),
        name="last_call",
    )(me, gk, act, ga, x, gr, gain, *k_pieces)


def xor_permute(value, axis, mask):
    count = lax.axis_size(axis)
    return lax.ppermute(value, axis, [(source, source ^ mask) for source in range(count)])


def gather_pieces(shard):
    across = xor_permute(shard, "fsdp", 2)
    beside = xor_permute(shard, "fsdp", 1)
    both = xor_permute(across, "fsdp", 1)
    return (shard, beside, across, both)


def sum_over_dp(value):
    rows, cols = value.shape
    count = lax.axis_size("dp")
    if count != 8:
        split = value.astype(BF).reshape(count, rows // count, cols)
        owned = jnp.sum(lax.all_to_all(split, "dp", 0, 0).astype(F32), axis=0).astype(BF)
        spread = jnp.broadcast_to(owned[None], (count,) + owned.shape)
        return lax.all_to_all(spread, "dp", 0, 0).reshape(rows, cols).astype(F32)
    low = lax.axis_index("dp") % 2
    halves = value.reshape(2, rows // 2, cols)
    keep = lax.dynamic_index_in_dim(halves, low, 0, keepdims=False)
    send = lax.dynamic_index_in_dim(halves, 1 - low, 0, keepdims=False).astype(BF)
    half = keep + xor_permute(send, "dp", 1).astype(F32)
    lines = [[0, 2, 4, 6], [1, 3, 5, 7]]
    split = half.astype(BF).reshape(4, rows // 8, cols)
    parts = lax.all_to_all(split, "dp", 0, 0, axis_index_groups=lines)
    owned = jnp.sum(parts.astype(F32), axis=0).astype(BF)
    spread = jnp.broadcast_to(owned[None], (4,) + owned.shape)
    half = lax.all_to_all(spread, "dp", 0, 0, axis_index_groups=lines).reshape(rows // 2, cols)
    other = xor_permute(half, "dp", 1)
    first = jnp.where(low == 0, half, other)
    second = jnp.where(low == 0, other, half)
    return jnp.concatenate([first, second], axis=0).astype(F32)


def reduce_grads(keep, send):
    came = xor_permute(send, "fsdp", 1)
    away = (keep[1] + came[1].astype(F32)).astype(BF)
    total = keep[0] + came[0].astype(F32) + xor_permute(away, "fsdp", 2).astype(F32)
    return sum_over_dp(total)


def kernel_rows(rate, freq, coef, skip, lags, reach):
    lag = lags.astype(F32)
    inside = (lags >= 0) & (lags < reach)
    clipped = jnp.where(inside, lag, 0.0)
    decay = jnp.exp(-rate[:, :, None] * clipped)
    angle = freq[:, :, None] * clipped
    wave = coef[0][:, :, None] * jnp.cos(angle) - coef[1][:, :, None] * jnp.sin(angle)
    first = (lags == 0).astype(F32)
    return jnp.where(inside, jnp.sum(decay * wave, axis=1) + skip[:, None] * first, 0.0)


def shards(
    tokens, segments, ln1_gain, ln1_bias, w_query, w_key, w_value, shift_taps, ssm_rate, ssm_freq,
    ssm_coef, ssm_skip, w_out, ln2_gain, ln2_bias, w_up, w_down, cotangent,
):
    seqs, rows, width = tokens.shape
    fsdp = lax.axis_size("fsdp")
    dp = lax.axis_size("dp")
    run = HOPS
    place = lax.axis_index("fsdp")
    me = lax.axis_index("dp")
    chunk, inner = me // run, me % run
    group_count = run // seqs
    share = width // group_count
    seq, group = inner // group_count, inner % group_count
    span = run * rows
    multi = dp > run
    groups = [list(range(base, base + run)) for base in range(0, dp, run)] if multi else None
    reach = HOPS * rows + rows
    assert dp % run == 0 and rows == TILE and fsdp == 4 and group_count == fsdp
    blocks = (run, share, rows)

    def exchange(value):
        return lax.all_to_all(value, "dp", 0, 0, axis_index_groups=groups)

    def from_prev(value):
        if not multi:
            return jnp.zeros_like(value)
        return lax.ppermute(value, "dp", [(src, src + run) for src in range(dp - run)])

    def from_next(value):
        return lax.ppermute(value, "dp", [(src + run, src) for src in range(dp - run)])

    small_parts = (ln1_gain, ln1_bias, shift_taps, ssm_rate, ssm_freq, ssm_coef, ssm_skip, ln2_gain, ln2_bias)
    flat = jnp.concatenate([part.reshape(-1) for part in small_parts])
    padded = -(-flat.shape[0] // 1024) * 1024
    flat = jnp.pad(flat, (0, padded - flat.shape[0])).reshape(padded // 128, 128)
    in_order = jnp.stack(gather_pieces(flat)).reshape(fsdp, padded)
    small = in_order[jnp.arange(fsdp) ^ place]
    pieces, at = [], 0
    for part in small_parts:
        pieces.append(small[:, at : at + part.size])
        at += part.size
    gain_one, bias_one, gain_two, bias_two = (
        pieces[index].reshape(1, width).astype(F32) for index in (0, 1, 7, 8)
    )

    def mine(piece, shape):
        return lax.dynamic_index_in_dim(piece, group, 0, keepdims=False).reshape(shape).astype(F32)

    taps = mine(pieces[2], shift_taps.shape)
    rate = mine(pieces[3], ssm_rate.shape)
    freq = mine(pieces[4], ssm_freq.shape)
    coef = mine(pieces[5], ssm_coef.shape)
    skip = mine(pieces[6], ssm_skip.shape)
    key_w = gather_pieces(w_key)
    query_w = gather_pieces(w_query)
    value_w = gather_pieces(w_value)
    out_w = gather_pieces(w_out)
    up_w = gather_pieces(w_up)
    down_w = gather_pieces(w_down)

    lags = jnp.arange(reach + TILE) - TILE
    kern, kern_pull = jax.vjp(lambda *leaves: kernel_rows(*leaves, lags, reach), rate, freq, coef, skip)
    kern = kern[:, None, :]

    seg_row = lax.dynamic_index_in_dim(segments, seq, 0, keepdims=False)
    seg_wide = jnp.concatenate(
        [jnp.full((span,), -1, jnp.int32), seg_row, jnp.full((HALO,), -2, jnp.int32)]
    )
    seg_full = lax.dynamic_slice_in_dim(seg_wide, chunk * span + span - HALO, span + 2 * HALO, 0)
    seg_q = seg_full[HALO : HALO + span]
    seg_k = lax.dynamic_slice_in_dim(seg_wide, chunk * span, 2 * span, 0) if multi else seg_q

    taps_tiles = jnp.pad(taps, ((0, 0), (0, -share % 128)))
    taps_tiles = taps_tiles.reshape(SHIFT, -1, 128).transpose(1, 0, 2)

    which = place.reshape(1).astype(jnp.int32)
    x = tokens.reshape(seqs * rows, width)
    cot = cotangent.reshape(seqs * rows, width)
    act_one, k_mine = key_call(which, x, gain_one, bias_one, key_w, blocks)
    k_own = exchange(k_mine)
    q_mine, v_mine = query_value_call(which, act_one, query_w, value_w, blocks)
    q_own, v_own = exchange(q_mine), exchange(v_mine)
    k_halo = from_prev(k_own[-1, :, rows - HALO :].T)
    ks_own = shift_fwd(seg_full, k_own, k_halo, taps_tiles)
    if multi:
        ks_win = jnp.concatenate([from_prev(ks_own), ks_own], axis=0)
        v_win = jnp.concatenate([from_prev(v_own), v_own], axis=0)
    else:
        ks_win, v_win = ks_own, v_own
    y_mine = exchange(mix_fwd(q_own, ks_win, v_win, kern, seg_q, seg_k))
    resid, act_two, hidden, gz, gr, gy_mine, gln_two = middle_call(
        which, y_mine, x, gain_two, bias_two, cot, out_w, up_w, down_w
    )
    gy_own = exchange(gy_mine)
    output, keep_a, send_a = ffn_grads_call(
        which, y_mine, resid, act_two, hidden, gz, gr, cot, down_w
    )

    gq_own, gks_win, gv_win, gkern = mix_bwd(q_own, ks_win, v_win, gy_own, kern, seg_q, seg_k)
    if multi:
        gks_own = gks_win[span:] + from_next(gks_win[:span].astype(BF)).astype(F32)
        gv_own = (gv_win[run:] + from_next(gv_win[:run].astype(BF)).astype(F32)).astype(BF)
        gks_halo = from_next(gks_own[:HALO].astype(BF)).astype(F32)
    else:
        gks_own, gv_own = gks_win, gv_win
        gks_halo = jnp.zeros((HALO, share), F32)
    gq_mine, gv_mine = exchange(gq_own), exchange(gv_own)
    gk_own, taps_grad = shift_bwd(seg_full, k_own, k_halo, gks_own, gks_halo, taps_tiles)
    gk_mine = exchange(gk_own)
    rate_grad, freq_grad, coef_grad, skip_grad = kern_pull(gkern[:, 0, :])
    keep_b, send_b, ga = qv_grads_call(which, gq_mine, gv_mine, act_one, query_w, value_w)
    keep_c, send_c, input_grad, gln_one = last_call(
        which, gk_mine, act_one, ga, x, gr, gain_one, key_w
    )

    shard = width // fsdp
    wide = w_down.shape[0]
    sum_a = reduce_grads(keep_a, send_a)
    sum_b = reduce_grads(keep_b, send_b)
    key_grad = reduce_grads(keep_c, send_c)
    down_grad = sum_a[:wide]
    up_grad = sum_a[wide : wide + w_up.size // width]
    up_grad = up_grad.reshape(-1, shard, width).transpose(1, 0, 2).reshape(w_up.shape)
    out_grad = sum_a[-shard:]
    query_grad, value_grad = sum_b[:shard], sum_b[shard:]

    by_shard = jnp.concatenate(
        [line.reshape(fsdp, shard) for line in (gln_one[0], gln_one[1], gln_two[0], gln_two[1])], axis=1
    )
    by_group = jnp.concatenate(
        [grad.reshape(-1) for grad in (taps_grad, rate_grad, freq_grad, coef_grad, skip_grad)]
    )
    slots = (jnp.arange(group_count) == group)[:, None]
    packed = jnp.concatenate([by_shard, jnp.where(slots, by_group[None], 0.0)], axis=1)
    long = -(-packed.shape[1] // 1024) * 1024
    packed = jnp.pad(packed, ((0, 0), (0, long - packed.shape[1]))).reshape(fsdp, long // 128, 128)
    mine_sum = jnp.sum(lax.all_to_all(packed, "fsdp", 0, 0), axis=0)
    spread = jnp.broadcast_to(mine_sum[None], (dp,) + mine_sum.shape)
    owned = jnp.sum(lax.all_to_all(spread, "dp", 0, 0), axis=0).reshape(long)
    shapes = [ln1_gain.shape, ln1_bias.shape, ln2_gain.shape, ln2_bias.shape, shift_taps.shape]
    shapes += [ssm_rate.shape, ssm_freq.shape, ssm_coef.shape, ssm_skip.shape]
    little, at = [], 0
    for shape in shapes:
        count = int(np.prod(shape))
        little.append(owned[at : at + count].reshape(shape))
        at += count
    return (
        output.reshape(seqs, rows, width),
        input_grad.reshape(seqs, rows, width),
        little[0],
        little[1],
        query_grad,
        key_grad,
        value_grad,
        little[4],
        little[5],
        little[6],
        little[7],
        little[8],
        out_grad,
        little[2],
        little[3],
        up_grad,
        down_grad,
    )


def solution(mesh):
    return jax.shard_map(
        shards,
        mesh=mesh,
        in_specs=(
            P("fsdp", "dp", None),
            P("fsdp", None),
            P("fsdp"),
            P("fsdp"),
            P("fsdp", None),
            P("fsdp", None),
            P("fsdp", None),
            P(None, "fsdp"),
            P("fsdp", None),
            P("fsdp", None),
            P(None, "fsdp", None),
            P("fsdp"),
            P("fsdp", None),
            P("fsdp"),
            P("fsdp"),
            P("fsdp", None),
            P("fsdp", None),
            P("fsdp", "dp", None),
        ),
        out_specs=(
            P("fsdp", "dp", None),
            P("fsdp", "dp", None),
            P("fsdp"),
            P("fsdp"),
            P("fsdp", None),
            P("fsdp", None),
            P("fsdp", None),
            P(None, "fsdp"),
            P("fsdp", None),
            P("fsdp", None),
            P(None, "fsdp", None),
            P("fsdp"),
            P("fsdp", None),
            P("fsdp"),
            P("fsdp"),
            P("fsdp", None),
            P("fsdp", None),
        ),
        check_vma=False,
    )
```

```python
import functools

import jax
import jax.numpy as jnp
import numpy as np
from jax import lax
from jax.experimental import pallas as pl
from jax.experimental.pallas import tpu as pltpu
from jax.sharding import PartitionSpec as P

SHIFT = 64
HOPS = 8
TILE = 256
HALO = 64
EPS = 1e-05
BF = jnp.bfloat16
F32 = jnp.float32
VMEM_BYTES = 56 * 1024 * 1024


def vmem():
    return pl.BlockSpec(memory_space=pltpu.VMEM)


def smem():
    return pl.BlockSpec(memory_space=pltpu.SMEM)


def hbm():
    return pl.BlockSpec(memory_space=pl.ANY)


def params():
    return pltpu.CompilerParams(vmem_limit_bytes=VMEM_BYTES)


def cost(micros, moved):
    return pl.CostEstimate(flops=int(micros * 1.0e9), bytes_accessed=int(moved), transcendentals=0)


def mm(left, right):
    return lax.dot_general(left, right, (((1,), (0,)), ((), ())), preferred_element_type=F32)


def mm_nt(left, right):
    return lax.dot_general(left, right, (((1,), (1,)), ((), ())), preferred_element_type=F32)


def tn(left, right):
    return lax.dot_general(left, right, (((0,), (0,)), ((), ())), preferred_element_type=F32)


def lane_tiles(width):
    return [(base, min(128, width - base)) for base in range(0, width, 128)]


def fill_ext(ext_ref, first_row, rows, source_ref, width):
    for index, (base, size) in enumerate(lane_tiles(width)):
        if size < 128:
            ext_ref[index, pl.ds(first_row, rows), :] = jnp.zeros((rows, 128), F32)
        ext_ref[index, pl.ds(first_row, rows), 0:size] = source_ref[:, base : base + size].astype(F32)


def fill_ext_t(ext_ref, first_row, source_ref):
    count, width, rows = source_ref.shape
    for index, (base, size) in enumerate(lane_tiles(width)):
        for block in range(count):
            part = source_ref[block, base : base + size, :].astype(F32).T
            if size < 128:
                part = jnp.concatenate([part, jnp.zeros((rows, 128 - size), F32)], axis=1)
            ext_ref[index, pl.ds(first_row + block * rows, rows), :] = part


def shift_fwd_kernel(seg_s, k_ref, halo_ref, taps_ref, segcol_ref, out_ref, ext, seg_b):
    width = k_ref.shape[1]
    rows = k_ref.shape[0] * k_ref.shape[2]
    fill_ext(ext, 0, HALO, halo_ref, width)
    fill_ext_t(ext, HALO, k_ref)
    seg_b[...] = jnp.broadcast_to(segcol_ref[...], seg_b.shape)
    for index, (base, size) in enumerate(lane_tiles(width)):

        def tap_row(lag):
            return taps_ref[index, lag : lag + 1, :]

        def body(tile, carry):
            start = pl.multiple_of(tile * 64, 64)

            def plain():
                total = jnp.zeros((64, 128), F32)
                for lag in range(SHIFT):
                    total = total + ext[index, pl.ds(start + HALO - lag, 64), :] * tap_row(lag)
                return total

            def masked():
                total = jnp.zeros((64, 128), F32)
                now = seg_b[pl.ds(start + HALO, 64), :]
                for lag in range(SHIFT):
                    same = seg_b[pl.ds(start + HALO - lag, 64), :] == now
                    part = ext[index, pl.ds(start + HALO - lag, 64), :] * tap_row(lag)
                    total = total + jnp.where(same, part, 0.0)
                return total

            total = lax.cond(seg_s[start + 1] == seg_s[start + HALO + 63], plain, masked)
            out_ref[pl.ds(start, 64), base : base + size] = total[:, 0:size].astype(BF)
            return carry

        lax.fori_loop(0, rows // 64, body, 0)


def shift_fwd(seg_full, k_own, k_halo, taps):
    width = k_own.shape[1]
    rows = k_own.shape[0] * k_own.shape[2]
    tiles = len(lane_tiles(width))
    return pl.pallas_call(
        shift_fwd_kernel,
        out_shape=jax.ShapeDtypeStruct((rows, width), BF),
        in_specs=[smem(), vmem(), vmem(), vmem(), vmem()],
        out_specs=vmem(),
        scratch_shapes=[
            pltpu.VMEM((tiles, HALO + rows, 128), F32),
            pltpu.VMEM((HALO + rows, 128), jnp.int32),
        ],
        compiler_params=params(),
        cost_estimate=cost(12, 2 << 20),
        name="shift_fwd",
    )(seg_full, k_own, k_halo, taps, seg_full[: HALO + rows, None])


def shift_bwd_kernel(
    me_ref, seg_s, k_ref, halo_ref, g_ref, ghalo_ref, taps_ref, segcol_ref, tg_ref, *rest
):
    outs, (ext, gext, seg_b, acc, gk_rows) = rest[:-5], rest[-5:]
    width = k_ref.shape[1]
    rows = k_ref.shape[0] * k_ref.shape[2]
    fill_ext(ext, 0, HALO, halo_ref, width)
    fill_ext_t(ext, HALO, k_ref)
    fill_ext(gext, 0, rows, g_ref, width)
    fill_ext(gext, rows, HALO, ghalo_ref, width)
    seg_b[...] = jnp.broadcast_to(segcol_ref[...], seg_b.shape)
    acc[...] = jnp.zeros_like(acc)
    for index, (base, size) in enumerate(lane_tiles(width)):

        def tap_row(lag):
            return taps_ref[index, lag : lag + 1, :]

        def fold(part):
            total = part[0:8]
            for piece in range(1, 8):
                total = total + part[8 * piece : 8 * piece + 8]
            return total

        def body(tile, carry):
            start = pl.multiple_of(tile * 64, 64)

            def plain():
                total = jnp.zeros((64, 128), F32)
                for lag in range(SHIFT):
                    total = total + gext[index, pl.ds(start + lag, 64), :] * tap_row(lag)
                return total

            def masked():
                total = jnp.zeros((64, 128), F32)
                now = seg_b[pl.ds(start + HALO, 64), :]
                for lag in range(SHIFT):
                    same = seg_b[pl.ds(start + HALO + lag, 64), :] == now
                    part = gext[index, pl.ds(start + lag, 64), :] * tap_row(lag)
                    total = total + jnp.where(same, part, 0.0)
                return total

            total = lax.cond(seg_s[start + HALO] == seg_s[start + HALO + 126], plain, masked)
            gk_rows[index, pl.ds(start, 64), :] = total
            grad = gext[index, pl.ds(start, 64), :]
            clear = seg_s[start + 1] == seg_s[start + HALO + 63]

            @pl.when(clear)
            def _():
                for lag in range(SHIFT):
                    part = ext[index, pl.ds(start + HALO - lag, 64), :] * grad
                    acc[index, lag] = acc[index, lag] + fold(part)

            @pl.when(jnp.logical_not(clear))
            def _():
                now = seg_b[pl.ds(start + HALO, 64), :]
                for lag in range(SHIFT):
                    same = seg_b[pl.ds(start + HALO - lag, 64), :] == now
                    part = ext[index, pl.ds(start + HALO - lag, 64), :] * grad
                    acc[index, lag] = acc[index, lag] + fold(jnp.where(same, part, 0.0))

            return carry

        lax.fori_loop(0, rows // 64, body, 0)
        tg_ref[:, base : base + size] = jnp.sum(acc[index], axis=1)[:, 0:size]
        for mask, out in enumerate(outs):
            there = pl.ds(pl.multiple_of((me_ref[1] ^ mask) * TILE, TILE), TILE)
            out[base : base + size, :] = gk_rows[index, there, :].T[0:size].astype(BF)


def shift_bwd(me, seg_full, k_own, k_halo, grad, grad_halo, taps):
    count, width, _ = k_own.shape
    rows = count * TILE
    tiles = len(lane_tiles(width))
    return pl.pallas_call(
        shift_bwd_kernel,
        out_shape=(
            jax.ShapeDtypeStruct((SHIFT, width), F32),
            *[jax.ShapeDtypeStruct((width, TILE), BF)] * count,
        ),
        in_specs=[smem(), smem()] + [vmem()] * 6,
        out_specs=(vmem(),) * (1 + count),
        scratch_shapes=[
            pltpu.VMEM((tiles, HALO + rows, 128), F32),
            pltpu.VMEM((tiles, HALO + rows, 128), F32),
            pltpu.VMEM((2 * HALO + rows, 128), jnp.int32),
            pltpu.VMEM((tiles, SHIFT, 8, 128), F32),
            pltpu.VMEM((tiles, rows, 128), F32),
        ],
        compiler_params=params(),
        cost_estimate=cost(25, 4 << 20),
        name="shift_bwd",
    )(me, seg_full, k_own, k_halo, grad, grad_halo, taps, seg_full[:, None])


def tile_table(query_blocks, key_blocks, unroll):
    offset = key_blocks - query_blocks
    pairs = []
    for distance in range(HOPS + 1):
        for row in range(query_blocks):
            if row + offset - distance >= 0:
                pairs.append((row, row + offset - distance))
    assert len(pairs) % unroll == 0
    return np.array(pairs, np.int32)


def build_bands(bands, row):
    length = row.shape[1]
    skewed = pltpu.roll(jnp.broadcast_to(row, (8, length)), 0, 1, stride=1, stride_axis=0)
    for step in range(16):
        bands[step] = pltpu.roll(skewed, 8 * step, 1) if step else skewed


def read_band(bands, first, second):
    upper = bands[:, :, pl.ds(first, TILE)].reshape(128, TILE)
    lower = bands[:, :, pl.ds(second, TILE)].reshape(128, TILE)
    return jnp.concatenate([upper, lower], axis=0)


UNROLL_F = 4
UNROLL_B = 2


def head_rows(dest, source, heads, size):
    for head in range(heads):
        dest[head] = source[:, head * size : (head + 1) * size]


def head_turn(dest, source, heads, size, base=0):
    for head in range(heads):
        for block in range(source.shape[0]):
            part = source[block, base + head * size : base + (head + 1) * size, :].astype(F32)
            dest[head, block * TILE : (block + 1) * TILE, :] = part.T.astype(dest.dtype)


def mix_fwd_kernel(v_base, tab, q_ref, k_ref, v_ref, row_ref, segq_ref, segk_ref, y_ref, kh, yacc, bands, seg_b):
    heads, length = row_ref.shape[0], row_ref.shape[2]
    size = k_ref.shape[1] // heads
    offset = v_ref.shape[0] - q_ref.shape[0]
    tiles = tab.shape[0]
    head_rows(kh, k_ref, heads, size)
    seg_b[...] = jnp.broadcast_to(segk_ref[...], seg_b.shape)
    yacc[...] = jnp.zeros_like(yacc)

    def head_body(head, carry):
        build_bands(bands, row_ref[head])
        own = pl.ds(pl.multiple_of(head * size, size), size)
        own_v = pl.ds(pl.multiple_of(v_base + head * size, size), size)

        def body(step, carry):
            for unrolled in range(UNROLL_F):
                row = tab[step * UNROLL_F + unrolled, 0]
                col = tab[step * UNROLL_F + unrolled, 1]
                cols = pl.ds(pl.multiple_of(col * TILE, TILE), TILE)
                first = pl.multiple_of(TILE + TILE * (row + offset - col), TILE)
                kern = read_band(bands, first, pl.multiple_of(first - 128, 128))
                score = mm(kh[head, cols, :], q_ref[row, own, :])
                seg_now = seg_b[cols, :]
                live = jnp.concatenate([seg_now, seg_now], axis=1) == segq_ref[row]
                weight = jnp.where(live, score * kern, 0.0).astype(BF)
                yacc[row, own, :] += mm(v_ref[col, own_v, :], weight)
            return carry

        lax.fori_loop(0, tiles // UNROLL_F, body, 0)
        return carry

    lax.fori_loop(0, heads, head_body, 0)
    y_ref[...] = yacc[...].astype(BF)


def mix_fwd(q, k_win, v_win, kern_asc, seg_q, seg_k):
    blocks = q.shape[0]
    wide, width = k_win.shape
    shape = (blocks, width, TILE)
    heads, _, length = kern_asc.shape
    size = width // heads
    table = tile_table(blocks, wide // TILE, UNROLL_F)
    return pl.pallas_call(
        functools.partial(mix_fwd_kernel, v_win.shape[1] - width),
        out_shape=jax.ShapeDtypeStruct(shape, BF),
        in_specs=[smem()] + [vmem()] * 6,
        out_specs=vmem(),
        scratch_shapes=[
            pltpu.VMEM((heads, wide, size), BF),
            pltpu.VMEM(shape, F32),
            pltpu.VMEM((16, 8, length), F32),
            pltpu.VMEM((wide, 128), jnp.int32),
        ],
        compiler_params=params(),
        cost_estimate=cost(20, 4 << 20),
        name="mix_fwd",
    )(table, q, k_win, v_win, kern_asc, seg_q.reshape(blocks, 1, TILE), seg_k[:, None])


def mix_bwd_kernel(
    v_base, tab, q_ref, k_ref, v_ref, g_ref, row_ref, segq_ref, segk_ref, gq_ref, gk_ref, gv_ref, gkern_ref,
    qh, kh, vh, gh, kt, gqt, gkacc, gvacc, bands, gbands, seg_b,
):
    heads, length = row_ref.shape[0], row_ref.shape[2]
    size = k_ref.shape[1] // heads
    query_blocks, key_blocks = q_ref.shape[0], v_ref.shape[0]
    offset = key_blocks - query_blocks
    tiles = tab.shape[0]
    head_turn(qh, q_ref, heads, size)
    head_rows(kh, k_ref, heads, size)
    head_turn(vh, v_ref, heads, size, v_base)
    head_turn(gh, g_ref, heads, size)
    for head in range(heads):
        for block in range(key_blocks):
            part = kh[head, block * TILE : (block + 1) * TILE, :].astype(F32)
            kt[block, head * size : (head + 1) * size, :] = part.T.astype(BF)
    seg_b[...] = jnp.broadcast_to(segk_ref[...], seg_b.shape)
    gqt[...] = jnp.zeros_like(gqt)
    gkacc[...] = jnp.zeros_like(gkacc)
    gvacc[...] = jnp.zeros_like(gvacc)

    def head_body(head, carry):
        build_bands(bands, row_ref[head])
        gbands[...] = jnp.zeros_like(gbands)
        own = pl.ds(pl.multiple_of(head * size, size), size)

        def body(step, carry):
            for unrolled in range(UNROLL_B):
                row = tab[step * UNROLL_B + unrolled, 0]
                col = tab[step * UNROLL_B + unrolled, 1]
                rows = pl.ds(pl.multiple_of(row * TILE, TILE), TILE)
                cols = pl.ds(pl.multiple_of(col * TILE, TILE), TILE)
                first = pl.multiple_of(TILE + TILE * (row + offset - col), TILE)
                second = pl.multiple_of(first - 128, 128)
                kern = read_band(bands, first, second)
                score = mm(kh[head, cols, :], q_ref[row, own, :])
                grad = mm(vh[head, cols, :], g_ref[row, own, :])
                seg_now = seg_b[cols, :]
                live = jnp.concatenate([seg_now, seg_now], axis=1) == segq_ref[row]
                grad = jnp.where(live, grad, 0.0)
                weight = jnp.where(live, score * kern, 0.0).astype(BF)
                gscore = (grad * kern).astype(BF)
                both = grad * score
                gbands[:, :, pl.ds(first, TILE)] += both[0:128].reshape(16, 8, TILE)
                gbands[:, :, pl.ds(second, TILE)] += both[128:256].reshape(16, 8, TILE)
                gkacc[head, cols, :] += mm(gscore, qh[head, rows, :])
                gvacc[head, cols, :] += mm(weight, gh[head, rows, :])
                gqt[row, own, :] += mm(kt[col, own, :], gscore)
            return carry

        lax.fori_loop(0, tiles // UNROLL_B, body, 0)
        total = gbands[0]
        for step in range(1, 16):
            total = total + pltpu.roll(gbands[step], length - 8 * step, 1)
        line = total[0:1]
        for sub in range(1, 8):
            line = line + pltpu.roll(total, length - sub, 1)[sub : sub + 1]
        gkern_ref[head] = line
        return carry

    lax.fori_loop(0, heads, head_body, 0)
    gq_ref[:, 0 : heads * size, :] = gqt[...].astype(BF)
    for head in range(heads):
        gk_ref[:, head * size : (head + 1) * size] = gkacc[head]
        for block in range(key_blocks):
            part = gvacc[head, block * TILE : (block + 1) * TILE, :].T
            gv_ref[block, v_base + head * size : v_base + (head + 1) * size, :] = part.astype(gv_ref.dtype)


def mix_bwd_merged(v_base, *refs):
    mix_bwd_kernel(v_base, *refs[:8], refs[8], refs[9], refs[8], *refs[10:])


def mix_bwd(q, k_win, v_win, grad, kern_asc, seg_q, seg_k):
    blocks = q.shape[0]
    wide, width = k_win.shape
    heads, _, length = kern_asc.shape
    size = width // heads
    rows = blocks * TILE
    shape = (blocks, width, TILE)
    table = tile_table(blocks, wide // TILE, UNROLL_B)
    v_base = v_win.shape[1] - width
    outs = [
        jax.ShapeDtypeStruct((blocks, v_win.shape[1], TILE), BF),
        jax.ShapeDtypeStruct((wide, width), F32),
        jax.ShapeDtypeStruct((heads, 1, length), F32),
    ]
    if not v_base:
        outs.insert(2, jax.ShapeDtypeStruct(v_win.shape, F32))
    return pl.pallas_call(
        functools.partial(mix_bwd_merged if v_base else mix_bwd_kernel, v_base),
        out_shape=tuple(outs),
        in_specs=[smem()] + [vmem()] * 7,
        out_specs=(vmem(),) * len(outs),
        scratch_shapes=[
            pltpu.VMEM((heads, rows, size), BF),
            pltpu.VMEM((heads, wide, size), BF),
            pltpu.VMEM((heads, wide, size), BF),
            pltpu.VMEM((heads, rows, size), BF),
            pltpu.VMEM((wide // TILE, width, TILE), BF),
            pltpu.VMEM(shape, F32),
            pltpu.VMEM((heads, wide, size), F32),
            pltpu.VMEM((heads, wide, size), F32),
            pltpu.VMEM((16, 8, length), F32),
            pltpu.VMEM((16, 8, length), F32),
            pltpu.VMEM((wide, 128), jnp.int32),
        ],
        compiler_params=params(),
        cost_estimate=cost(40, 8 << 20),
        name="mix_bwd",
    )(table, q, k_win, v_win, grad, kern_asc, seg_q.reshape(blocks, 1, TILE), seg_k[:, None])


def load_pieces(me, pieces, full, sem, base):
    rows = pieces[0].shape[0]
    copies = []
    for mask, piece in enumerate(pieces):
        place = pl.ds(pl.multiple_of((me ^ mask) * rows, 64), rows)
        copies.append(pltpu.make_async_copy(piece, full.at[place], sem.at[base + mask]))
    for copy in copies:
        copy.start()

    def wait():
        for copy in copies:
            copy.wait()

    return wait


def normal_stats(value):
    center = value - jnp.mean(value, axis=-1, keepdims=True)
    scale = lax.rsqrt(jnp.mean(center * center, axis=-1, keepdims=True) + EPS)
    return center * scale, scale


def normal_grad(grad, hat, scale, gain):
    lead = grad * gain
    first = jnp.mean(lead, axis=-1, keepdims=True)
    second = jnp.mean(lead * hat, axis=-1, keepdims=True)
    return scale * (lead - first - hat * second)


def to_blocks(dest, turned, seqs, groups, base=0):
    share = turned.shape[0] // groups
    for seq in range(seqs):
        for group in range(groups):
            dest[seq * groups + group, base : base + share, :] = turned[
                group * share : (group + 1) * share, seq * TILE : (seq + 1) * TILE
            ]


def from_blocks(dest, blocks, seqs, groups, base=0):
    share = dest.shape[1] // groups
    for seq in range(seqs):
        whole = jnp.concatenate(
            [blocks[seq * groups + group, base : base + share, :] for group in range(groups)], axis=0
        )
        dest[seq * TILE : (seq + 1) * TILE, :] = whole.astype(F32).T.astype(BF)


def turn(value):
    return value.astype(F32).T.astype(BF)


def key_kernel(me_ref, x_ref, gain_ref, bias_ref, w0, w1, w2, w3, act_ref, out_ref, full, sem):
    wait = load_pieces(me_ref[0], (w0, w1, w2, w3), full, sem, 0)
    groups = full.shape[0] // out_ref.shape[1]
    seqs = x_ref.shape[0] // TILE
    hat, _ = normal_stats(x_ref[...].astype(F32))
    act_ref[...] = (hat * gain_ref[...] + bias_ref[...]).astype(BF)
    wait()
    to_blocks(out_ref, mm(act_ref[...], full[...]).T.astype(BF), seqs, groups)


def key_call(me, x, gain, bias, pieces, blocks):
    tokens, width = x.shape
    return pl.pallas_call(
        key_kernel,
        out_shape=(
            jax.ShapeDtypeStruct((tokens, width), BF),
            jax.ShapeDtypeStruct(blocks, BF),
        ),
        in_specs=[smem()] + [vmem()] * 3 + [hbm()] * 4,
        out_specs=(vmem(), vmem()),
        scratch_shapes=[pltpu.VMEM((width, width), BF), pltpu.SemaphoreType.DMA((4,))],
        compiler_params=params(),
        cost_estimate=cost(0.1, 1 << 16),
        name="key_call",
    )(me, x, gain, bias, *pieces)


def query_value_kernel(me_ref, act_ref, q0, q1, q2, q3, v0, v1, v2, v3, *rest):
    outs, (qfull, vfull, turned, sem) = rest[:-4], rest[-4:]
    wait_q = load_pieces(me_ref[0], (q0, q1, q2, q3), qfull, sem, 0)
    wait_v = load_pieces(me_ref[0], (v0, v1, v2, v3), vfull, sem, 4)
    share = outs[0].shape[0] // 2
    wait_q()
    turned[0] = mm(act_ref[...], qfull[...]).T.astype(BF)
    wait_v()
    turned[1] = mm(act_ref[...], vfull[...]).T.astype(BF)
    groups = qfull.shape[0] // share
    for mask, out in enumerate(outs):
        there = me_ref[1] ^ mask
        features = pl.ds(pl.multiple_of((there % groups) * share, 64), share)
        tokens = pl.ds(pl.multiple_of((there // groups) * TILE, TILE), TILE)
        out[0:share, :] = turned[0, features, tokens]
        out[share : 2 * share, :] = turned[1, features, tokens]


def query_value_call(me, act, q_pieces, v_pieces, blocks):
    width = act.shape[1]
    return pl.pallas_call(
        query_value_kernel,
        out_shape=(jax.ShapeDtypeStruct((2 * blocks[1], blocks[2]), BF),) * blocks[0],
        in_specs=[smem(), vmem()] + [hbm()] * 8,
        out_specs=(vmem(),) * blocks[0],
        scratch_shapes=[
            pltpu.VMEM((width, width), BF),
            pltpu.VMEM((width, width), BF),
            pltpu.VMEM((2, width, act.shape[0]), BF),
            pltpu.SemaphoreType.DMA((8,)),
        ],
        compiler_params=params(),
        cost_estimate=cost(0.1, 1 << 16),
        name="query_value_call",
    )(me, act, *q_pieces, *v_pieces)


GELU_A = 0.7978845608028654
GELU_B = 0.044715


def middle_kernel(
    me_ref, y_ref, x_ref, gain_ref, bias_ref, cot_ref, o0, o1, o2, o3, u0, u1, u2, u3, d0, d1, d2, d3,
    resid_ref, act_ref, hidden_ref, gz_ref, gr_ref, gy_ref, gln_ref,
    ofull, ufull, dfull, mixed, hat, gb, sem,
):
    me = me_ref[0]
    wait_o = load_pieces(me, (o0, o1, o2, o3), ofull, sem, 0)
    wait_u = load_pieces(me, (u0, u1, u2, u3), ufull, sem, 4)
    wait_d = load_pieces(me, (d0, d1, d2, d3), dfull, sem, 8)
    tokens, width = x_ref.shape
    groups = width // y_ref.shape[1]
    seqs = tokens // TILE
    chunk = width
    chunks = ufull.shape[1] // chunk
    from_blocks(mixed, y_ref, seqs, groups)
    wait_o()
    resid_ref[...] = x_ref[...].astype(F32) + mm(mixed[...], ofull[...])
    normed, scale = normal_stats(resid_ref[...])
    hat[...] = normed
    act_ref[...] = (normed * gain_ref[...] + bias_ref[...]).astype(BF)
    gb[...] = jnp.zeros_like(gb)
    wait_u()
    wait_d()

    def body(step, carry):
        rows = pl.ds(pl.multiple_of((step % seqs) * TILE, TILE), TILE)
        cols = pl.ds(pl.multiple_of((step // seqs) * chunk, chunk), chunk)
        z = mm(act_ref[rows, :], ufull[:, cols])
        dh = mm_nt(cot_ref[rows, :], dfull[cols, :])
        square = z * z
        t = jnp.tanh(GELU_A * z * (1.0 + GELU_B * square))
        half = 0.5 * (1.0 + t)
        hidden_ref[rows, cols] = (z * half).astype(BF)
        slope = half + 0.5 * z * (1.0 - t * t) * (GELU_A * (1.0 + 3.0 * GELU_B * square))
        gz = (slope * dh).astype(BF)
        gz_ref[rows, cols] = gz
        gb[rows, :] += mm_nt(gz, ufull[:, cols])
        return carry

    lax.fori_loop(0, seqs * chunks, body, 0)
    gln_ref[0:1, :] = jnp.sum(gb[...] * hat[...], axis=0, keepdims=True)
    gln_ref[1:2, :] = jnp.sum(gb[...], axis=0, keepdims=True)
    gr_ref[...] = cot_ref[...].astype(F32) + normal_grad(gb[...], hat[...], scale, gain_ref[...])
    to_blocks(gy_ref, mm_nt(ofull[...], gr_ref[...].astype(BF)).astype(BF), seqs, groups)


def middle_call(me, y, x, gain, bias, cot, o_pieces, u_pieces, d_pieces):
    tokens, width = x.shape
    hidden = u_pieces[0].shape[1]
    return pl.pallas_call(
        middle_kernel,
        out_shape=(
            jax.ShapeDtypeStruct((tokens, width), F32),
            jax.ShapeDtypeStruct((tokens, width), BF),
            jax.ShapeDtypeStruct((tokens, hidden), BF),
            jax.ShapeDtypeStruct((tokens, hidden), BF),
            jax.ShapeDtypeStruct((tokens, width), F32),
            jax.ShapeDtypeStruct(y.shape, BF),
            jax.ShapeDtypeStruct((2, width), F32),
        ),
        in_specs=[smem()] + [vmem()] * 5 + [hbm()] * 12,
        out_specs=(vmem(),) * 7,
        scratch_shapes=[
            pltpu.VMEM((width, width), BF),
            pltpu.VMEM((width, hidden), BF),
            pltpu.VMEM((hidden, width), BF),
            pltpu.VMEM((tokens, width), BF),
            pltpu.VMEM((tokens, width), F32),
            pltpu.VMEM((tokens, width), F32),
            pltpu.SemaphoreType.DMA((12,)),
        ],
        compiler_params=params(),
        cost_estimate=cost(15, 24 << 20),
        name="middle_call",
    )(me, y, x, gain, bias, cot, *o_pieces, *u_pieces, *d_pieces)


def down_grads_kernel(me_ref, hidden_ref, cot_ref, keep_ref, send_ref):
    me = me_ref[0]
    wide = keep_ref.shape[1]
    for slot in range(2):
        for dest, mask in ((keep_ref, 2 * slot), (send_ref, 2 * slot + 1)):
            part = hidden_ref[:, pl.ds(pl.multiple_of((me ^ mask) * wide, wide), wide)]
            dest[slot] = mm(turn(part), cot_ref[...]).astype(dest.dtype)


def down_grads_call(me, hidden, cot, shards_count):
    width = cot.shape[1]
    wide = hidden.shape[1] // shards_count
    return pl.pallas_call(
        down_grads_kernel,
        out_shape=(
            jax.ShapeDtypeStruct((2, wide, width), F32),
            jax.ShapeDtypeStruct((2, wide, width), BF),
        ),
        in_specs=[smem()] + [vmem()] * 2,
        out_specs=(vmem(),) * 2,
        compiler_params=params(),
        cost_estimate=cost(6, 16 << 20),
        name="down_grads_call",
    )(me, hidden, cot)


def up_grads_kernel(
    me_ref, y_ref, resid_ref, act_ref, hidden_ref, gz_ref, gr_ref, d0, d1, d2, d3,
    out_ref, keep_ref, send_ref, dfull, act_t, low, sem,
):
    me = me_ref[0]
    wait_d = load_pieces(me, (d0, d1, d2, d3), dfull, sem, 0)
    tokens, width = resid_ref.shape
    hidden = hidden_ref.shape[1]
    groups = width // y_ref.shape[1]
    share = width // groups
    seqs = tokens // TILE
    act_t[...] = turn(act_ref[...])
    low[...] = gr_ref[...].astype(BF)
    blocks = hidden // width
    for slot in range(2):
        for dest, mask in ((keep_ref, 2 * slot), (send_ref, 2 * slot + 1)):
            owner = me ^ mask
            part = act_t[pl.ds(pl.multiple_of(owner * share, share), share), :]
            for block in range(blocks):
                value = mm(part, gz_ref[:, block * width : (block + 1) * width])
                dest[slot, block * share : (block + 1) * share, :] = value.astype(dest.dtype)
            value = mm(y_ref[owner], low[0:TILE, :])
            for seq in range(1, seqs):
                value = value + mm(y_ref[seq * groups + owner], low[seq * TILE : (seq + 1) * TILE, :])
            dest[slot, blocks * share : (blocks + 1) * share, :] = value.astype(dest.dtype)
    wait_d()
    out_ref[...] = (resid_ref[...] + mm(hidden_ref[...], dfull[...])).astype(BF)


def up_grads_call(me, y, resid, act, hidden, gz, gr, d_pieces):
    tokens, width = resid.shape
    wide = hidden.shape[1]
    groups = width // y.shape[1]
    rows = (wide // width + 1) * (width // groups)
    return pl.pallas_call(
        up_grads_kernel,
        out_shape=(
            jax.ShapeDtypeStruct((tokens, width), BF),
            jax.ShapeDtypeStruct((2, rows, width), F32),
            jax.ShapeDtypeStruct((2, rows, width), BF),
        ),
        in_specs=[smem()] + [vmem()] * 6 + [hbm()] * 4,
        out_specs=(vmem(),) * 3,
        scratch_shapes=[
            pltpu.VMEM((wide, width), BF),
            pltpu.VMEM((width, tokens), BF),
            pltpu.VMEM((tokens, width), BF),
            pltpu.SemaphoreType.DMA((4,)),
        ],
        compiler_params=params(),
        cost_estimate=cost(10, 24 << 20),
        name="up_grads_call",
    )(me, y, resid, act, hidden, gz, gr, *d_pieces)


def input_grads(me, act_t, grad, share, base, keep_ref, send_ref):
    for slot in range(2):
        for dest, mask in ((keep_ref, 2 * slot), (send_ref, 2 * slot + 1)):
            part = act_t[pl.ds(pl.multiple_of((me ^ mask) * share, share), share), :]
            dest[slot, base : base + share, :] = mm(part, grad).astype(dest.dtype)


def qv_grads_kernel(
    me_ref, gqv_ref, act_ref, q0, q1, q2, q3, v0, v1, v2, v3,
    keep_ref, send_ref, ga_ref, qfull, vfull, act_t, rows, sem,
):
    me = me_ref[0]
    wait_q = load_pieces(me, (q0, q1, q2, q3), qfull, sem, 0)
    wait_v = load_pieces(me, (v0, v1, v2, v3), vfull, sem, 4)
    tokens, width = act_ref.shape
    share = gqv_ref.shape[1] // 2
    groups = width // share
    seqs = tokens // TILE
    act_t[...] = turn(act_ref[...])
    from_blocks(rows, gqv_ref, seqs, groups)
    input_grads(me, act_t, rows[...], share, 0, keep_ref, send_ref)
    wait_q()
    ga_ref[...] = mm_nt(rows[...], qfull[...])
    from_blocks(rows, gqv_ref, seqs, groups, share)
    input_grads(me, act_t, rows[...], share, share, keep_ref, send_ref)
    wait_v()
    ga_ref[...] += mm_nt(rows[...], vfull[...])


def qv_grads_call(me, gqv, act, q_pieces, v_pieces):
    tokens, width = act.shape
    share = gqv.shape[1] // 2
    return pl.pallas_call(
        qv_grads_kernel,
        out_shape=(
            jax.ShapeDtypeStruct((2, 2 * share, width), F32),
            jax.ShapeDtypeStruct((2, 2 * share, width), BF),
            jax.ShapeDtypeStruct((tokens, width), F32),
        ),
        in_specs=[smem()] + [vmem()] * 2 + [hbm()] * 8,
        out_specs=(vmem(),) * 3,
        scratch_shapes=[
            pltpu.VMEM((width, width), BF),
            pltpu.VMEM((width, width), BF),
            pltpu.VMEM((width, tokens), BF),
            pltpu.VMEM((tokens, width), BF),
            pltpu.SemaphoreType.DMA((8,)),
        ],
        compiler_params=params(),
        cost_estimate=cost(8, 12 << 20),
        name="qv_grads_call",
    )(me, gqv, act, *q_pieces, *v_pieces)


def last_kernel(
    me_ref, gk_ref, act_ref, ga_ref, x_ref, gr_ref, gain_ref, k0, k1, k2, k3,
    keep_ref, send_ref, gx_ref, gln_ref, kfull, act_t, rows, sem,
):
    me = me_ref[0]
    wait_k = load_pieces(me, (k0, k1, k2, k3), kfull, sem, 0)
    tokens, width = act_ref.shape
    share = gk_ref.shape[1]
    act_t[...] = turn(act_ref[...])
    from_blocks(rows, gk_ref, tokens // TILE, width // share)
    input_grads(me, act_t, rows[...], share, 0, keep_ref, send_ref)
    wait_k()
    ga = ga_ref[...] + mm_nt(rows[...], kfull[...])
    hat, scale = normal_stats(x_ref[...].astype(F32))
    gln_ref[0:1, :] = jnp.sum(ga * hat, axis=0, keepdims=True)
    gln_ref[1:2, :] = jnp.sum(ga, axis=0, keepdims=True)
    gx_ref[...] = (gr_ref[...] + normal_grad(ga, hat, scale, gain_ref[...])).astype(BF)


def last_call(me, gk, act, ga, x, gr, gain, k_pieces):
    tokens, width = act.shape
    share = gk.shape[1]
    return pl.pallas_call(
        last_kernel,
        out_shape=(
            jax.ShapeDtypeStruct((2, share, width), F32),
            jax.ShapeDtypeStruct((2, share, width), BF),
            jax.ShapeDtypeStruct((tokens, width), BF),
            jax.ShapeDtypeStruct((2, width), F32),
        ),
        in_specs=[smem()] + [vmem()] * 6 + [hbm()] * 4,
        out_specs=(vmem(),) * 4,
        scratch_shapes=[
            pltpu.VMEM((width, width), BF),
            pltpu.VMEM((width, tokens), BF),
            pltpu.VMEM((tokens, width), BF),
            pltpu.SemaphoreType.DMA((4,)),
        ],
        compiler_params=params(),
        cost_estimate=cost(6, 8 << 20),
        name="last_call",
    )(me, gk, act, ga, x, gr, gain, *k_pieces)


def xor_permute(value, axis, mask):
    count = lax.axis_size(axis)
    return lax.ppermute(value, axis, [(source, source ^ mask) for source in range(count)])


def collect_kernel(me_ref, *refs):
    parts, out = refs[:-1], refs[-1]
    for mask, part in enumerate(parts):
        out[me_ref[1] ^ mask] = part[...]


def swap_parts(me, parts, label):
    came = [parts[0]] + [xor_permute(part, "dp", mask) for mask, part in enumerate(parts) if mask]
    shape = (len(parts),) + parts[0].shape
    return pl.pallas_call(
        collect_kernel,
        out_shape=jax.ShapeDtypeStruct(shape, BF),
        in_specs=[smem()] + [vmem()] * len(parts),
        out_specs=vmem(),
        compiler_params=params(),
        cost_estimate=cost(0.5, 2 << 20),
        name=label,
    )(me, *came)


def gather_pieces(shard):
    across = xor_permute(shard, "fsdp", 2)
    beside = xor_permute(shard, "fsdp", 1)
    both = xor_permute(across, "fsdp", 1)
    return (shard, beside, across, both)


class Order:
    def __init__(self):
        self.last = None

    def __call__(self, value):
        if self.last is None:
            return value
        return lax.optimization_barrier((value, self.last))[0]

    def mark(self, value):
        self.last = value
        return value


def split_half(value, bit):
    halves = value.reshape((2, value.shape[0] // 2) + value.shape[1:])
    keep = lax.dynamic_index_in_dim(halves, bit, 0, keepdims=False)
    return keep, lax.dynamic_index_in_dim(halves, 1 - bit, 0, keepdims=False)


def join_halves(own, other, bit):
    first = jnp.where(bit == 0, own, other)
    second = jnp.where(bit == 0, other, own)
    return jnp.concatenate([first, second], axis=0)


DP_MASKS = (1, 2, 4)


class Reduction:
    def __init__(self, order, keep, send):
        self.order = order
        self.keep = keep
        self.move = send
        self.me = lax.axis_index("dp")
        self.binary = lax.axis_size("dp") == 8
        steps = [self.core, self.high]
        steps += [functools.partial(self.scatter, index) for index in range(3)]
        steps += [functools.partial(self.gather, index) for index in (2, 1, 0)]
        self.steps = steps if self.binary else steps[:2]

    def next(self):
        if self.steps:
            self.steps.pop(0)()
            self.order.mark(self.move)

    def core(self):
        came = xor_permute(self.move, "fsdp", 1)
        keep = self.order(self.keep)
        self.keep = keep[0] + came[0].astype(F32)
        self.move = (keep[1] + came[1].astype(F32)).astype(BF)

    def high(self):
        self.total = self.order(self.keep) + xor_permute(self.move, "fsdp", 2).astype(F32)
        self.cut(0)

    def cut(self, index):
        self.keep, send = split_half(self.total, (self.me // DP_MASKS[index]) % 2)
        self.move = send.astype(BF)

    def scatter(self, index):
        self.total = self.order(self.keep) + xor_permute(self.move, "dp", DP_MASKS[index]).astype(F32)
        if index < 2:
            self.cut(index + 1)
        else:
            self.move = self.total.astype(BF)

    def gather(self, index):
        other = xor_permute(self.move, "dp", DP_MASKS[index])
        self.move = join_halves(self.order(self.move), other, (self.me // DP_MASKS[index]) % 2)

    def result(self):
        while self.steps:
            self.next()
        if self.binary:
            return self.move.astype(F32)
        rows, cols = self.total.shape
        count = lax.axis_size("dp")
        split = self.total.astype(BF).reshape(count, rows // count, cols)
        owned = jnp.sum(lax.all_to_all(split, "dp", 0, 0).astype(F32), axis=0).astype(BF)
        spread = jnp.broadcast_to(owned[None], (count,) + owned.shape)
        return lax.all_to_all(spread, "dp", 0, 0).reshape(rows, cols).astype(F32)


class SmallSum:
    def __init__(self, order, common, grouped, group_bits):
        self.order = order
        self.common = common
        self.value = jnp.concatenate([common, grouped])
        size = lax.axis_size("dp")
        masks = [1 << bit for bit in range(size.bit_length() - 1)]
        self.group_bits = group_bits
        self.steps = [("fsdp", 1), ("fsdp", 2)]
        self.steps += [("dp", mask) for mask in masks if mask not in group_bits]
        self.steps += [("dp", mask) for mask in masks if mask in group_bits]
        self.stacks = None

    def next(self):
        if not self.steps:
            return
        axis, mask = self.steps.pop(0)
        size = self.common.shape[0]
        if axis == "dp" and mask in self.group_bits:
            if self.stacks is None:
                self.stacks = self.value[None, size:]
                self.value = self.value[:size]
            lines = self.stacks.shape[0]
            sent = jnp.concatenate([self.value, self.stacks.reshape(-1)])
            came = xor_permute(sent, axis, mask)
            self.value = self.order(self.value) + came[:size]
            other = came[size:].reshape(self.stacks.shape)
            bit = (lax.axis_index("dp") // mask) % 2
            self.stacks = join_halves(self.stacks, other, bit)
            self.order.mark(self.value)
        else:
            came = xor_permute(self.value, axis, mask)
            self.value = self.order(self.value) + came
            self.order.mark(self.value)

    def result(self, place):
        while self.steps:
            self.next()
        return self.value, lax.dynamic_index_in_dim(self.stacks, place, 0, keepdims=False)


def kernel_rows(rate, freq, coef, skip, lags, reach):
    lag = lags.astype(F32)
    inside = (lags >= 0) & (lags < reach)
    clipped = jnp.where(inside, lag, 0.0)
    decay = jnp.exp(-rate[:, :, None] * clipped)
    angle = freq[:, :, None] * clipped
    wave = coef[0][:, :, None] * jnp.cos(angle) - coef[1][:, :, None] * jnp.sin(angle)
    first = (lags == 0).astype(F32)
    return jnp.where(inside, jnp.sum(decay * wave, axis=1) + skip[:, None] * first, 0.0)


def shards(
    tokens, segments, ln1_gain, ln1_bias, w_query, w_key, w_value, shift_taps, ssm_rate, ssm_freq,
    ssm_coef, ssm_skip, w_out, ln2_gain, ln2_bias, w_up, w_down, cotangent,
):
    seqs, rows, width = tokens.shape
    fsdp = lax.axis_size("fsdp")
    dp = lax.axis_size("dp")
    run = HOPS
    place = lax.axis_index("fsdp")
    me = lax.axis_index("dp")
    chunk, inner = me // run, me % run
    group_count = run // seqs
    share = width // group_count
    seq, group = inner // group_count, inner % group_count
    span = run * rows
    multi = dp > run
    groups = [list(range(base, base + run)) for base in range(0, dp, run)] if multi else None
    reach = HOPS * rows + rows
    assert dp % run == 0 and rows == TILE and fsdp == 4 and group_count == fsdp
    blocks = (run, share, rows)

    def exchange(value):
        return lax.all_to_all(value, "dp", 0, 0, axis_index_groups=groups)

    def from_prev(value):
        if not multi:
            return jnp.zeros_like(value)
        return lax.ppermute(value, "dp", [(src, src + run) for src in range(dp - run)])

    def from_next(value):
        return lax.ppermute(value, "dp", [(src + run, src) for src in range(dp - run)])

    small_parts = (ln1_gain, ln1_bias, shift_taps, ssm_rate, ssm_freq, ssm_coef, ssm_skip, ln2_gain, ln2_bias)
    flat = jnp.concatenate([part.reshape(-1) for part in small_parts])
    padded = -(-flat.shape[0] // 1024) * 1024
    flat = jnp.pad(flat, (0, padded - flat.shape[0])).reshape(padded // 128, 128)
    in_order = jnp.stack(gather_pieces(flat)).reshape(fsdp, padded)
    small = in_order[jnp.arange(fsdp) ^ place]
    pieces, at = [], 0
    for part in small_parts:
        pieces.append(small[:, at : at + part.size])
        at += part.size
    gain_one, bias_one, gain_two, bias_two = (
        pieces[index].reshape(1, width).astype(F32) for index in (0, 1, 7, 8)
    )

    def mine(piece, shape):
        return lax.dynamic_index_in_dim(piece, group, 0, keepdims=False).reshape(shape).astype(F32)

    taps = mine(pieces[2], shift_taps.shape)
    rate = mine(pieces[3], ssm_rate.shape)
    freq = mine(pieces[4], ssm_freq.shape)
    coef = mine(pieces[5], ssm_coef.shape)
    skip = mine(pieces[6], ssm_skip.shape)
    key_w = gather_pieces(w_key)
    gain_one, bias_one, key_w = lax.optimization_barrier((gain_one, bias_one, key_w))
    w_query, w_value, _ = lax.optimization_barrier((w_query, w_value, key_w[3]))
    query_w = gather_pieces(w_query)
    value_w = gather_pieces(w_value)
    w_out, w_up, w_down, _ = lax.optimization_barrier((w_out, w_up, w_down, value_w[3]))
    out_w = gather_pieces(w_out)
    up_w = gather_pieces(w_up)
    down_w = gather_pieces(w_down)

    lags = jnp.arange(reach + TILE) - TILE
    kern, kern_pull = jax.vjp(lambda *leaves: kernel_rows(*leaves, lags, reach), rate, freq, coef, skip)
    kern = kern[:, None, :]

    seg_row = lax.dynamic_index_in_dim(segments, seq, 0, keepdims=False)
    seg_wide = jnp.concatenate(
        [jnp.full((span,), -1, jnp.int32), seg_row, jnp.full((HALO,), -2, jnp.int32)]
    )
    seg_full = lax.dynamic_slice_in_dim(seg_wide, chunk * span + span - HALO, span + 2 * HALO, 0)
    seg_q = seg_full[HALO : HALO + span]
    seg_k = lax.dynamic_slice_in_dim(seg_wide, chunk * span, 2 * span, 0) if multi else seg_q

    taps_tiles = jnp.pad(taps, ((0, 0), (0, -share % 128)))
    taps_tiles = taps_tiles.reshape(SHIFT, -1, 128).transpose(1, 0, 2)

    which = jnp.stack([place, inner]).astype(jnp.int32)
    x = tokens.reshape(seqs * rows, width)
    cot = cotangent.reshape(seqs * rows, width)
    act_one, k_mine = key_call(which, x, gain_one, bias_one, key_w, blocks)
    k_own = exchange(k_mine)
    qv_own = swap_parts(which, query_value_call(which, act_one, query_w, value_w, blocks), "collect_qv")
    k_halo = from_prev(k_own[-1, :, rows - HALO :].T)
    ks_own = shift_fwd(seg_full, k_own, k_halo, taps_tiles)
    if multi:
        ks_win = jnp.concatenate([from_prev(ks_own), ks_own], axis=0)
        v_own = qv_own[:, share:]
        v_win = jnp.concatenate([from_prev(v_own), v_own], axis=0)
    else:
        ks_win, v_win = ks_own, qv_own
    y_mine = exchange(mix_fwd(qv_own, ks_win, v_win, kern, seg_q, seg_k))
    resid, act_two, hidden, gz, gr, gy_mine, gln_two = middle_call(
        which, y_mine, x, gain_two, bias_two, cot, out_w, up_w, down_w
    )
    gy_own = exchange(gy_mine)
    order = Order()
    down_sum = Reduction(order, *down_grads_call(which, hidden, cot, fsdp))
    order.mark(down_sum.move)
    output, *up_parts = up_grads_call(which, y_mine, resid, order(act_two), hidden, gz, gr, down_w)
    up_sum = Reduction(order, *up_parts)
    order.mark(up_sum.move)

    down_sum.next()
    gy_own = order(gy_own)
    if multi:
        gq_own, gks_win, gv_win, gkern = mix_bwd(qv_own, ks_win, v_win, gy_own, kern, seg_q, seg_k)
        gks_own = gks_win[span:] + from_next(gks_win[:span].astype(BF)).astype(F32)
        gv_own = (gv_win[run:] + from_next(gv_win[:run].astype(BF)).astype(F32)).astype(BF)
        gqv_own = jnp.concatenate([gq_own, gv_own], axis=1)
        gks_halo = from_next(gks_own[:HALO].astype(BF)).astype(F32)
    else:
        gqv_own, gks_own, gkern = mix_bwd(qv_own, ks_win, v_win, gy_own, kern, seg_q, seg_k)
        gks_halo = jnp.zeros((HALO, share), F32)
    order.mark(gkern)
    gqv_mine = exchange(gqv_own)
    up_sum.next()
    down_sum.next()
    gks_own = order(gks_own)
    taps_grad, *gk_parts = shift_bwd(which, seg_full, k_own, k_halo, gks_own, gks_halo, taps_tiles)
    order.mark(taps_grad)
    down_sum.next()
    rate_grad, freq_grad, coef_grad, skip_grad = kern_pull(order(gkern)[:, 0, :])
    order.mark((rate_grad, freq_grad, coef_grad))
    up_sum.next()
    down_sum.next()
    *qv_parts, ga = qv_grads_call(which, order(gqv_mine), act_one, query_w, value_w)
    qv_sum = Reduction(order, *qv_parts)
    order.mark(qv_sum.move)
    up_sum.next()
    down_sum.next()
    qv_sum.next()
    gk_mine = swap_parts(which, gk_parts, "collect_gk")
    keep_c, send_c, input_grad, gln_one = last_call(
        which, order(gk_mine), act_one, ga, x, gr, gain_one, key_w
    )
    key_sum = Reduction(order, keep_c, send_c)
    order.mark(send_c)

    shard = width // fsdp
    wide = w_down.shape[0]

    common = jnp.concatenate(
        [line.reshape(fsdp, shard) for line in (gln_one[0], gln_one[1], gln_two[0], gln_two[1])], axis=1
    ).reshape(-1)
    by_group = jnp.concatenate(
        [grad.reshape(-1) for grad in (taps_grad, rate_grad, freq_grad, coef_grad, skip_grad)]
    )
    small_sum = SmallSum(order, common, by_group, (1, 2))
    for _ in range(8):
        for chain in (key_sum, small_sum, qv_sum, up_sum, down_sum):
            chain.next()
    key_grad, query_value, up_out, down_grad = (
        chain.result() for chain in (key_sum, qv_sum, up_sum, down_sum)
    )
    up_grad = up_out[:-shard]
    up_grad = up_grad.reshape(-1, shard, width).transpose(1, 0, 2).reshape(w_up.shape)
    out_grad = up_out[-shard:]
    query_grad, value_grad = query_value[:shard], query_value[shard:]
    common, by_group = small_sum.result(place)
    common = lax.dynamic_index_in_dim(common.reshape(fsdp, -1), place, 0, keepdims=False)
    owned = jnp.concatenate([common, by_group])
    shapes = [ln1_gain.shape, ln1_bias.shape, ln2_gain.shape, ln2_bias.shape, shift_taps.shape]
    shapes += [ssm_rate.shape, ssm_freq.shape, ssm_coef.shape, ssm_skip.shape]
    little, at = [], 0
    for shape in shapes:
        count = int(np.prod(shape))
        little.append(owned[at : at + count].reshape(shape))
        at += count
    return (
        output.reshape(seqs, rows, width),
        input_grad.reshape(seqs, rows, width),
        little[0],
        little[1],
        query_grad,
        key_grad,
        value_grad,
        little[4],
        little[5],
        little[6],
        little[7],
        little[8],
        out_grad,
        little[2],
        little[3],
        up_grad,
        down_grad,
    )


def solution(mesh):
    return jax.shard_map(
        shards,
        mesh=mesh,
        in_specs=(
            P("fsdp", "dp", None),
            P("fsdp", None),
            P("fsdp"),
            P("fsdp"),
            P("fsdp", None),
            P("fsdp", None),
            P("fsdp", None),
            P(None, "fsdp"),
            P("fsdp", None),
            P("fsdp", None),
            P(None, "fsdp", None),
            P("fsdp"),
            P("fsdp", None),
            P("fsdp"),
            P("fsdp"),
            P("fsdp", None),
            P("fsdp", None),
            P("fsdp", "dp", None),
        ),
        out_specs=(
            P("fsdp", "dp", None),
            P("fsdp", "dp", None),
            P("fsdp"),
            P("fsdp"),
            P("fsdp", None),
            P("fsdp", None),
            P("fsdp", None),
            P(None, "fsdp"),
            P("fsdp", None),
            P("fsdp", None),
            P(None, "fsdp", None),
            P("fsdp"),
            P("fsdp", None),
            P("fsdp"),
            P("fsdp"),
            P("fsdp", None),
            P("fsdp", None),
        ),
        check_vma=False,
    )
```

```python
import functools

import jax
import jax.numpy as jnp
import numpy as np
from jax import lax
from jax.experimental import pallas as pl
from jax.experimental.pallas import tpu as pltpu
from jax.sharding import PartitionSpec as P

SHIFT = 64
HOPS = 8
TILE = 256
HALO = 64
EPS = 1e-05
BF = jnp.bfloat16
F32 = jnp.float32
VMEM_BYTES = 56 * 1024 * 1024


def vmem():
    return pl.BlockSpec(memory_space=pltpu.VMEM)


def smem():
    return pl.BlockSpec(memory_space=pltpu.SMEM)


def hbm():
    return pl.BlockSpec(memory_space=pl.ANY)


def params():
    return pltpu.CompilerParams(vmem_limit_bytes=VMEM_BYTES)


SCALE = 1000


def cost(micros, moved):
    return pl.CostEstimate(
        flops=int(micros * 1.0e9) // SCALE, bytes_accessed=int(moved) // (8 * SCALE), transcendentals=0
    )


def mm(left, right):
    return lax.dot_general(left, right, (((1,), (0,)), ((), ())), preferred_element_type=F32)


def mm_nt(left, right):
    return lax.dot_general(left, right, (((1,), (1,)), ((), ())), preferred_element_type=F32)


def tn(left, right):
    return lax.dot_general(left, right, (((0,), (0,)), ((), ())), preferred_element_type=F32)


def cut_lanes(width, rows):
    tiles = [(base, 128, rows, False) for base in range(0, width - 127, 128)]
    if width % 128:
        assert width % 128 == 64
        tiles.append((width - 64, 64, rows // 2, True))
    return tiles


def fill_ext_t(ext, source, halo, width, lead):
    rows = source.shape[0] * TILE
    first = HALO if lead else 0
    for index, (base, size, span, packed) in enumerate(cut_lanes(width, rows)):
        halo_at = 0 if lead else span
        blocks = span // TILE
        sides = [(0, 0)] + ([(64, span)] if packed else [])
        for lane, token in sides:
            lanes = slice(lane, lane + size)
            for block in range(blocks):
                part = source[token // TILE + block, base : base + size, :].astype(F32).T
                ext[index, first + block * TILE : first + (block + 1) * TILE, lanes] = part
            if lead and token:
                part = source[token // TILE - 1, base : base + size, TILE - 128 :].astype(F32).T[128 - HALO :]
            else:
                part = halo[:, base : base + size].astype(F32)
            ext[index, halo_at : halo_at + HALO, lanes] = part


def fill_ext(ext, source, halo, width):
    rows = source.shape[0]
    for index, (base, size, span, packed) in enumerate(cut_lanes(width, rows)):
        features = slice(base, base + size)
        if packed:
            ext[index, 0 : span + HALO, 0:size] = source[0 : span + HALO, features]
            ext[index, 0:span, size : 2 * size] = source[span:rows, features]
            ext[index, span : span + HALO, size : 2 * size] = halo[:, features]
        else:
            ext[index, 0:span, :] = source[:, features]
            ext[index, span : span + HALO, :] = halo[:, features]


def fill_segments(seg_b, seg_p, column):
    total = column.shape[0]
    seg_b[...] = jnp.broadcast_to(column[...], seg_b.shape)
    if seg_p is not None:
        half = seg_p.shape[0]
        seg_p[:, 0:64] = seg_b[0:half, 0:64]
        seg_p[:, 64:128] = seg_b[total - half : total, 64:128]


def windows(source, index, start, way):
    for fine in range(8):
        if way < 0:
            window = source[index, pl.ds(start + HALO - 56 - fine, 120), :]
        else:
            window = source[index, pl.ds(start + fine, 120), :]
        for coarse in range(SHIFT // 8):
            at = 56 - 8 * coarse if way < 0 else 8 * coarse
            yield 8 * coarse + fine, window[at : at + 64]


def seg_windows(seg_b, start, way):
    for fine in range(8):
        if way < 0:
            window = seg_b[pl.ds(start + HALO - 56 - fine, 120), :]
        else:
            window = seg_b[pl.ds(start + HALO + fine, 120), :]
        for coarse in range(SHIFT // 8):
            at = 56 - 8 * coarse if way < 0 else 8 * coarse
            yield window[at : at + 64]


def filtered(source, index, start, taps_ref, seg, way, clear):
    def plain():
        total = jnp.zeros((64, 128), F32)
        for lag, part in windows(source, index, start, way):
            total = total + part * taps_ref[index, lag : lag + 1, :]
        return total

    def masked():
        total = jnp.zeros((64, 128), F32)
        now = seg[pl.ds(start + HALO, 64), :]
        pairs = zip(windows(source, index, start, way), seg_windows(seg, start, way))
        for (lag, part), there in pairs:
            total = total + jnp.where(there == now, part * taps_ref[index, lag : lag + 1, :], 0.0)
        return total

    return lax.cond(clear, plain, masked)


def all_same(seg_s, start, first, last, packed, span):
    same = seg_s[start + first] == seg_s[start + last]
    if packed:
        same = jnp.logical_and(same, seg_s[span + start + first] == seg_s[span + start + last])
    return same


def shift_fwd_kernel(seg_s, k_ref, halo_ref, taps_ref, segcol_ref, out_ref, ext, seg_b, seg_p):
    width = k_ref.shape[1]
    rows = k_ref.shape[0] * TILE
    fill_ext_t(ext, k_ref, halo_ref, width, True)
    fill_segments(seg_b, seg_p, segcol_ref)
    for index, (base, size, span, packed) in enumerate(cut_lanes(width, rows)):

        def body(tile, carry):
            start = pl.multiple_of(tile * 64, 64)
            clear = all_same(seg_s, start, 1, HALO + 63, packed, span)
            total = filtered(ext, index, start, taps_ref, seg_p if packed else seg_b, -1, clear)
            out_ref[pl.ds(start, 64), base : base + size] = total[:, 0:size].astype(BF)
            if packed:
                out_ref[pl.ds(start + span, 64), base : base + size] = total[:, size:].astype(BF)
            return carry

        lax.fori_loop(0, span // 64, body, 0)


def lane_taps(taps):
    tiles = []
    for base, size, _, packed in cut_lanes(taps.shape[1], 0):
        part = taps[:, base : base + size]
        tiles.append(jnp.concatenate([part, part], axis=1) if packed else part)
    return jnp.stack(tiles)


def shift_fwd(seg_full, k_own, k_halo, taps):
    count, width, _ = k_own.shape
    rows = count * TILE
    tiles = len(cut_lanes(width, rows))
    return pl.pallas_call(
        shift_fwd_kernel,
        out_shape=jax.ShapeDtypeStruct((rows, width), BF),
        in_specs=[smem(), vmem(), vmem(), vmem(), vmem()],
        out_specs=vmem(),
        scratch_shapes=[
            pltpu.VMEM((tiles, HALO + rows, 128), F32),
            pltpu.VMEM((2 * HALO + rows, 128), jnp.int32),
            pltpu.VMEM((2 * HALO + rows // 2, 128), jnp.int32),
        ],
        compiler_params=params(),
        cost_estimate=cost(10, 2 << 20),
        name="shift_fwd",
    )(seg_full, k_own, k_halo, taps, seg_full[:, None])


def shift_bwd_kernel(
    seg_s, k_ref, halo_ref, g_ref, ghalo_ref, taps_ref, segcol_ref, tg_ref, out_ref,
    ext, gext, seg_b, seg_p, acc, gk_rows,
):
    width = k_ref.shape[1]
    rows = k_ref.shape[0] * TILE
    fill_ext_t(ext, k_ref, halo_ref, width, True)
    fill_ext(gext, g_ref, ghalo_ref, width)
    fill_segments(seg_b, seg_p, segcol_ref)
    acc[...] = jnp.zeros_like(acc)

    def fold(part):
        total = part[0:8]
        for piece in range(1, 8):
            total = total + part[8 * piece : 8 * piece + 8]
        return total

    for index, (base, size, span, packed) in enumerate(cut_lanes(width, rows)):
        seg = seg_p if packed else seg_b

        def body(tile, carry):
            start = pl.multiple_of(tile * 64, 64)
            clear = all_same(seg_s, start, HALO, HALO + 126, packed, span)
            gk_rows[index, pl.ds(start, 64), :] = filtered(gext, index, start, taps_ref, seg, 1, clear)
            grad = gext[index, pl.ds(start, 64), :]
            clear = all_same(seg_s, start, 1, HALO + 63, packed, span)

            @pl.when(clear)
            def _():
                for lag, part in windows(ext, index, start, -1):
                    acc[index, lag] += fold(part * grad)

            @pl.when(jnp.logical_not(clear))
            def _():
                now = seg[pl.ds(start + HALO, 64), :]
                pairs = zip(windows(ext, index, start, -1), seg_windows(seg, start, -1))
                for (lag, part), there in pairs:
                    acc[index, lag] += fold(jnp.where(there == now, part * grad, 0.0))

            return carry

        lax.fori_loop(0, span // 64, body, 0)
        line = jnp.sum(acc[index], axis=1)
        if packed:
            line = line[:, 0:size] + line[:, size:]
        tg_ref[:, base : base + size] = line
        blocks = span // TILE
        for block in range(rows // TILE):
            at = (block % blocks) * TILE
            part = gk_rows[index, at : at + TILE, :].T
            lane = (block // blocks) * size
            out_ref[block, base : base + size, :] = part[lane : lane + size].astype(BF)


def shift_bwd(seg_full, k_own, k_halo, grad, grad_halo, taps):
    count, width, _ = k_own.shape
    rows = count * TILE
    tiles = len(cut_lanes(width, rows))
    return pl.pallas_call(
        shift_bwd_kernel,
        out_shape=(
            jax.ShapeDtypeStruct((SHIFT, width), F32),
            jax.ShapeDtypeStruct(k_own.shape, BF),
        ),
        in_specs=[smem()] + [vmem()] * 6,
        out_specs=(vmem(),) * 2,
        scratch_shapes=[
            pltpu.VMEM((tiles, HALO + rows, 128), F32),
            pltpu.VMEM((tiles, HALO + rows, 128), F32),
            pltpu.VMEM((2 * HALO + rows, 128), jnp.int32),
            pltpu.VMEM((2 * HALO + rows // 2, 128), jnp.int32),
            pltpu.VMEM((tiles, SHIFT, 8, 128), F32),
            pltpu.VMEM((tiles, rows, 128), F32),
        ],
        compiler_params=params(),
        cost_estimate=cost(20, 4 << 20),
        name="shift_bwd",
    )(seg_full, k_own, k_halo, grad, grad_halo, taps, seg_full[:, None])


def build_bands(bands, row):
    length = row.shape[1]
    skewed = pltpu.roll(jnp.broadcast_to(row, (8, length)), 0, 1, stride=1, stride_axis=0)
    for step in range(16):
        bands[step] = pltpu.roll(skewed, 8 * step, 1) if step else skewed


def band_parts(distance, first, count):
    parts = []
    for row in range(first, first + count, 128):
        high = min(128, first + count - row)
        lane = TILE * (1 + distance) - (row // 128) * 128
        parts.append((slice((row % 128) // 8, (row % 128 + high) // 8), slice(lane, lane + TILE), high))
    return parts


def read_band(bands, parts):
    pieces = [bands[steps, :, lanes].reshape(high, TILE) for steps, lanes, high in parts]
    return pieces[0] if len(pieces) == 1 else jnp.concatenate(pieces, axis=0)


def alike(seg_b, rows, seg_line):
    now = seg_b[rows, :]
    return jnp.concatenate([now, now], axis=1) == seg_line


def head_rows(dest, source, heads, size):
    for head in range(heads):
        dest[head] = source[:, head * size : (head + 1) * size]


def head_turn(dest, source, heads, size, base=0):
    for head in range(heads):
        for block in range(source.shape[0]):
            part = source[block, base + head * size : base + (head + 1) * size, :].astype(F32)
            dest[head, block * TILE : (block + 1) * TILE, :] = part.T.astype(dest.dtype)


STRIP = 64


def mix_fwd_kernel(v_base, q_ref, k_ref, v_ref, row_ref, segq_ref, segk_ref, y_ref, kh, bands, seg_b):
    heads = row_ref.shape[0]
    size = k_ref.shape[1] // heads
    query_blocks, key_blocks = q_ref.shape[0], v_ref.shape[0]
    offset = key_blocks - query_blocks
    head_rows(kh, k_ref, heads, size)
    seg_b[...] = jnp.broadcast_to(segk_ref[...], seg_b.shape)

    def head_body(head, carry):
        build_bands(bands, row_ref[head])
        own = pl.ds(pl.multiple_of(head * size, size), size)
        own_v = pl.ds(pl.multiple_of(v_base + head * size, size), size)
        for row in range(query_blocks):
            query = q_ref[row, own, :]
            total = jnp.zeros((size, TILE), F32)
            for col in range(max(0, row + offset - HOPS), row + offset + 1):
                for first in range(0, TILE, STRIP):
                    kern = read_band(bands, band_parts(row + offset - col, first, STRIP))
                    rows = slice(col * TILE + first, col * TILE + first + STRIP)
                    weight = mm(kh[head, rows, :], query) * kern
                    weight = jnp.where(alike(seg_b, rows, segq_ref[row]), weight, 0.0).astype(BF)
                    total = total + mm(v_ref[col, own_v, first : first + STRIP], weight)
            y_ref[row, own, :] = total.astype(BF)
        return carry

    lax.fori_loop(0, heads, head_body, 0)


def mix_fwd(q, k_win, v_win, kern_asc, seg_q, seg_k):
    blocks = q.shape[0]
    wide, width = k_win.shape
    shape = (blocks, width, TILE)
    heads, _, length = kern_asc.shape
    size = width // heads
    return pl.pallas_call(
        functools.partial(mix_fwd_kernel, v_win.shape[1] - width),
        out_shape=jax.ShapeDtypeStruct(shape, BF),
        in_specs=[vmem()] * 6,
        out_specs=vmem(),
        scratch_shapes=[
            pltpu.VMEM((heads, wide, size), BF),
            pltpu.VMEM((16, 8, length), F32),
            pltpu.VMEM((wide, 128), jnp.int32),
        ],
        compiler_params=params(),
        cost_estimate=cost(20, 4 << 20),
        name="mix_fwd",
    )(q, k_win, v_win, kern_asc, seg_q.reshape(blocks, 1, TILE), seg_k[:, None])


def mix_bwd_kernel(
    v_base, q_ref, k_ref, v_ref, g_ref, row_ref, segq_ref, segk_ref, gq_ref, gk_ref, gv_ref, gkern_ref,
    qh, kh, vh, gh, kt, gqt, gkacc, gvacc, bands, gbands, seg_b,
):
    heads, length = row_ref.shape[0], row_ref.shape[2]
    size = k_ref.shape[1] // heads
    query_blocks, key_blocks = q_ref.shape[0], v_ref.shape[0]
    offset = key_blocks - query_blocks
    head_turn(qh, q_ref, heads, size)
    head_rows(kh, k_ref, heads, size)
    head_turn(vh, v_ref, heads, size, v_base)
    head_turn(gh, g_ref, heads, size)
    for head in range(heads):
        for block in range(key_blocks):
            part = kh[head, block * TILE : (block + 1) * TILE, :].astype(F32)
            kt[block, head * size : (head + 1) * size, :] = part.T.astype(BF)
    seg_b[...] = jnp.broadcast_to(segk_ref[...], seg_b.shape)
    gqt[...] = jnp.zeros_like(gqt)

    def head_body(head, carry):
        build_bands(bands, row_ref[head])
        gbands[...] = jnp.zeros_like(gbands)
        own = pl.ds(pl.multiple_of(head * size, size), size)
        for col in range(key_blocks):
            rows = slice(col * TILE, (col + 1) * TILE)
            gk = jnp.zeros((TILE, size), F32)
            gv = jnp.zeros((TILE, size), F32)
            for row in range(max(0, col - offset), min(query_blocks, col - offset + HOPS + 1)):
                parts = band_parts(row + offset - col, 0, TILE)
                kern = read_band(bands, parts)
                score = mm(kh[head, rows, :], q_ref[row, own, :])
                grad = mm(vh[head, rows, :], g_ref[row, own, :])
                live = alike(seg_b, rows, segq_ref[row])
                grad = jnp.where(live, grad, 0.0)
                weight = jnp.where(live, score * kern, 0.0).astype(BF)
                gscore = (grad * kern).astype(BF)
                both = grad * score
                at = 0
                for steps, lanes, high in parts:
                    gbands[steps, :, lanes] += both[at : at + high].reshape(high // 8, 8, TILE)
                    at += high
                queries = slice(row * TILE, (row + 1) * TILE)
                gk = gk + mm(gscore, qh[head, queries, :])
                gv = gv + mm(weight, gh[head, queries, :])
                gqt[row, own, :] += mm(kt[col, own, :], gscore)
            gkacc[head, rows, :] = gk
            gvacc[head, rows, :] = gv
        total = gbands[0]
        for step in range(1, 16):
            total = total + pltpu.roll(gbands[step], length - 8 * step, 1)
        line = total[0:1]
        for sub in range(1, 8):
            line = line + pltpu.roll(total, length - sub, 1)[sub : sub + 1]
        gkern_ref[head] = line
        return carry

    lax.fori_loop(0, heads, head_body, 0)
    gq_ref[:, 0 : heads * size, :] = gqt[...].astype(BF)
    for head in range(heads):
        gk_ref[:, head * size : (head + 1) * size] = gkacc[head]
        for block in range(key_blocks):
            part = gvacc[head, block * TILE : (block + 1) * TILE, :].T
            gv_ref[block, v_base + head * size : v_base + (head + 1) * size, :] = part.astype(gv_ref.dtype)


def mix_bwd_merged(v_base, *refs):
    mix_bwd_kernel(v_base, *refs[:7], refs[7], refs[8], refs[7], *refs[9:])


def mix_bwd(q, k_win, v_win, grad, kern_asc, seg_q, seg_k):
    blocks = q.shape[0]
    wide, width = k_win.shape
    heads, _, length = kern_asc.shape
    size = width // heads
    rows = blocks * TILE
    shape = (blocks, width, TILE)
    v_base = v_win.shape[1] - width
    outs = [
        jax.ShapeDtypeStruct((blocks, v_win.shape[1], TILE), BF),
        jax.ShapeDtypeStruct((wide, width), F32),
        jax.ShapeDtypeStruct((heads, 1, length), F32),
    ]
    if not v_base:
        outs.insert(2, jax.ShapeDtypeStruct(v_win.shape, F32))
    return pl.pallas_call(
        functools.partial(mix_bwd_merged if v_base else mix_bwd_kernel, v_base),
        out_shape=tuple(outs),
        in_specs=[vmem()] * 7,
        out_specs=(vmem(),) * len(outs),
        scratch_shapes=[
            pltpu.VMEM((heads, rows, size), BF),
            pltpu.VMEM((heads, wide, size), BF),
            pltpu.VMEM((heads, wide, size), BF),
            pltpu.VMEM((heads, rows, size), BF),
            pltpu.VMEM((wide // TILE, width, TILE), BF),
            pltpu.VMEM(shape, F32),
            pltpu.VMEM((heads, wide, size), F32),
            pltpu.VMEM((heads, wide, size), F32),
            pltpu.VMEM((16, 8, length), F32),
            pltpu.VMEM((16, 8, length), F32),
            pltpu.VMEM((wide, 128), jnp.int32),
        ],
        compiler_params=params(),
        cost_estimate=cost(40, 8 << 20),
        name="mix_bwd",
    )(q, k_win, v_win, grad, kern_asc, seg_q.reshape(blocks, 1, TILE), seg_k[:, None])


def load_pieces(me, pieces, full, sem, base):
    rows = pieces[0].shape[0]
    copies = []
    for mask, piece in enumerate(pieces):
        place = pl.ds(pl.multiple_of((me ^ mask) * rows, 64), rows)
        copies.append(pltpu.make_async_copy(piece, full.at[place], sem.at[base + mask]))
    for copy in copies:
        copy.start()

    def wait():
        for copy in copies:
            copy.wait()

    return wait


def normal_stats(value):
    center = value - jnp.mean(value, axis=-1, keepdims=True)
    scale = lax.rsqrt(jnp.mean(center * center, axis=-1, keepdims=True) + EPS)
    return center * scale, scale


def normal_grad(grad, hat, scale, gain):
    lead = grad * gain
    first = jnp.mean(lead, axis=-1, keepdims=True)
    second = jnp.mean(lead * hat, axis=-1, keepdims=True)
    return scale * (lead - first - hat * second)


def to_blocks(dest, turned, seqs, groups, base=0):
    share = turned.shape[0] // groups
    for seq in range(seqs):
        for group in range(groups):
            dest[seq * groups + group, base : base + share, :] = turned[
                group * share : (group + 1) * share, seq * TILE : (seq + 1) * TILE
            ]


def from_blocks(dest, blocks, seqs, groups, base=0):
    share = dest.shape[1] // groups
    for seq in range(seqs):
        whole = jnp.concatenate(
            [blocks[seq * groups + group, base : base + share, :] for group in range(groups)], axis=0
        )
        dest[seq * TILE : (seq + 1) * TILE, :] = whole.astype(F32).T.astype(BF)


def turn(value):
    return value.astype(F32).T.astype(BF)


def key_kernel(me_ref, x_ref, n0, n1, n2, n3, w0, w1, w2, w3, act_ref, out_ref, norm_ref, full, sem):
    wait = load_pieces(me_ref[0], (w0, w1, w2, w3), full, sem, 0)
    width = full.shape[0]
    groups = width // out_ref.shape[1]
    seqs = x_ref.shape[0] // TILE
    share = n0.shape[1]
    for owner in range(width // share):
        mask = me_ref[0] ^ owner
        low = jnp.where(mask == 0, n0[...].astype(F32), n1[...].astype(F32))
        high = jnp.where(mask == 2, n2[...].astype(F32), n3[...].astype(F32))
        norm_ref[:, owner * share : (owner + 1) * share] = jnp.where(mask < 2, low, high)
    hat, _ = normal_stats(x_ref[...].astype(F32))
    act_ref[...] = (hat * norm_ref[0:1, :] + norm_ref[1:2, :]).astype(BF)
    wait()
    to_blocks(out_ref, mm(act_ref[...], full[...]).T.astype(BF), seqs, groups)


def key_call(me, x, norms, pieces, blocks):
    tokens, width = x.shape
    return pl.pallas_call(
        key_kernel,
        out_shape=(
            jax.ShapeDtypeStruct((tokens, width), BF),
            jax.ShapeDtypeStruct(blocks, BF),
            jax.ShapeDtypeStruct((2, width), F32),
        ),
        in_specs=[smem()] + [vmem()] * 5 + [hbm()] * 4,
        out_specs=(vmem(),) * 3,
        scratch_shapes=[pltpu.VMEM((width, width), BF), pltpu.SemaphoreType.DMA((4,))],
        compiler_params=params(),
        cost_estimate=cost(0.1, 1 << 16),
        name="key_call",
    )(me, x, *norms, *pieces)


def query_value_kernel(me_ref, act_ref, q0, q1, q2, q3, v0, v1, v2, v3, *rest):
    outs, (qfull, vfull, turned, sem) = rest[:-4], rest[-4:]
    wait_q = load_pieces(me_ref[0], (q0, q1, q2, q3), qfull, sem, 0)
    wait_v = load_pieces(me_ref[0], (v0, v1, v2, v3), vfull, sem, 4)
    share = outs[0].shape[0] // 2
    wait_q()
    turned[0] = mm(act_ref[...], qfull[...]).T.astype(BF)
    wait_v()
    turned[1] = mm(act_ref[...], vfull[...]).T.astype(BF)
    groups = qfull.shape[0] // share
    for mask, out in enumerate(outs):
        there = me_ref[1] ^ mask
        features = pl.ds(pl.multiple_of(lax.rem(there, groups) * share, 64), share)
        tokens = pl.ds(pl.multiple_of(lax.div(there, groups) * TILE, TILE), TILE)
        out[0:share, :] = turned[0, features, tokens]
        out[share : 2 * share, :] = turned[1, features, tokens]


def query_value_call(me, act, q_pieces, v_pieces, blocks):
    width = act.shape[1]
    return pl.pallas_call(
        query_value_kernel,
        out_shape=(jax.ShapeDtypeStruct((2 * blocks[1], blocks[2]), BF),) * blocks[0],
        in_specs=[smem(), vmem()] + [hbm()] * 8,
        out_specs=(vmem(),) * blocks[0],
        scratch_shapes=[
            pltpu.VMEM((width, width), BF),
            pltpu.VMEM((width, width), BF),
            pltpu.VMEM((2, width, act.shape[0]), BF),
            pltpu.SemaphoreType.DMA((8,)),
        ],
        compiler_params=params(),
        cost_estimate=cost(0.1, 1 << 16),
        name="query_value_call",
    )(me, act, *q_pieces, *v_pieces)


GELU_A = 0.7978845608028654
GELU_B = 0.044715


def middle_kernel(
    me_ref, y_ref, x_ref, gain_ref, bias_ref, cot_ref, o0, o1, o2, o3, u0, u1, u2, u3, d0, d1, d2, d3,
    resid_ref, act_ref, hidden_ref, gz_ref, gr_ref, gy_ref, gln_ref,
    ofull, ufull, dfull, mixed, hat, gb, sem,
):
    me = me_ref[0]
    wait_o = load_pieces(me, (o0, o1, o2, o3), ofull, sem, 0)
    wait_u = load_pieces(me, (u0, u1, u2, u3), ufull, sem, 4)
    wait_d = load_pieces(me, (d0, d1, d2, d3), dfull, sem, 8)
    tokens, width = x_ref.shape
    groups = width // y_ref.shape[1]
    seqs = tokens // TILE
    chunk = width
    chunks = ufull.shape[1] // chunk
    from_blocks(mixed, y_ref, seqs, groups)
    wait_o()
    resid_ref[...] = x_ref[...].astype(F32) + mm(mixed[...], ofull[...])
    normed, scale = normal_stats(resid_ref[...])
    hat[...] = normed
    act_ref[...] = (normed * gain_ref[...] + bias_ref[...]).astype(BF)
    gb[...] = jnp.zeros_like(gb)
    wait_u()
    wait_d()

    def body(step, carry):
        rows = pl.ds(pl.multiple_of(lax.rem(step, seqs) * TILE, TILE), TILE)
        cols = pl.ds(pl.multiple_of(lax.div(step, seqs) * chunk, chunk), chunk)
        z = mm(act_ref[rows, :], ufull[:, cols])
        dh = mm_nt(cot_ref[rows, :], dfull[cols, :])
        square = z * z
        t = jnp.tanh(GELU_A * z * (1.0 + GELU_B * square))
        half = 0.5 * (1.0 + t)
        hidden_ref[rows, cols] = (z * half).astype(BF)
        slope = half + 0.5 * z * (1.0 - t * t) * (GELU_A * (1.0 + 3.0 * GELU_B * square))
        gz = (slope * dh).astype(BF)
        gz_ref[rows, cols] = gz
        gb[rows, :] += mm_nt(gz, ufull[:, cols])
        return carry

    lax.fori_loop(0, seqs * chunks, body, 0)
    gln_ref[0:1, :] = jnp.sum(gb[...] * hat[...], axis=0, keepdims=True)
    gln_ref[1:2, :] = jnp.sum(gb[...], axis=0, keepdims=True)
    gr_ref[...] = cot_ref[...].astype(F32) + normal_grad(gb[...], hat[...], scale, gain_ref[...])
    to_blocks(gy_ref, mm_nt(ofull[...], gr_ref[...].astype(BF)).astype(BF), seqs, groups)


def middle_call(me, y, x, gain, bias, cot, o_pieces, u_pieces, d_pieces):
    tokens, width = x.shape
    hidden = u_pieces[0].shape[1]
    return pl.pallas_call(
        middle_kernel,
        out_shape=(
            jax.ShapeDtypeStruct((tokens, width), F32),
            jax.ShapeDtypeStruct((tokens, width), BF),
            jax.ShapeDtypeStruct((tokens, hidden), BF),
            jax.ShapeDtypeStruct((tokens, hidden), BF),
            jax.ShapeDtypeStruct((tokens, width), F32),
            jax.ShapeDtypeStruct(y.shape, BF),
            jax.ShapeDtypeStruct((2, width), F32),
        ),
        in_specs=[smem()] + [vmem()] * 5 + [hbm()] * 12,
        out_specs=(vmem(),) * 7,
        scratch_shapes=[
            pltpu.VMEM((width, width), BF),
            pltpu.VMEM((width, hidden), BF),
            pltpu.VMEM((hidden, width), BF),
            pltpu.VMEM((tokens, width), BF),
            pltpu.VMEM((tokens, width), F32),
            pltpu.VMEM((tokens, width), F32),
            pltpu.SemaphoreType.DMA((12,)),
        ],
        compiler_params=params(),
        cost_estimate=cost(15, 24 << 20),
        name="middle_call",
    )(me, y, x, gain, bias, cot, *o_pieces, *u_pieces, *d_pieces)


def down_grads_kernel(me_ref, hidden_ref, cot_ref, keep_ref, send_ref):
    me = me_ref[0]
    wide = keep_ref.shape[1]
    for slot in range(2):
        for dest, mask in ((keep_ref, 2 * slot), (send_ref, 2 * slot + 1)):
            part = hidden_ref[:, pl.ds(pl.multiple_of((me ^ mask) * wide, wide), wide)]
            dest[slot] = mm(turn(part), cot_ref[...]).astype(dest.dtype)


def down_grads_call(me, hidden, cot, shards_count):
    width = cot.shape[1]
    wide = hidden.shape[1] // shards_count
    return pl.pallas_call(
        down_grads_kernel,
        out_shape=(
            jax.ShapeDtypeStruct((2, wide, width), BF),
            jax.ShapeDtypeStruct((2, wide, width), BF),
        ),
        in_specs=[smem()] + [vmem()] * 2,
        out_specs=(vmem(),) * 2,
        compiler_params=params(),
        cost_estimate=cost(6, 16 << 20),
        name="down_grads_call",
    )(me, hidden, cot)


def up_grads_kernel(
    me_ref, y_ref, resid_ref, act_ref, hidden_ref, gz_ref, gr_ref, d0, d1, d2, d3,
    out_ref, keep_ref, send_ref, dfull, act_t, low, sem,
):
    me = me_ref[0]
    wait_d = load_pieces(me, (d0, d1, d2, d3), dfull, sem, 0)
    tokens, width = resid_ref.shape
    hidden = hidden_ref.shape[1]
    groups = width // y_ref.shape[1]
    share = width // groups
    seqs = tokens // TILE
    act_t[...] = turn(act_ref[...])
    low[...] = gr_ref[...].astype(BF)
    blocks = hidden // width
    for slot in range(2):
        for dest, mask in ((keep_ref, 2 * slot), (send_ref, 2 * slot + 1)):
            owner = me ^ mask
            part = act_t[pl.ds(pl.multiple_of(owner * share, share), share), :]
            for block in range(blocks):
                value = mm(part, gz_ref[:, block * width : (block + 1) * width])
                dest[slot, block * share : (block + 1) * share, :] = value.astype(dest.dtype)
            value = mm(y_ref[owner], low[0:TILE, :])
            for seq in range(1, seqs):
                value = value + mm(y_ref[seq * groups + owner], low[seq * TILE : (seq + 1) * TILE, :])
            dest[slot, blocks * share : (blocks + 1) * share, :] = value.astype(dest.dtype)
    wait_d()
    out_ref[...] = (resid_ref[...] + mm(hidden_ref[...], dfull[...])).astype(BF)


def up_grads_call(me, y, resid, act, hidden, gz, gr, d_pieces):
    tokens, width = resid.shape
    wide = hidden.shape[1]
    groups = width // y.shape[1]
    rows = (wide // width + 1) * (width // groups)
    return pl.pallas_call(
        up_grads_kernel,
        out_shape=(
            jax.ShapeDtypeStruct((tokens, width), BF),
            jax.ShapeDtypeStruct((2, rows, width), BF),
            jax.ShapeDtypeStruct((2, rows, width), BF),
        ),
        in_specs=[smem()] + [vmem()] * 6 + [hbm()] * 4,
        out_specs=(vmem(),) * 3,
        scratch_shapes=[
            pltpu.VMEM((wide, width), BF),
            pltpu.VMEM((width, tokens), BF),
            pltpu.VMEM((tokens, width), BF),
            pltpu.SemaphoreType.DMA((4,)),
        ],
        compiler_params=params(),
        cost_estimate=cost(10, 24 << 20),
        name="up_grads_call",
    )(me, y, resid, act, hidden, gz, gr, *d_pieces)


def input_grads(me, act_t, grad, share, base, keep_ref, send_ref):
    for slot in range(2):
        for dest, mask in ((keep_ref, 2 * slot), (send_ref, 2 * slot + 1)):
            part = act_t[pl.ds(pl.multiple_of((me ^ mask) * share, share), share), :]
            dest[slot, base : base + share, :] = mm(part, grad).astype(dest.dtype)


def qv_grads_kernel(
    me_ref, gqv_ref, act_ref, q0, q1, q2, q3, v0, v1, v2, v3,
    keep_ref, send_ref, ga_ref, qfull, vfull, act_t, rows, sem,
):
    me = me_ref[0]
    wait_q = load_pieces(me, (q0, q1, q2, q3), qfull, sem, 0)
    wait_v = load_pieces(me, (v0, v1, v2, v3), vfull, sem, 4)
    tokens, width = act_ref.shape
    share = gqv_ref.shape[1] // 2
    groups = width // share
    seqs = tokens // TILE
    act_t[...] = turn(act_ref[...])
    from_blocks(rows, gqv_ref, seqs, groups)
    input_grads(me, act_t, rows[...], share, 0, keep_ref, send_ref)
    wait_q()
    ga_ref[...] = mm_nt(rows[...], qfull[...])
    from_blocks(rows, gqv_ref, seqs, groups, share)
    input_grads(me, act_t, rows[...], share, share, keep_ref, send_ref)
    wait_v()
    ga_ref[...] += mm_nt(rows[...], vfull[...])


def qv_grads_call(me, gqv, act, q_pieces, v_pieces):
    tokens, width = act.shape
    share = gqv.shape[1] // 2
    return pl.pallas_call(
        qv_grads_kernel,
        out_shape=(
            jax.ShapeDtypeStruct((2, 2 * share, width), BF),
            jax.ShapeDtypeStruct((2, 2 * share, width), BF),
            jax.ShapeDtypeStruct((tokens, width), F32),
        ),
        in_specs=[smem()] + [vmem()] * 2 + [hbm()] * 8,
        out_specs=(vmem(),) * 3,
        scratch_shapes=[
            pltpu.VMEM((width, width), BF),
            pltpu.VMEM((width, width), BF),
            pltpu.VMEM((width, tokens), BF),
            pltpu.VMEM((tokens, width), BF),
            pltpu.SemaphoreType.DMA((8,)),
        ],
        compiler_params=params(),
        cost_estimate=cost(8, 12 << 20),
        name="qv_grads_call",
    )(me, gqv, act, *q_pieces, *v_pieces)


def last_kernel(
    me_ref, gk_ref, act_ref, ga_ref, x_ref, gr_ref, norm_ref, extra_ref, k0, k1, k2, k3,
    keep_ref, send_ref, gx_ref, kfull, act_t, rows, sem,
):
    me = me_ref[0]
    wait_k = load_pieces(me, (k0, k1, k2, k3), kfull, sem, 0)
    tokens, width = act_ref.shape
    share = gk_ref.shape[1]
    act_t[...] = turn(act_ref[...])
    from_blocks(rows, gk_ref, tokens // TILE, width // share)
    input_grads(me, act_t, rows[...], share, 0, keep_ref, send_ref)
    wait_k()
    ga = ga_ref[...] + mm_nt(rows[...], kfull[...])
    hat, scale = normal_stats(x_ref[...].astype(F32))
    gain = jnp.sum(ga * hat, axis=0, keepdims=True)
    bias = jnp.sum(ga, axis=0, keepdims=True)
    lines = jnp.concatenate([gain, bias, jnp.zeros((6, width), F32)], axis=0).astype(BF)
    for slot in range(2):
        for dest, mask in ((keep_ref, 2 * slot), (send_ref, 2 * slot + 1)):
            dest[slot, share : share + 8, :] = lines
            dest[slot, share + 8 :, :] = extra_ref[mask]
    gx_ref[...] = (gr_ref[...] + normal_grad(ga, hat, scale, norm_ref[0:1, :])).astype(BF)


def last_call(me, gk, act, ga, x, gr, norm, extra, k_pieces):
    tokens, width = act.shape
    rows = gk.shape[1] + 8 + extra.shape[1]
    return pl.pallas_call(
        last_kernel,
        out_shape=(
            jax.ShapeDtypeStruct((2, rows, width), BF),
            jax.ShapeDtypeStruct((2, rows, width), BF),
            jax.ShapeDtypeStruct((tokens, width), BF),
        ),
        in_specs=[smem()] + [vmem()] * 7 + [hbm()] * 4,
        out_specs=(vmem(),) * 3,
        scratch_shapes=[
            pltpu.VMEM((width, width), BF),
            pltpu.VMEM((width, tokens), BF),
            pltpu.VMEM((tokens, width), BF),
            pltpu.SemaphoreType.DMA((4,)),
        ],
        compiler_params=params(),
        cost_estimate=cost(6, 8 << 20),
        name="last_call",
    )(me, gk, act, ga, x, gr, norm, extra, *k_pieces)


def xor_permute(value, axis, mask):
    count = lax.axis_size(axis)
    return lax.ppermute(value, axis, [(source, source ^ mask) for source in range(count)])


def collect_kernel(me_ref, *refs):
    parts, out = refs[:-1], refs[-1]
    for mask, part in enumerate(parts):
        out[me_ref[1] ^ mask] = part[...]


def swap_parts(me, parts, label, order):
    came = [order(parts[0])] + [xor_permute(part, "dp", mask) for mask, part in enumerate(parts) if mask]
    shape = (len(parts),) + parts[0].shape
    return pl.pallas_call(
        collect_kernel,
        out_shape=jax.ShapeDtypeStruct(shape, BF),
        in_specs=[smem()] + [vmem()] * len(parts),
        out_specs=vmem(),
        compiler_params=params(),
        cost_estimate=cost(0.5, 2 << 20),
        name=label,
    )(me, *came)


def gather_pieces(shard):
    across = xor_permute(shard, "fsdp", 2)
    beside = xor_permute(shard, "fsdp", 1)
    both = xor_permute(across, "fsdp", 1)
    return (shard, beside, across, both)


class Order:
    def __init__(self):
        self.last = None

    def __call__(self, value):
        if self.last is None:
            return value
        return lax.optimization_barrier((value, self.last))[0]

    def mark(self, value):
        self.last = value
        return value


def join_halves(own, other, bit):
    first = jnp.where(bit == 0, own, other)
    second = jnp.where(bit == 0, other, own)
    return jnp.concatenate([first, second], axis=0)


DP_MASKS = (1, 2, 4)


class Reduction:
    def __init__(self, order, keep, send, direct=False, near_first=False):
        self.order = order
        self.keep = keep
        self.move = send
        self.me = lax.axis_index("dp")
        self.steps = [self.core]
        self.near_first = near_first and lax.axis_size("dp") == 8
        if direct or lax.axis_size("dp") != 8:
            self.cuts = []
            self.steps += [self.high, self.scatter_all, self.gather_all]
        else:
            self.cuts = list(DP_MASKS)
            scatters = [functools.partial(self.scatter, mask) for mask in DP_MASKS]
            self.steps += scatters[:1] + [self.high] + scatters[1:] if near_first else [self.high] + scatters
            self.steps += [functools.partial(self.gather, mask) for mask in DP_MASKS[::-1]]

    def next(self):
        if self.steps:
            self.steps.pop(0)()
            self.order.mark(self.move)

    def add(self, came):
        return (self.order(self.keep).astype(F32) + came.astype(F32)).astype(BF)

    def core(self):
        came = xor_permute(self.move, "fsdp", 1)
        total = self.add(came)
        if self.near_first:
            self.cut(total, 1)
        else:
            self.keep, self.move = total[0], total[1]

    def high(self):
        self.cut(self.add(xor_permute(self.move, "fsdp", 2)))

    def cut(self, total, axis=0):
        self.move = total
        if self.cuts:
            bit = (self.me // self.cuts.pop(0)) % 2
            rows = total.shape[axis] // 2
            halves = total.reshape(total.shape[:axis] + (2, rows) + total.shape[axis + 1 :])
            self.keep = lax.dynamic_index_in_dim(halves, bit, axis, keepdims=False)
            self.move = lax.dynamic_index_in_dim(halves, 1 - bit, axis, keepdims=False)

    def scatter(self, mask):
        total = self.add(xor_permute(self.move, "dp", mask))
        if total.ndim == 3:
            self.keep, self.move = total[0], total[1]
        else:
            self.cut(total)

    def gather(self, mask):
        other = xor_permute(self.move, "dp", mask)
        self.move = join_halves(self.order(self.move), other, (self.me // mask) % 2)

    def scatter_all(self):
        rows, cols = self.move.shape
        count = lax.axis_size("dp")
        parts = lax.all_to_all(self.move.reshape(count, rows // count, cols), "dp", 0, 0)
        self.move = jnp.sum(self.order(parts).astype(F32), axis=0).astype(BF)

    def gather_all(self):
        rows, cols = self.move.shape
        count = lax.axis_size("dp")
        spread = jnp.broadcast_to(self.move[None], (count, rows, cols))
        self.move = lax.all_to_all(spread, "dp", 0, 0).reshape(count * rows, cols)

    def result(self):
        while self.steps:
            self.next()
        return self.move.astype(F32)


def kernel_rows(rate, freq, coef, skip, lags, reach):
    lag = lags.astype(F32)
    inside = (lags >= 0) & (lags < reach)
    clipped = jnp.where(inside, lag, 0.0)
    decay = jnp.exp(-rate[:, :, None] * clipped)
    angle = freq[:, :, None] * clipped
    wave = coef[0][:, :, None] * jnp.cos(angle) - coef[1][:, :, None] * jnp.sin(angle)
    first = (lags == 0).astype(F32)
    return jnp.where(inside, jnp.sum(decay * wave, axis=1) + skip[:, None] * first, 0.0)


def shards(
    tokens, segments, ln1_gain, ln1_bias, w_query, w_key, w_value, shift_taps, ssm_rate, ssm_freq,
    ssm_coef, ssm_skip, w_out, ln2_gain, ln2_bias, w_up, w_down, cotangent,
):
    seqs, rows, width = tokens.shape
    fsdp = lax.axis_size("fsdp")
    dp = lax.axis_size("dp")
    run = HOPS
    place = lax.axis_index("fsdp")
    me = lax.axis_index("dp")
    chunk, inner = me // run, me % run
    group_count = run // seqs
    share = width // group_count
    seq, group = inner // group_count, inner % group_count
    span = run * rows
    multi = dp > run
    groups = [list(range(base, base + run)) for base in range(0, dp, run)] if multi else None
    reach = HOPS * rows + rows
    assert dp % run == 0 and rows == TILE and fsdp == 4 and group_count == fsdp
    blocks = (run, share, rows)

    def exchange(value):
        return lax.all_to_all(value, "dp", 0, 0, axis_index_groups=groups)

    def from_prev(value):
        if not multi:
            return jnp.zeros_like(value)
        return lax.ppermute(value, "dp", [(src, src + run) for src in range(dp - run)])

    def from_next(value):
        return lax.ppermute(value, "dp", [(src + run, src) for src in range(dp - run)])

    key_w = gather_pieces(w_key)
    norm_one = gather_pieces(jnp.stack([ln1_gain, ln1_bias]))
    w_query, w_value, w_out, _ = lax.optimization_barrier((w_query, w_value, w_out, key_w[2]))
    query_w = gather_pieces(w_query)
    value_w = gather_pieces(w_value)
    out_w = gather_pieces(w_out)
    w_up, w_down, _ = lax.optimization_barrier((w_up, w_down, value_w[2]))
    up_w = gather_pieces(w_up)
    down_w = gather_pieces(w_down)
    small_parts = (shift_taps, ssm_rate, ssm_freq, ssm_coef, ssm_skip, ln2_gain, ln2_bias)
    flat = jnp.concatenate([part.reshape(-1) for part in small_parts])
    padded = -(-flat.shape[0] // 1024) * 1024
    flat = jnp.pad(flat, (0, padded - flat.shape[0])).reshape(padded // 128, 128)
    flat, _ = lax.optimization_barrier((flat, key_w[2]))
    in_order = jnp.stack(gather_pieces(flat)).reshape(fsdp, padded)
    small = in_order[jnp.arange(fsdp) ^ place]
    pieces, at = [], 0
    for part in small_parts:
        pieces.append(small[:, at : at + part.size])
        at += part.size
    gain_two, bias_two = (pieces[index].reshape(1, width).astype(F32) for index in (5, 6))

    def mine(piece, shape):
        return lax.dynamic_index_in_dim(piece, group, 0, keepdims=False).reshape(shape).astype(F32)

    taps = mine(pieces[0], shift_taps.shape)
    rate = mine(pieces[1], ssm_rate.shape)
    freq = mine(pieces[2], ssm_freq.shape)
    coef = mine(pieces[3], ssm_coef.shape)
    skip = mine(pieces[4], ssm_skip.shape)

    lags = jnp.arange(reach + TILE) - TILE
    kern, kern_pull = jax.vjp(lambda *leaves: kernel_rows(*leaves, lags, reach), rate, freq, coef, skip)
    kern = kern[:, None, :]

    segments, _ = lax.optimization_barrier((segments, key_w[3]))
    seg_row = lax.dynamic_index_in_dim(segments, seq, 0, keepdims=False)
    seg_wide = jnp.concatenate(
        [jnp.full((span,), -1, jnp.int32), seg_row, jnp.full((HALO,), -2, jnp.int32)]
    )
    seg_full = lax.dynamic_slice_in_dim(seg_wide, chunk * span + span - HALO, span + 2 * HALO, 0)
    seg_q = seg_full[HALO : HALO + span]
    seg_k = lax.dynamic_slice_in_dim(seg_wide, chunk * span, 2 * span, 0) if multi else seg_q

    taps_tiles = lane_taps(taps)

    which = jnp.stack([place, inner]).astype(jnp.int32)
    x = tokens.reshape(seqs * rows, width)
    cot = cotangent.reshape(seqs * rows, width)
    act_one, k_mine, norm = key_call(which, x, norm_one, key_w, blocks)
    k_own = exchange(k_mine)
    qv_parts = query_value_call(which, act_one, query_w, value_w, blocks)
    k_halo = from_prev(k_own[-1, :, rows - HALO :].T)
    ks_own = shift_fwd(seg_full, k_own, k_halo, taps_tiles)
    forward = Order()
    forward.mark((ks_own, up_w[2], out_w[3]))
    qv_own = swap_parts(which, qv_parts, "collect_qv", forward)
    if multi:
        ks_win = jnp.concatenate([from_prev(ks_own), ks_own], axis=0)
        v_own = qv_own[:, share:]
        v_win = jnp.concatenate([from_prev(v_own), v_own], axis=0)
    else:
        ks_win, v_win = ks_own, qv_own
    y_own = mix_fwd(qv_own, ks_win, v_win, kern, seg_q, seg_k)
    forward.mark(down_w[2])
    y_mine = exchange(forward(y_own))
    resid, act_two, hidden, gz, gr, gy_mine, gln_two = middle_call(
        which, y_mine, x, gain_two, bias_two, cot, out_w, up_w, down_w
    )
    gy_own = exchange(gy_mine)
    order = Order()
    down_sum = Reduction(order, *down_grads_call(which, hidden, cot, fsdp), near_first=True)
    order.mark(down_sum.move)
    down_sum.next()
    output, *up_parts = up_grads_call(which, y_mine, resid, order(act_two), hidden, gz, gr, down_w)
    up_sum = Reduction(order, *up_parts)

    up_sum.move, gy_own = lax.optimization_barrier((up_sum.move, gy_own))
    up_sum.next()
    gy_own = order(gy_own)
    if multi:
        gq_own, gks_win, gv_win, gkern = mix_bwd(qv_own, ks_win, v_win, gy_own, kern, seg_q, seg_k)
        gks_own = gks_win[span:] + from_next(gks_win[:span].astype(BF)).astype(F32)
        gv_own = (gv_win[run:] + from_next(gv_win[:run].astype(BF)).astype(F32)).astype(BF)
        gqv_own = jnp.concatenate([gq_own, gv_own], axis=1)
        gks_halo = from_next(gks_own[:HALO].astype(BF)).astype(F32)
    else:
        gqv_own, gks_own, gkern = mix_bwd(qv_own, ks_win, v_win, gy_own, kern, seg_q, seg_k)
        gks_halo = jnp.zeros((HALO, share), F32)
    order.mark(gkern)
    gqv_mine = exchange(gqv_own)
    down_sum.next()
    up_sum.next()
    gks_own = order(gks_own)
    taps_grad, gk_own = shift_bwd(seg_full, k_own, k_halo, gks_own, gks_halo, taps_tiles)
    order.mark(taps_grad)
    down_sum.next()
    up_sum.next()
    rate_grad, freq_grad, coef_grad, skip_grad = kern_pull(order(gkern)[:, 0, :])

    ssm_line = jnp.concatenate([grad.reshape(-1) for grad in (rate_grad, freq_grad, coef_grad, skip_grad)])
    ssm_line = jnp.pad(ssm_line, (0, width - ssm_line.shape[0]))[None]
    by_group = jnp.concatenate([taps_grad.reshape(-1, width), ssm_line])
    slots = (jnp.arange(fsdp) ^ place) == group
    by_group = jnp.where(slots[:, None, None], by_group[None], 0.0)
    extra = jnp.concatenate([jnp.broadcast_to(gln_two, (fsdp, 2, width)), by_group], axis=1).astype(BF)
    extra = jnp.pad(extra, ((0, 0), (0, 56 - extra.shape[1]), (0, 0)))
    order.mark(extra)
    down_sum.next()
    gk_own, gqv_mine = lax.optimization_barrier((gk_own, order(gqv_mine)))
    gk_mine = exchange(gk_own)
    *qv_grads, ga = qv_grads_call(which, gqv_mine, act_one, query_w, value_w)
    qv_sum = Reduction(order, *qv_grads)
    order.mark(qv_sum.move)
    qv_sum.next()
    up_sum.next()
    keep_c, send_c, input_grad = last_call(which, order(gk_mine), act_one, ga, x, gr, norm, extra, key_w)
    key_sum = Reduction(order, keep_c, send_c, direct=True)
    order.mark(send_c)

    shard = width // fsdp
    chains = {"k": key_sum, "q": qv_sum, "u": up_sum, "d": down_sum}
    for name in "dkuqdkuqdukqduqkq":
        chains[name].next()
    key_rows, query_value, up_out, down_grad = (
        chain.result() for chain in (key_sum, qv_sum, up_sum, down_sum)
    )
    key_grad = key_rows[:shard]
    up_grad = up_out[:-shard]
    up_grad = up_grad.reshape(-1, shard, width).transpose(1, 0, 2).reshape(w_up.shape)
    out_grad = up_out[-shard:]
    query_grad, value_grad = query_value[:shard], query_value[shard:]
    norms = jnp.concatenate([key_rows[shard : shard + 2], key_rows[shard + 8 : shard + 10]])
    norms = lax.dynamic_slice_in_dim(norms, place * shard, shard, 1)
    owned = jnp.concatenate([norms.reshape(-1), key_rows[shard + 10 :].reshape(-1)])
    shapes = [ln1_gain.shape, ln1_bias.shape, ln2_gain.shape, ln2_bias.shape, shift_taps.shape]
    shapes += [ssm_rate.shape, ssm_freq.shape, ssm_coef.shape, ssm_skip.shape]
    little, at = [], 0
    for shape in shapes:
        count = int(np.prod(shape))
        little.append(owned[at : at + count].reshape(shape))
        at += count
    return (
        output.reshape(seqs, rows, width),
        input_grad.reshape(seqs, rows, width),
        little[0],
        little[1],
        query_grad,
        key_grad,
        value_grad,
        little[4],
        little[5],
        little[6],
        little[7],
        little[8],
        out_grad,
        little[2],
        little[3],
        up_grad,
        down_grad,
    )


def solution(mesh):
    return jax.shard_map(
        shards,
        mesh=mesh,
        in_specs=(
            P("fsdp", "dp", None),
            P("fsdp", None),
            P("fsdp"),
            P("fsdp"),
            P("fsdp", None),
            P("fsdp", None),
            P("fsdp", None),
            P(None, "fsdp"),
            P("fsdp", None),
            P("fsdp", None),
            P(None, "fsdp", None),
            P("fsdp"),
            P("fsdp", None),
            P("fsdp"),
            P("fsdp"),
            P("fsdp", None),
            P("fsdp", None),
            P("fsdp", "dp", None),
        ),
        out_specs=(
            P("fsdp", "dp", None),
            P("fsdp", "dp", None),
            P("fsdp"),
            P("fsdp"),
            P("fsdp", None),
            P("fsdp", None),
            P("fsdp", None),
            P(None, "fsdp"),
            P("fsdp", None),
            P("fsdp", None),
            P(None, "fsdp", None),
            P("fsdp"),
            P("fsdp", None),
            P("fsdp"),
            P("fsdp"),
            P("fsdp", None),
            P("fsdp", None),
        ),
        check_vma=False,
    )
```

```python
import functools

import jax
import jax.numpy as jnp
import numpy as np
from jax import lax
from jax.experimental import pallas as pl
from jax.experimental.pallas import tpu as pltpu
from jax.sharding import PartitionSpec as P

SHIFT = 64
HOPS = 8
TILE = 256
HALO = 64
EPS = 1e-05
BF = jnp.bfloat16
F32 = jnp.float32
VMEM_BYTES = 56 * 1024 * 1024


def vmem():
    return pl.BlockSpec(memory_space=pltpu.VMEM)


def smem():
    return pl.BlockSpec(memory_space=pltpu.SMEM)


def hbm():
    return pl.BlockSpec(memory_space=pl.ANY)


def params():
    return pltpu.CompilerParams(vmem_limit_bytes=VMEM_BYTES)


SCALE = 1


def cost(micros, moved):
    return pl.CostEstimate(
        flops=int(micros * 1.0e9) // SCALE, bytes_accessed=int(moved) // (8 * SCALE), transcendentals=0
    )


def mm(left, right):
    return lax.dot_general(left, right, (((1,), (0,)), ((), ())), preferred_element_type=F32)


def mm_nt(left, right):
    return lax.dot_general(left, right, (((1,), (1,)), ((), ())), preferred_element_type=F32)


def tn(left, right):
    return lax.dot_general(left, right, (((0,), (0,)), ((), ())), preferred_element_type=F32)


def cut_lanes(width, rows):
    tiles = [(base, 128, rows, False) for base in range(0, width - 127, 128)]
    if width % 128:
        assert width % 128 == 64
        tiles.append((width - 64, 64, rows // 2, True))
    return tiles


def fill_ext_t(ext, source, halo, width, lead):
    rows = source.shape[0] * TILE
    first = HALO if lead else 0
    for index, (base, size, span, packed) in enumerate(cut_lanes(width, rows)):
        halo_at = 0 if lead else span
        blocks = span // TILE
        sides = [(0, 0)] + ([(64, span)] if packed else [])
        for lane, token in sides:
            lanes = slice(lane, lane + size)
            for block in range(blocks):
                part = source[token // TILE + block, base : base + size, :].astype(F32).T
                ext[index, first + block * TILE : first + (block + 1) * TILE, lanes] = part
            if lead and token:
                part = source[token // TILE - 1, base : base + size, TILE - 128 :].astype(F32).T[128 - HALO :]
            else:
                part = halo[:, base : base + size].astype(F32)
            ext[index, halo_at : halo_at + HALO, lanes] = part


def fill_ext(ext, source, halo, width):
    rows = source.shape[0]
    for index, (base, size, span, packed) in enumerate(cut_lanes(width, rows)):
        features = slice(base, base + size)
        if packed:
            ext[index, 0 : span + HALO, 0:size] = source[0 : span + HALO, features]
            ext[index, 0:span, size : 2 * size] = source[span:rows, features]
            ext[index, span : span + HALO, size : 2 * size] = halo[:, features]
        else:
            ext[index, 0:span, :] = source[:, features]
            ext[index, span : span + HALO, :] = halo[:, features]


def fill_segments(seg_b, seg_p, column):
    total = column.shape[0]
    seg_b[...] = jnp.broadcast_to(column[...], seg_b.shape)
    if seg_p is not None:
        half = seg_p.shape[0]
        seg_p[:, 0:64] = seg_b[0:half, 0:64]
        seg_p[:, 64:128] = seg_b[total - half : total, 64:128]


def windows(source, index, start, way):
    for fine in range(8):
        if way < 0:
            window = source[index, pl.ds(start + HALO - 56 - fine, 120), :]
        else:
            window = source[index, pl.ds(start + fine, 120), :]
        for coarse in range(SHIFT // 8):
            at = 56 - 8 * coarse if way < 0 else 8 * coarse
            yield 8 * coarse + fine, window[at : at + 64]


def seg_windows(seg_b, start, way):
    for fine in range(8):
        if way < 0:
            window = seg_b[pl.ds(start + HALO - 56 - fine, 120), :]
        else:
            window = seg_b[pl.ds(start + HALO + fine, 120), :]
        for coarse in range(SHIFT // 8):
            at = 56 - 8 * coarse if way < 0 else 8 * coarse
            yield window[at : at + 64]


def filtered(source, index, start, taps_ref, seg, way, clear):
    def plain():
        total = jnp.zeros((64, 128), F32)
        for lag, part in windows(source, index, start, way):
            total = total + part * taps_ref[index, lag : lag + 1, :]
        return total

    def masked():
        total = jnp.zeros((64, 128), F32)
        now = seg[pl.ds(start + HALO, 64), :]
        pairs = zip(windows(source, index, start, way), seg_windows(seg, start, way))
        for (lag, part), there in pairs:
            total = total + jnp.where(there == now, part * taps_ref[index, lag : lag + 1, :], 0.0)
        return total

    return lax.cond(clear, plain, masked)


def all_same(seg_s, start, first, last, packed, span):
    same = seg_s[start + first] == seg_s[start + last]
    if packed:
        same = jnp.logical_and(same, seg_s[span + start + first] == seg_s[span + start + last])
    return same


def shift_fwd_kernel(seg_s, k_ref, halo_ref, taps_ref, segcol_ref, out_ref, ext, seg_b, seg_p):
    width = k_ref.shape[1]
    rows = k_ref.shape[0] * TILE
    fill_ext_t(ext, k_ref, halo_ref, width, True)
    fill_segments(seg_b, seg_p, segcol_ref)
    for index, (base, size, span, packed) in enumerate(cut_lanes(width, rows)):

        def body(tile, carry):
            start = pl.multiple_of(tile * 64, 64)
            clear = all_same(seg_s, start, 1, HALO + 63, packed, span)
            total = filtered(ext, index, start, taps_ref, seg_p if packed else seg_b, -1, clear)
            out_ref[pl.ds(start, 64), base : base + size] = total[:, 0:size].astype(BF)
            if packed:
                out_ref[pl.ds(start + span, 64), base : base + size] = total[:, size:].astype(BF)
            return carry

        lax.fori_loop(0, span // 64, body, 0)


def lane_taps(taps):
    tiles = []
    for base, size, _, packed in cut_lanes(taps.shape[1], 0):
        part = taps[:, base : base + size]
        tiles.append(jnp.concatenate([part, part], axis=1) if packed else part)
    return jnp.stack(tiles)


def shift_fwd(seg_full, k_own, k_halo, taps):
    count, width, _ = k_own.shape
    rows = count * TILE
    tiles = len(cut_lanes(width, rows))
    return pl.pallas_call(
        shift_fwd_kernel,
        out_shape=jax.ShapeDtypeStruct((rows, width), BF),
        in_specs=[smem(), vmem(), vmem(), vmem(), vmem()],
        out_specs=vmem(),
        scratch_shapes=[
            pltpu.VMEM((tiles, HALO + rows, 128), F32),
            pltpu.VMEM((2 * HALO + rows, 128), jnp.int32),
            pltpu.VMEM((2 * HALO + rows // 2, 128), jnp.int32),
        ],
        compiler_params=params(),
        cost_estimate=cost(10, 2 << 20),
        name="shift_fwd",
    )(seg_full, k_own, k_halo, taps, seg_full[:, None])


def shift_bwd_kernel(
    seg_s, k_ref, halo_ref, g_ref, ghalo_ref, taps_ref, segcol_ref, tg_ref, out_ref,
    ext, gext, seg_b, seg_p, acc, gk_rows,
):
    width = k_ref.shape[1]
    rows = k_ref.shape[0] * TILE
    fill_ext_t(ext, k_ref, halo_ref, width, True)
    fill_ext(gext, g_ref, ghalo_ref, width)
    fill_segments(seg_b, seg_p, segcol_ref)
    acc[...] = jnp.zeros_like(acc)

    def fold(part):
        total = part[0:8]
        for piece in range(1, 8):
            total = total + part[8 * piece : 8 * piece + 8]
        return total

    for index, (base, size, span, packed) in enumerate(cut_lanes(width, rows)):
        seg = seg_p if packed else seg_b

        def body(tile, carry):
            start = pl.multiple_of(tile * 64, 64)
            clear = all_same(seg_s, start, HALO, HALO + 126, packed, span)
            gk_rows[index, pl.ds(start, 64), :] = filtered(gext, index, start, taps_ref, seg, 1, clear)
            grad = gext[index, pl.ds(start, 64), :]
            clear = all_same(seg_s, start, 1, HALO + 63, packed, span)

            @pl.when(clear)
            def _():
                for lag, part in windows(ext, index, start, -1):
                    acc[index, lag] += fold(part * grad)

            @pl.when(jnp.logical_not(clear))
            def _():
                now = seg[pl.ds(start + HALO, 64), :]
                pairs = zip(windows(ext, index, start, -1), seg_windows(seg, start, -1))
                for (lag, part), there in pairs:
                    acc[index, lag] += fold(jnp.where(there == now, part * grad, 0.0))

            return carry

        lax.fori_loop(0, span // 64, body, 0)
        line = jnp.sum(acc[index], axis=1)
        if packed:
            line = line[:, 0:size] + line[:, size:]
        tg_ref[:, base : base + size] = line
        blocks = span // TILE
        for block in range(rows // TILE):
            at = (block % blocks) * TILE
            part = gk_rows[index, at : at + TILE, :].T
            lane = (block // blocks) * size
            out_ref[block, base : base + size, :] = part[lane : lane + size].astype(BF)


def shift_bwd(seg_full, k_own, k_halo, grad, grad_halo, taps):
    count, width, _ = k_own.shape
    rows = count * TILE
    tiles = len(cut_lanes(width, rows))
    return pl.pallas_call(
        shift_bwd_kernel,
        out_shape=(
            jax.ShapeDtypeStruct((SHIFT, width), F32),
            jax.ShapeDtypeStruct(k_own.shape, BF),
        ),
        in_specs=[smem()] + [vmem()] * 6,
        out_specs=(vmem(),) * 2,
        scratch_shapes=[
            pltpu.VMEM((tiles, HALO + rows, 128), F32),
            pltpu.VMEM((tiles, HALO + rows, 128), F32),
            pltpu.VMEM((2 * HALO + rows, 128), jnp.int32),
            pltpu.VMEM((2 * HALO + rows // 2, 128), jnp.int32),
            pltpu.VMEM((tiles, SHIFT, 8, 128), F32),
            pltpu.VMEM((tiles, rows, 128), F32),
        ],
        compiler_params=params(),
        cost_estimate=cost(20, 4 << 20),
        name="shift_bwd",
    )(seg_full, k_own, k_halo, grad, grad_halo, taps, seg_full[:, None])


def build_bands(bands, row):
    length = row.shape[1]
    skewed = pltpu.roll(jnp.broadcast_to(row, (8, length)), 0, 1, stride=1, stride_axis=0)
    for step in range(16):
        bands[step] = pltpu.roll(skewed, 8 * step, 1) if step else skewed


def band_parts(distance, first, count):
    parts = []
    for row in range(first, first + count, 128):
        high = min(128, first + count - row)
        lane = TILE * (1 + distance) - (row // 128) * 128
        parts.append((slice((row % 128) // 8, (row % 128 + high) // 8), slice(lane, lane + TILE), high))
    return parts


def read_band(bands, parts):
    pieces = [bands[steps, :, lanes].reshape(high, TILE) for steps, lanes, high in parts]
    return pieces[0] if len(pieces) == 1 else jnp.concatenate(pieces, axis=0)


def alike(seg_b, rows, seg_line):
    now = seg_b[rows, :]
    return jnp.concatenate([now, now], axis=1) == seg_line


def head_rows(dest, source, heads, size):
    for head in range(heads):
        dest[head] = source[:, head * size : (head + 1) * size]


def head_turn(dest, source, heads, size, base=0):
    for head in range(heads):
        for block in range(source.shape[0]):
            part = source[block, base + head * size : base + (head + 1) * size, :].astype(F32)
            dest[head, block * TILE : (block + 1) * TILE, :] = part.T.astype(dest.dtype)


STRIP = 64


def mix_fwd_kernel(v_base, q_ref, k_ref, v_ref, row_ref, segq_ref, segk_ref, y_ref, kh, bands, seg_b):
    heads = row_ref.shape[0]
    size = k_ref.shape[1] // heads
    query_blocks, key_blocks = q_ref.shape[0], v_ref.shape[0]
    offset = key_blocks - query_blocks
    head_rows(kh, k_ref, heads, size)
    seg_b[...] = jnp.broadcast_to(segk_ref[...], seg_b.shape)

    def head_body(head, carry):
        build_bands(bands, row_ref[head])
        own = pl.ds(pl.multiple_of(head * size, size), size)
        own_v = pl.ds(pl.multiple_of(v_base + head * size, size), size)
        for row in range(query_blocks):
            query = q_ref[row, own, :]
            total = jnp.zeros((size, TILE), F32)
            for col in range(max(0, row + offset - HOPS), row + offset + 1):
                for first in range(0, TILE, STRIP):
                    kern = read_band(bands, band_parts(row + offset - col, first, STRIP))
                    rows = slice(col * TILE + first, col * TILE + first + STRIP)
                    weight = mm(kh[head, rows, :], query) * kern
                    weight = jnp.where(alike(seg_b, rows, segq_ref[row]), weight, 0.0).astype(BF)
                    total = total + mm(v_ref[col, own_v, first : first + STRIP], weight)
            y_ref[row, own, :] = total.astype(BF)
        return carry

    lax.fori_loop(0, heads, head_body, 0)


def mix_fwd(q, k_win, v_win, kern_asc, seg_q, seg_k):
    blocks = q.shape[0]
    wide, width = k_win.shape
    shape = (blocks, width, TILE)
    heads, _, length = kern_asc.shape
    size = width // heads
    return pl.pallas_call(
        functools.partial(mix_fwd_kernel, v_win.shape[1] - width),
        out_shape=jax.ShapeDtypeStruct(shape, BF),
        in_specs=[vmem()] * 6,
        out_specs=vmem(),
        scratch_shapes=[
            pltpu.VMEM((heads, wide, size), BF),
            pltpu.VMEM((16, 8, length), F32),
            pltpu.VMEM((wide, 128), jnp.int32),
        ],
        compiler_params=params(),
        cost_estimate=cost(20, 4 << 20),
        name="mix_fwd",
    )(q, k_win, v_win, kern_asc, seg_q.reshape(blocks, 1, TILE), seg_k[:, None])


def mix_bwd_kernel(
    v_base, q_ref, k_ref, v_ref, g_ref, row_ref, segq_ref, segk_ref, gq_ref, gk_ref, gv_ref, gkern_ref,
    qh, kh, vh, gh, kt, gqt, gkacc, gvacc, bands, gbands, seg_b,
):
    heads, length = row_ref.shape[0], row_ref.shape[2]
    size = k_ref.shape[1] // heads
    query_blocks, key_blocks = q_ref.shape[0], v_ref.shape[0]
    offset = key_blocks - query_blocks
    head_turn(qh, q_ref, heads, size)
    head_rows(kh, k_ref, heads, size)
    head_turn(vh, v_ref, heads, size, v_base)
    head_turn(gh, g_ref, heads, size)
    for head in range(heads):
        for block in range(key_blocks):
            part = kh[head, block * TILE : (block + 1) * TILE, :].astype(F32)
            kt[block, head * size : (head + 1) * size, :] = part.T.astype(BF)
    seg_b[...] = jnp.broadcast_to(segk_ref[...], seg_b.shape)
    gqt[...] = jnp.zeros_like(gqt)

    def head_body(head, carry):
        build_bands(bands, row_ref[head])
        gbands[...] = jnp.zeros_like(gbands)
        own = pl.ds(pl.multiple_of(head * size, size), size)
        for col in range(key_blocks):
            rows = slice(col * TILE, (col + 1) * TILE)
            gk = jnp.zeros((TILE, size), F32)
            gv = jnp.zeros((TILE, size), F32)
            for row in range(max(0, col - offset), min(query_blocks, col - offset + HOPS + 1)):
                parts = band_parts(row + offset - col, 0, TILE)
                kern = read_band(bands, parts)
                score = mm(kh[head, rows, :], q_ref[row, own, :])
                grad = mm(vh[head, rows, :], g_ref[row, own, :])
                live = alike(seg_b, rows, segq_ref[row])
                grad = jnp.where(live, grad, 0.0)
                weight = jnp.where(live, score * kern, 0.0).astype(BF)
                gscore = (grad * kern).astype(BF)
                both = grad * score
                at = 0
                for steps, lanes, high in parts:
                    gbands[steps, :, lanes] += both[at : at + high].reshape(high // 8, 8, TILE)
                    at += high
                queries = slice(row * TILE, (row + 1) * TILE)
                gk = gk + mm(gscore, qh[head, queries, :])
                gv = gv + mm(weight, gh[head, queries, :])
                gqt[row, own, :] += mm(kt[col, own, :], gscore)
            gkacc[head, rows, :] = gk
            gvacc[head, rows, :] = gv
        total = gbands[0]
        for step in range(1, 16):
            total = total + pltpu.roll(gbands[step], length - 8 * step, 1)
        line = total[0:1]
        for sub in range(1, 8):
            line = line + pltpu.roll(total, length - sub, 1)[sub : sub + 1]
        gkern_ref[head] = line
        return carry

    lax.fori_loop(0, heads, head_body, 0)
    gq_ref[:, 0 : heads * size, :] = gqt[...].astype(BF)
    for head in range(heads):
        gk_ref[:, head * size : (head + 1) * size] = gkacc[head]
        for block in range(key_blocks):
            part = gvacc[head, block * TILE : (block + 1) * TILE, :].T
            gv_ref[block, v_base + head * size : v_base + (head + 1) * size, :] = part.astype(gv_ref.dtype)


def mix_bwd_merged(v_base, *refs):
    mix_bwd_kernel(v_base, *refs[:7], refs[7], refs[8], refs[7], *refs[9:])


def mix_bwd(q, k_win, v_win, grad, kern_asc, seg_q, seg_k):
    blocks = q.shape[0]
    wide, width = k_win.shape
    heads, _, length = kern_asc.shape
    size = width // heads
    rows = blocks * TILE
    shape = (blocks, width, TILE)
    v_base = v_win.shape[1] - width
    outs = [
        jax.ShapeDtypeStruct((blocks, v_win.shape[1], TILE), BF),
        jax.ShapeDtypeStruct((wide, width), F32),
        jax.ShapeDtypeStruct((heads, 1, length), F32),
    ]
    if not v_base:
        outs.insert(2, jax.ShapeDtypeStruct(v_win.shape, F32))
    return pl.pallas_call(
        functools.partial(mix_bwd_merged if v_base else mix_bwd_kernel, v_base),
        out_shape=tuple(outs),
        in_specs=[vmem()] * 7,
        out_specs=(vmem(),) * len(outs),
        scratch_shapes=[
            pltpu.VMEM((heads, rows, size), BF),
            pltpu.VMEM((heads, wide, size), BF),
            pltpu.VMEM((heads, wide, size), BF),
            pltpu.VMEM((heads, rows, size), BF),
            pltpu.VMEM((wide // TILE, width, TILE), BF),
            pltpu.VMEM(shape, F32),
            pltpu.VMEM((heads, wide, size), F32),
            pltpu.VMEM((heads, wide, size), F32),
            pltpu.VMEM((16, 8, length), F32),
            pltpu.VMEM((16, 8, length), F32),
            pltpu.VMEM((wide, 128), jnp.int32),
        ],
        compiler_params=params(),
        cost_estimate=cost(40, 8 << 20),
        name="mix_bwd",
    )(q, k_win, v_win, grad, kern_asc, seg_q.reshape(blocks, 1, TILE), seg_k[:, None])


def load_pieces(me, pieces, full, sem, base):
    rows = pieces[0].shape[0]
    copies = []
    for mask, piece in enumerate(pieces):
        place = pl.ds(pl.multiple_of((me ^ mask) * rows, 64), rows)
        copies.append(pltpu.make_async_copy(piece, full.at[place], sem.at[base + mask]))
    for copy in copies:
        copy.start()

    def wait():
        for copy in copies:
            copy.wait()

    return wait


def normal_stats(value):
    center = value - jnp.mean(value, axis=-1, keepdims=True)
    scale = lax.rsqrt(jnp.mean(center * center, axis=-1, keepdims=True) + EPS)
    return center * scale, scale


def normal_grad(grad, hat, scale, gain):
    lead = grad * gain
    first = jnp.mean(lead, axis=-1, keepdims=True)
    second = jnp.mean(lead * hat, axis=-1, keepdims=True)
    return scale * (lead - first - hat * second)


def to_blocks(dest, turned, seqs, groups, base=0):
    share = turned.shape[0] // groups
    for seq in range(seqs):
        for group in range(groups):
            dest[seq * groups + group, base : base + share, :] = turned[
                group * share : (group + 1) * share, seq * TILE : (seq + 1) * TILE
            ]


def from_blocks(dest, blocks, seqs, groups, base=0):
    share = dest.shape[1] // groups
    for seq in range(seqs):
        whole = jnp.concatenate(
            [blocks[seq * groups + group, base : base + share, :] for group in range(groups)], axis=0
        )
        dest[seq * TILE : (seq + 1) * TILE, :] = whole.astype(F32).T.astype(BF)


def turn(value):
    return value.astype(F32).T.astype(BF)


def key_kernel(me_ref, x_ref, n0, n1, n2, n3, w0, w1, w2, w3, act_ref, out_ref, norm_ref, full, sem):
    wait = load_pieces(me_ref[0], (w0, w1, w2, w3), full, sem, 0)
    width = full.shape[0]
    groups = width // out_ref.shape[1]
    seqs = x_ref.shape[0] // TILE
    share = n0.shape[1]
    for owner in range(width // share):
        mask = me_ref[0] ^ owner
        low = jnp.where(mask == 0, n0[...].astype(F32), n1[...].astype(F32))
        high = jnp.where(mask == 2, n2[...].astype(F32), n3[...].astype(F32))
        norm_ref[:, owner * share : (owner + 1) * share] = jnp.where(mask < 2, low, high)
    hat, _ = normal_stats(x_ref[...].astype(F32))
    act_ref[...] = (hat * norm_ref[0:1, :] + norm_ref[1:2, :]).astype(BF)
    wait()
    to_blocks(out_ref, mm(act_ref[...], full[...]).T.astype(BF), seqs, groups)


def key_call(me, x, norms, pieces, blocks):
    tokens, width = x.shape
    return pl.pallas_call(
        key_kernel,
        out_shape=(
            jax.ShapeDtypeStruct((tokens, width), BF),
            jax.ShapeDtypeStruct(blocks, BF),
            jax.ShapeDtypeStruct((2, width), F32),
        ),
        in_specs=[smem()] + [vmem()] * 5 + [hbm()] * 4,
        out_specs=(vmem(),) * 3,
        scratch_shapes=[pltpu.VMEM((width, width), BF), pltpu.SemaphoreType.DMA((4,))],
        compiler_params=params(),
        cost_estimate=cost(0.1, 1 << 16),
        name="key_call",
    )(me, x, *norms, *pieces)


def query_value_kernel(me_ref, act_ref, q0, q1, q2, q3, v0, v1, v2, v3, *rest):
    outs, (qfull, vfull, turned, sem) = rest[:-4], rest[-4:]
    wait_q = load_pieces(me_ref[0], (q0, q1, q2, q3), qfull, sem, 0)
    wait_v = load_pieces(me_ref[0], (v0, v1, v2, v3), vfull, sem, 4)
    share = outs[0].shape[0] // 2
    wait_q()
    turned[0] = mm(act_ref[...], qfull[...]).T.astype(BF)
    wait_v()
    turned[1] = mm(act_ref[...], vfull[...]).T.astype(BF)
    groups = qfull.shape[0] // share
    for mask, out in enumerate(outs):
        there = me_ref[1] ^ mask
        features = pl.ds(pl.multiple_of(lax.rem(there, groups) * share, 64), share)
        tokens = pl.ds(pl.multiple_of(lax.div(there, groups) * TILE, TILE), TILE)
        out[0:share, :] = turned[0, features, tokens]
        out[share : 2 * share, :] = turned[1, features, tokens]


def query_value_call(me, act, q_pieces, v_pieces, blocks):
    width = act.shape[1]
    return pl.pallas_call(
        query_value_kernel,
        out_shape=(jax.ShapeDtypeStruct((2 * blocks[1], blocks[2]), BF),) * blocks[0],
        in_specs=[smem(), vmem()] + [hbm()] * 8,
        out_specs=(vmem(),) * blocks[0],
        scratch_shapes=[
            pltpu.VMEM((width, width), BF),
            pltpu.VMEM((width, width), BF),
            pltpu.VMEM((2, width, act.shape[0]), BF),
            pltpu.SemaphoreType.DMA((8,)),
        ],
        compiler_params=params(),
        cost_estimate=cost(0.1, 1 << 16),
        name="query_value_call",
    )(me, act, *q_pieces, *v_pieces)


GELU_A = 0.7978845608028654
GELU_B = 0.044715


def middle_kernel(
    me_ref, y_ref, x_ref, gain_ref, bias_ref, cot_ref, o0, o1, o2, o3, u0, u1, u2, u3, d0, d1, d2, d3,
    resid_ref, act_ref, hidden_ref, gz_ref, gr_ref, gy_ref, gln_ref,
    ofull, ufull, dfull, mixed, hat, gb, sem,
):
    me = me_ref[0]
    wait_o = load_pieces(me, (o0, o1, o2, o3), ofull, sem, 0)
    wait_u = load_pieces(me, (u0, u1, u2, u3), ufull, sem, 4)
    wait_d = load_pieces(me, (d0, d1, d2, d3), dfull, sem, 8)
    tokens, width = x_ref.shape
    groups = width // y_ref.shape[1]
    seqs = tokens // TILE
    chunk = width
    chunks = ufull.shape[1] // chunk
    from_blocks(mixed, y_ref, seqs, groups)
    wait_o()
    resid_ref[...] = x_ref[...].astype(F32) + mm(mixed[...], ofull[...])
    normed, scale = normal_stats(resid_ref[...])
    hat[...] = normed
    act_ref[...] = (normed * gain_ref[...] + bias_ref[...]).astype(BF)
    gb[...] = jnp.zeros_like(gb)
    wait_u()
    wait_d()

    def body(step, carry):
        rows = pl.ds(pl.multiple_of(lax.rem(step, seqs) * TILE, TILE), TILE)
        cols = pl.ds(pl.multiple_of(lax.div(step, seqs) * chunk, chunk), chunk)
        z = mm(act_ref[rows, :], ufull[:, cols])
        dh = mm_nt(cot_ref[rows, :], dfull[cols, :])
        square = z * z
        t = jnp.tanh(GELU_A * z * (1.0 + GELU_B * square))
        half = 0.5 * (1.0 + t)
        hidden_ref[rows, cols] = (z * half).astype(BF)
        slope = half + 0.5 * z * (1.0 - t * t) * (GELU_A * (1.0 + 3.0 * GELU_B * square))
        gz = (slope * dh).astype(BF)
        gz_ref[rows, cols] = gz
        gb[rows, :] += mm_nt(gz, ufull[:, cols])
        return carry

    lax.fori_loop(0, seqs * chunks, body, 0)
    gln_ref[0:1, :] = jnp.sum(gb[...] * hat[...], axis=0, keepdims=True)
    gln_ref[1:2, :] = jnp.sum(gb[...], axis=0, keepdims=True)
    gr_ref[...] = cot_ref[...].astype(F32) + normal_grad(gb[...], hat[...], scale, gain_ref[...])
    to_blocks(gy_ref, mm_nt(ofull[...], gr_ref[...].astype(BF)).astype(BF), seqs, groups)


def middle_call(me, y, x, gain, bias, cot, o_pieces, u_pieces, d_pieces):
    tokens, width = x.shape
    hidden = u_pieces[0].shape[1]
    return pl.pallas_call(
        middle_kernel,
        out_shape=(
            jax.ShapeDtypeStruct((tokens, width), F32),
            jax.ShapeDtypeStruct((tokens, width), BF),
            jax.ShapeDtypeStruct((tokens, hidden), BF),
            jax.ShapeDtypeStruct((tokens, hidden), BF),
            jax.ShapeDtypeStruct((tokens, width), F32),
            jax.ShapeDtypeStruct(y.shape, BF),
            jax.ShapeDtypeStruct((2, width), F32),
        ),
        in_specs=[smem()] + [vmem()] * 5 + [hbm()] * 12,
        out_specs=(vmem(),) * 7,
        scratch_shapes=[
            pltpu.VMEM((width, width), BF),
            pltpu.VMEM((width, hidden), BF),
            pltpu.VMEM((hidden, width), BF),
            pltpu.VMEM((tokens, width), BF),
            pltpu.VMEM((tokens, width), F32),
            pltpu.VMEM((tokens, width), F32),
            pltpu.SemaphoreType.DMA((12,)),
        ],
        compiler_params=params(),
        cost_estimate=cost(15, 24 << 20),
        name="middle_call",
    )(me, y, x, gain, bias, cot, *o_pieces, *u_pieces, *d_pieces)


def ffn_grads_kernel(
    me_ref, y_ref, resid_ref, act_ref, hidden_ref, gz_ref, gr_ref, cot_ref, d0, d1, d2, d3,
    out_ref, down_keep, down_send, up_keep, up_send, dfull, act_t, low, sem,
):
    me = me_ref[0]
    wait_d = load_pieces(me, (d0, d1, d2, d3), dfull, sem, 0)
    tokens, width = resid_ref.shape
    hidden = hidden_ref.shape[1]
    groups = width // y_ref.shape[1]
    share = width // groups
    wide = hidden // groups
    seqs = tokens // TILE
    act_t[...] = turn(act_ref[...])
    low[...] = gr_ref[...].astype(BF)
    blocks = hidden // width

    def body(slot, carry):
        for down, up, side in ((down_keep, up_keep, 0), (down_send, up_send, 1)):
            owner = me ^ (2 * slot + side)
            part = hidden_ref[:, pl.ds(pl.multiple_of(owner * wide, wide), wide)]
            down[slot] = mm(turn(part), cot_ref[...]).astype(BF)
            part = act_t[pl.ds(pl.multiple_of(owner * share, share), share), :]
            for block in range(blocks):
                value = mm(part, gz_ref[:, block * width : (block + 1) * width])
                up[slot, block * share : (block + 1) * share, :] = value.astype(BF)
            value = mm(y_ref[owner], low[0:TILE, :])
            for seq in range(1, seqs):
                value = value + mm(y_ref[seq * groups + owner], low[seq * TILE : (seq + 1) * TILE, :])
            up[slot, blocks * share : (blocks + 1) * share, :] = value.astype(BF)
        return carry

    lax.fori_loop(0, 2, body, 0)
    wait_d()
    out_ref[...] = (resid_ref[...] + mm(hidden_ref[...], dfull[...])).astype(BF)


def ffn_grads_call(me, y, resid, act, hidden, gz, gr, cot, d_pieces):
    tokens, width = resid.shape
    wide = hidden.shape[1]
    groups = width // y.shape[1]
    down_rows = wide // groups
    up_rows = (wide // width + 1) * (width // groups)
    return pl.pallas_call(
        ffn_grads_kernel,
        out_shape=(
            jax.ShapeDtypeStruct((tokens, width), BF),
            jax.ShapeDtypeStruct((2, down_rows, width), BF),
            jax.ShapeDtypeStruct((2, down_rows, width), BF),
            jax.ShapeDtypeStruct((2, up_rows, width), BF),
            jax.ShapeDtypeStruct((2, up_rows, width), BF),
        ),
        in_specs=[smem()] + [vmem()] * 7 + [hbm()] * 4,
        out_specs=(vmem(),) * 5,
        scratch_shapes=[
            pltpu.VMEM((wide, width), BF),
            pltpu.VMEM((width, tokens), BF),
            pltpu.VMEM((tokens, width), BF),
            pltpu.SemaphoreType.DMA((4,)),
        ],
        compiler_params=params(),
        cost_estimate=cost(19, 24 << 20),
        name="ffn_grads_call",
    )(me, y, resid, act, hidden, gz, gr, cot, *d_pieces)


def input_grads(me, act_t, grad_ref, share, base, keep_ref, send_ref):
    def body(slot, carry):
        for dest, side in ((keep_ref, 0), (send_ref, 1)):
            owner = me ^ (2 * slot + side)
            part = act_t[pl.ds(pl.multiple_of(owner * share, share), share), :]
            dest[slot, base : base + share, :] = mm(part, grad_ref[...]).astype(dest.dtype)
        return carry

    lax.fori_loop(0, 2, body, 0)


def qv_grads_kernel(
    me_ref, gqv_ref, act_ref, q0, q1, q2, q3, v0, v1, v2, v3,
    keep_ref, send_ref, ga_ref, qfull, vfull, act_t, rows, sem,
):
    me = me_ref[0]
    wait_q = load_pieces(me, (q0, q1, q2, q3), qfull, sem, 0)
    wait_v = load_pieces(me, (v0, v1, v2, v3), vfull, sem, 4)
    tokens, width = act_ref.shape
    share = gqv_ref.shape[1] // 2
    groups = width // share
    seqs = tokens // TILE
    act_t[...] = turn(act_ref[...])
    from_blocks(rows, gqv_ref, seqs, groups)
    input_grads(me, act_t, rows, share, 0, keep_ref, send_ref)
    wait_q()
    ga_ref[...] = mm_nt(rows[...], qfull[...])
    from_blocks(rows, gqv_ref, seqs, groups, share)
    input_grads(me, act_t, rows, share, share, keep_ref, send_ref)
    wait_v()
    ga_ref[...] += mm_nt(rows[...], vfull[...])


def qv_grads_call(me, gqv, act, q_pieces, v_pieces):
    tokens, width = act.shape
    share = gqv.shape[1] // 2
    return pl.pallas_call(
        qv_grads_kernel,
        out_shape=(
            jax.ShapeDtypeStruct((2, 2 * share, width), BF),
            jax.ShapeDtypeStruct((2, 2 * share, width), BF),
            jax.ShapeDtypeStruct((tokens, width), F32),
        ),
        in_specs=[smem()] + [vmem()] * 2 + [hbm()] * 8,
        out_specs=(vmem(),) * 3,
        scratch_shapes=[
            pltpu.VMEM((width, width), BF),
            pltpu.VMEM((width, width), BF),
            pltpu.VMEM((width, tokens), BF),
            pltpu.VMEM((tokens, width), BF),
            pltpu.SemaphoreType.DMA((8,)),
        ],
        compiler_params=params(),
        cost_estimate=cost(8, 12 << 20),
        name="qv_grads_call",
    )(me, gqv, act, *q_pieces, *v_pieces)


def last_kernel(
    me_ref, gk_ref, act_ref, ga_ref, x_ref, gr_ref, norm_ref, extra_ref, k0, k1, k2, k3,
    keep_ref, send_ref, gx_ref, kfull, act_t, rows, sem,
):
    me = me_ref[0]
    wait_k = load_pieces(me, (k0, k1, k2, k3), kfull, sem, 0)
    tokens, width = act_ref.shape
    share = gk_ref.shape[1]
    act_t[...] = turn(act_ref[...])
    from_blocks(rows, gk_ref, tokens // TILE, width // share)
    input_grads(me, act_t, rows, share, 0, keep_ref, send_ref)
    wait_k()
    ga = ga_ref[...] + mm_nt(rows[...], kfull[...])
    hat, scale = normal_stats(x_ref[...].astype(F32))
    gain = jnp.sum(ga * hat, axis=0, keepdims=True)
    bias = jnp.sum(ga, axis=0, keepdims=True)
    lines = jnp.concatenate([gain, bias, jnp.zeros((6, width), F32)], axis=0).astype(BF)
    for slot in range(2):
        for dest, mask in ((keep_ref, 2 * slot), (send_ref, 2 * slot + 1)):
            dest[slot, share : share + 8, :] = lines
            dest[slot, share + 8 :, :] = extra_ref[mask]
    gx_ref[...] = (gr_ref[...] + normal_grad(ga, hat, scale, norm_ref[0:1, :])).astype(BF)


def last_call(me, gk, act, ga, x, gr, norm, extra, k_pieces):
    tokens, width = act.shape
    rows = gk.shape[1] + 8 + extra.shape[1]
    return pl.pallas_call(
        last_kernel,
        out_shape=(
            jax.ShapeDtypeStruct((2, rows, width), BF),
            jax.ShapeDtypeStruct((2, rows, width), BF),
            jax.ShapeDtypeStruct((tokens, width), BF),
        ),
        in_specs=[smem()] + [vmem()] * 7 + [hbm()] * 4,
        out_specs=(vmem(),) * 3,
        scratch_shapes=[
            pltpu.VMEM((width, width), BF),
            pltpu.VMEM((width, tokens), BF),
            pltpu.VMEM((tokens, width), BF),
            pltpu.SemaphoreType.DMA((4,)),
        ],
        compiler_params=params(),
        cost_estimate=cost(6, 8 << 20),
        name="last_call",
    )(me, gk, act, ga, x, gr, norm, extra, *k_pieces)


def xor_permute(value, axis, mask):
    count = lax.axis_size(axis)
    return lax.ppermute(value, axis, [(source, source ^ mask) for source in range(count)])


def collect_kernel(me_ref, *refs):
    parts, out = refs[:-1], refs[-1]
    for mask, part in enumerate(parts):
        out[me_ref[1] ^ mask] = part[...]


def swap_parts(me, parts, label, order):
    came = [order(parts[0])] + [xor_permute(part, "dp", mask) for mask, part in enumerate(parts) if mask]
    shape = (len(parts),) + parts[0].shape
    return pl.pallas_call(
        collect_kernel,
        out_shape=jax.ShapeDtypeStruct(shape, BF),
        in_specs=[smem()] + [vmem()] * len(parts),
        out_specs=vmem(),
        compiler_params=params(),
        cost_estimate=cost(0.5, 2 << 20),
        name=label,
    )(me, *came)


def gather_pieces(shard):
    across = xor_permute(shard, "fsdp", 2)
    beside = xor_permute(shard, "fsdp", 1)
    both = xor_permute(across, "fsdp", 1)
    return (shard, beside, across, both)


class Order:
    def __init__(self):
        self.last = None

    def __call__(self, value):
        if self.last is None:
            return value
        return lax.optimization_barrier((value, self.last))[0]

    def mark(self, value):
        self.last = value
        return value


def join_halves(own, other, bit):
    first = jnp.where(bit == 0, own, other)
    second = jnp.where(bit == 0, other, own)
    return jnp.concatenate([first, second], axis=0)


DP_MASKS = (1, 2, 4)


class Reduction:
    def __init__(self, order, keep, send, direct=False, near_first=False):
        self.order = order
        self.keep = keep
        self.move = send
        self.me = lax.axis_index("dp")
        self.steps = [self.core]
        self.near_first = near_first and lax.axis_size("dp") == 8
        if direct or lax.axis_size("dp") != 8:
            self.cuts = []
            self.steps += [self.high, self.scatter_all, self.gather_all]
        else:
            self.cuts = list(DP_MASKS)
            scatters = [functools.partial(self.scatter, mask) for mask in DP_MASKS]
            self.steps += scatters[:1] + [self.high] + scatters[1:] if near_first else [self.high] + scatters
            self.steps += [functools.partial(self.gather, mask) for mask in DP_MASKS[::-1]]

    def next(self):
        if self.steps:
            self.steps.pop(0)()
            self.order.mark(self.move)

    def add(self, came):
        return (self.order(self.keep).astype(F32) + came.astype(F32)).astype(BF)

    def core(self):
        came = xor_permute(self.move, "fsdp", 1)
        total = self.add(came)
        if self.near_first:
            self.cut(total, 1)
        else:
            self.keep, self.move = total[0], total[1]

    def high(self):
        self.cut(self.add(xor_permute(self.move, "fsdp", 2)))

    def cut(self, total, axis=0):
        self.move = total
        if self.cuts:
            bit = (self.me // self.cuts.pop(0)) % 2
            rows = total.shape[axis] // 2
            halves = total.reshape(total.shape[:axis] + (2, rows) + total.shape[axis + 1 :])
            self.keep = lax.dynamic_index_in_dim(halves, bit, axis, keepdims=False)
            self.move = lax.dynamic_index_in_dim(halves, 1 - bit, axis, keepdims=False)

    def scatter(self, mask):
        total = self.add(xor_permute(self.move, "dp", mask))
        if total.ndim == 3:
            self.keep, self.move = total[0], total[1]
        else:
            self.cut(total)

    def gather(self, mask):
        other = xor_permute(self.move, "dp", mask)
        self.move = join_halves(self.order(self.move), other, (self.me // mask) % 2)

    def scatter_all(self):
        rows, cols = self.move.shape
        count = lax.axis_size("dp")
        parts = lax.all_to_all(self.move.reshape(count, rows // count, cols), "dp", 0, 0)
        self.move = jnp.sum(self.order(parts).astype(F32), axis=0).astype(BF)

    def gather_all(self):
        rows, cols = self.move.shape
        count = lax.axis_size("dp")
        spread = jnp.broadcast_to(self.move[None], (count, rows, cols))
        self.move = lax.all_to_all(spread, "dp", 0, 0).reshape(count * rows, cols)

    def result(self):
        while self.steps:
            self.next()
        return self.move.astype(F32)


def kernel_rows(rate, freq, coef, skip, lags, reach):
    lag = lags.astype(F32)
    inside = (lags >= 0) & (lags < reach)
    clipped = jnp.where(inside, lag, 0.0)
    decay = jnp.exp(-rate[:, :, None] * clipped)
    angle = freq[:, :, None] * clipped
    wave = coef[0][:, :, None] * jnp.cos(angle) - coef[1][:, :, None] * jnp.sin(angle)
    first = (lags == 0).astype(F32)
    return jnp.where(inside, jnp.sum(decay * wave, axis=1) + skip[:, None] * first, 0.0)


def shards(
    tokens, segments, ln1_gain, ln1_bias, w_query, w_key, w_value, shift_taps, ssm_rate, ssm_freq,
    ssm_coef, ssm_skip, w_out, ln2_gain, ln2_bias, w_up, w_down, cotangent,
):
    seqs, rows, width = tokens.shape
    fsdp = lax.axis_size("fsdp")
    dp = lax.axis_size("dp")
    run = HOPS
    place = lax.axis_index("fsdp")
    me = lax.axis_index("dp")
    chunk, inner = me // run, me % run
    group_count = run // seqs
    share = width // group_count
    seq, group = inner // group_count, inner % group_count
    span = run * rows
    multi = dp > run
    groups = [list(range(base, base + run)) for base in range(0, dp, run)] if multi else None
    reach = HOPS * rows + rows
    assert dp % run == 0 and rows == TILE and fsdp == 4 and group_count == fsdp
    blocks = (run, share, rows)

    def exchange(value):
        return lax.all_to_all(value, "dp", 0, 0, axis_index_groups=groups)

    def from_prev(value):
        if not multi:
            return jnp.zeros_like(value)
        return lax.ppermute(value, "dp", [(src, src + run) for src in range(dp - run)])

    def from_next(value):
        return lax.ppermute(value, "dp", [(src + run, src) for src in range(dp - run)])

    key_w = gather_pieces(w_key)
    norm_one = gather_pieces(jnp.stack([ln1_gain, ln1_bias]))
    w_query, w_value, w_out, _ = lax.optimization_barrier((w_query, w_value, w_out, key_w[2]))
    query_w = gather_pieces(w_query)
    value_w = gather_pieces(w_value)
    out_w = gather_pieces(w_out)
    w_up, w_down, _ = lax.optimization_barrier((w_up, w_down, value_w[2]))
    up_w = gather_pieces(w_up)
    down_w = gather_pieces(w_down)
    small_parts = (shift_taps, ssm_rate, ssm_freq, ssm_coef, ssm_skip, ln2_gain, ln2_bias)
    flat = jnp.concatenate([part.reshape(-1) for part in small_parts])
    padded = -(-flat.shape[0] // 1024) * 1024
    flat = jnp.pad(flat, (0, padded - flat.shape[0])).reshape(padded // 128, 128)
    flat, _ = lax.optimization_barrier((flat, key_w[2]))
    in_order = jnp.stack(gather_pieces(flat)).reshape(fsdp, padded)
    small = in_order[jnp.arange(fsdp) ^ place]
    pieces, at = [], 0
    for part in small_parts:
        pieces.append(small[:, at : at + part.size])
        at += part.size
    gain_two, bias_two = (pieces[index].reshape(1, width).astype(F32) for index in (5, 6))

    def mine(piece, shape):
        return lax.dynamic_index_in_dim(piece, group, 0, keepdims=False).reshape(shape).astype(F32)

    taps = mine(pieces[0], shift_taps.shape)
    rate = mine(pieces[1], ssm_rate.shape)
    freq = mine(pieces[2], ssm_freq.shape)
    coef = mine(pieces[3], ssm_coef.shape)
    skip = mine(pieces[4], ssm_skip.shape)

    lags = jnp.arange(reach + TILE) - TILE
    kern, kern_pull = jax.vjp(lambda *leaves: kernel_rows(*leaves, lags, reach), rate, freq, coef, skip)
    kern = kern[:, None, :]

    seg_row = lax.dynamic_index_in_dim(segments, seq, 0, keepdims=False)
    seg_wide = jnp.concatenate(
        [jnp.full((span,), -1, jnp.int32), seg_row, jnp.full((HALO,), -2, jnp.int32)]
    )
    seg_full = lax.dynamic_slice_in_dim(seg_wide, chunk * span + span - HALO, span + 2 * HALO, 0)
    seg_q = seg_full[HALO : HALO + span]
    seg_k = lax.dynamic_slice_in_dim(seg_wide, chunk * span, 2 * span, 0) if multi else seg_q

    taps_tiles = lane_taps(taps)

    which = jnp.stack([place, inner]).astype(jnp.int32)
    x = tokens.reshape(seqs * rows, width)
    cot = cotangent.reshape(seqs * rows, width)
    act_one, k_mine, norm = key_call(which, x, norm_one, key_w, blocks)
    k_own = exchange(k_mine)
    qv_parts = query_value_call(which, act_one, query_w, value_w, blocks)
    k_halo = from_prev(k_own[-1, :, rows - HALO :].T)
    ks_own = shift_fwd(seg_full, k_own, k_halo, taps_tiles)
    forward = Order()
    forward.mark((ks_own, up_w[2]))
    qv_own = swap_parts(which, qv_parts, "collect_qv", forward)
    if multi:
        ks_win = jnp.concatenate([from_prev(ks_own), ks_own], axis=0)
        v_own = qv_own[:, share:]
        v_win = jnp.concatenate([from_prev(v_own), v_own], axis=0)
    else:
        ks_win, v_win = ks_own, qv_own
    y_own = mix_fwd(qv_own, ks_win, v_win, kern, seg_q, seg_k)
    forward.mark(down_w[2])
    y_mine = exchange(forward(y_own))
    resid, act_two, hidden, gz, gr, gy_mine, gln_two = middle_call(
        which, y_mine, x, gain_two, bias_two, cot, out_w, up_w, down_w
    )
    gy_own = exchange(gy_mine)
    order = Order()
    output, down_keep, down_send, up_keep, up_send = ffn_grads_call(
        which, y_mine, resid, act_two, hidden, gz, gr, cot, down_w
    )
    down_sum = Reduction(order, down_keep, down_send, near_first=True)
    up_sum = Reduction(order, up_keep, up_send)

    down_sum.move, up_sum.move, gy_own = lax.optimization_barrier((down_sum.move, up_sum.move, gy_own))
    down_sum.next()
    up_sum.next()
    gy_own = order(gy_own)
    if multi:
        gq_own, gks_win, gv_win, gkern = mix_bwd(qv_own, ks_win, v_win, gy_own, kern, seg_q, seg_k)
        gks_own = gks_win[span:] + from_next(gks_win[:span].astype(BF)).astype(F32)
        gv_own = (gv_win[run:] + from_next(gv_win[:run].astype(BF)).astype(F32)).astype(BF)
        gqv_own = jnp.concatenate([gq_own, gv_own], axis=1)
        gks_halo = from_next(gks_own[:HALO].astype(BF)).astype(F32)
    else:
        gqv_own, gks_own, gkern = mix_bwd(qv_own, ks_win, v_win, gy_own, kern, seg_q, seg_k)
        gks_halo = jnp.zeros((HALO, share), F32)
    order.mark(gkern)
    gqv_mine = exchange(gqv_own)
    down_sum.next()
    up_sum.next()
    gks_own = order(gks_own)
    taps_grad, gk_own = shift_bwd(seg_full, k_own, k_halo, gks_own, gks_halo, taps_tiles)
    order.mark(taps_grad)
    down_sum.next()
    up_sum.next()
    rate_grad, freq_grad, coef_grad, skip_grad = kern_pull(order(gkern)[:, 0, :])

    ssm_line = jnp.concatenate([grad.reshape(-1) for grad in (rate_grad, freq_grad, coef_grad, skip_grad)])
    ssm_line = jnp.pad(ssm_line, (0, width - ssm_line.shape[0]))[None]
    by_group = jnp.concatenate([taps_grad.reshape(-1, width), ssm_line])
    slots = (jnp.arange(fsdp) ^ place) == group
    by_group = jnp.where(slots[:, None, None], by_group[None], 0.0)
    extra = jnp.concatenate([jnp.broadcast_to(gln_two, (fsdp, 2, width)), by_group], axis=1).astype(BF)
    extra = jnp.pad(extra, ((0, 0), (0, 56 - extra.shape[1]), (0, 0)))
    order.mark(extra)
    gk_own, gqv_mine = lax.optimization_barrier((gk_own, order(gqv_mine)))
    gk_mine = exchange(gk_own)
    *qv_grads, ga = qv_grads_call(which, gqv_mine, act_one, query_w, value_w)
    qv_sum = Reduction(order, *qv_grads)
    order.mark(qv_sum.move)
    chains = {"q": qv_sum, "u": up_sum, "d": down_sum}
    for name in "":
        chains[name].next()
    keep_c, send_c, input_grad = last_call(which, order(gk_mine), act_one, ga, x, gr, norm, extra, key_w)
    key_sum = Reduction(order, keep_c, send_c, direct=True)
    order.mark(send_c)

    shard = width // fsdp
    chains["k"] = key_sum
    for name in "qdukdquqdukqdukqkqqq":
        chains[name].next()
    key_rows, query_value, up_out, down_grad = (
        chain.result() for chain in (key_sum, qv_sum, up_sum, down_sum)
    )
    key_grad = key_rows[:shard]
    up_grad = up_out[:-shard]
    up_grad = up_grad.reshape(-1, shard, width).transpose(1, 0, 2).reshape(w_up.shape)
    out_grad = up_out[-shard:]
    query_grad, value_grad = query_value[:shard], query_value[shard:]
    norms = jnp.concatenate([key_rows[shard : shard + 2], key_rows[shard + 8 : shard + 10]])
    norms = lax.dynamic_slice_in_dim(norms, place * shard, shard, 1)
    owned = jnp.concatenate([norms.reshape(-1), key_rows[shard + 10 :].reshape(-1)])
    shapes = [ln1_gain.shape, ln1_bias.shape, ln2_gain.shape, ln2_bias.shape, shift_taps.shape]
    shapes += [ssm_rate.shape, ssm_freq.shape, ssm_coef.shape, ssm_skip.shape]
    little, at = [], 0
    for shape in shapes:
        count = int(np.prod(shape))
        little.append(owned[at : at + count].reshape(shape))
        at += count
    return (
        output.reshape(seqs, rows, width),
        input_grad.reshape(seqs, rows, width),
        little[0],
        little[1],
        query_grad,
        key_grad,
        value_grad,
        little[4],
        little[5],
        little[6],
        little[7],
        little[8],
        out_grad,
        little[2],
        little[3],
        up_grad,
        down_grad,
    )


def solution(mesh):
    return jax.shard_map(
        shards,
        mesh=mesh,
        in_specs=(
            P("fsdp", "dp", None),
            P("fsdp", None),
            P("fsdp"),
            P("fsdp"),
            P("fsdp", None),
            P("fsdp", None),
            P("fsdp", None),
            P(None, "fsdp"),
            P("fsdp", None),
            P("fsdp", None),
            P(None, "fsdp", None),
            P("fsdp"),
            P("fsdp", None),
            P("fsdp"),
            P("fsdp"),
            P("fsdp", None),
            P("fsdp", None),
            P("fsdp", "dp", None),
        ),
        out_specs=(
            P("fsdp", "dp", None),
            P("fsdp", "dp", None),
            P("fsdp"),
            P("fsdp"),
            P("fsdp", None),
            P("fsdp", None),
            P("fsdp", None),
            P(None, "fsdp"),
            P("fsdp", None),
            P("fsdp", None),
            P(None, "fsdp", None),
            P("fsdp"),
            P("fsdp", None),
            P("fsdp"),
            P("fsdp"),
            P("fsdp", None),
            P("fsdp", None),
        ),
        check_vma=False,
    )
```

```python
import functools

import jax
import jax.numpy as jnp
import numpy as np
from jax import lax
from jax.experimental import pallas as pl
from jax.experimental.pallas import tpu as pltpu
from jax.sharding import PartitionSpec as P

SHIFT = 64
HOPS = 8
TILE = 256
HALO = 64
EPS = 1e-05
BF = jnp.bfloat16
F32 = jnp.float32
VMEM_BYTES = 56 * 1024 * 1024


def vmem():
    return pl.BlockSpec(memory_space=pltpu.VMEM)


def smem():
    return pl.BlockSpec(memory_space=pltpu.SMEM)


def hbm():
    return pl.BlockSpec(memory_space=pl.ANY)


def params():
    return pltpu.CompilerParams(vmem_limit_bytes=VMEM_BYTES)


SCALE = 1


def cost(micros, moved):
    return pl.CostEstimate(
        flops=int(micros * 1.0e9) // SCALE, bytes_accessed=int(moved) // (8 * SCALE), transcendentals=0
    )


def mm(left, right):
    return lax.dot_general(left, right, (((1,), (0,)), ((), ())), preferred_element_type=F32)


def mm_nt(left, right):
    return lax.dot_general(left, right, (((1,), (1,)), ((), ())), preferred_element_type=F32)


def tn(left, right):
    return lax.dot_general(left, right, (((0,), (0,)), ((), ())), preferred_element_type=F32)


def cut_lanes(width, rows):
    tiles = [(base, 128, rows, False) for base in range(0, width - 127, 128)]
    if width % 128:
        assert width % 128 == 64
        tiles.append((width - 64, 64, rows // 2, True))
    return tiles


def fill_ext_t(ext, source, halo, width, lead):
    rows = source.shape[0] * TILE
    first = HALO if lead else 0
    for index, (base, size, span, packed) in enumerate(cut_lanes(width, rows)):
        halo_at = 0 if lead else span
        blocks = span // TILE
        sides = [(0, 0)] + ([(64, span)] if packed else [])
        for lane, token in sides:
            lanes = slice(lane, lane + size)
            for block in range(blocks):
                part = source[token // TILE + block, base : base + size, :].astype(F32).T
                ext[index, first + block * TILE : first + (block + 1) * TILE, lanes] = part
            if lead and token:
                part = source[token // TILE - 1, base : base + size, TILE - 128 :].astype(F32).T[128 - HALO :]
            else:
                part = halo[:, base : base + size].astype(F32)
            ext[index, halo_at : halo_at + HALO, lanes] = part


def fill_ext(ext, source, halo, width):
    rows = source.shape[0]
    for index, (base, size, span, packed) in enumerate(cut_lanes(width, rows)):
        features = slice(base, base + size)
        if packed:
            ext[index, 0 : span + HALO, 0:size] = source[0 : span + HALO, features]
            ext[index, 0:span, size : 2 * size] = source[span:rows, features]
            ext[index, span : span + HALO, size : 2 * size] = halo[:, features]
        else:
            ext[index, 0:span, :] = source[:, features]
            ext[index, span : span + HALO, :] = halo[:, features]


def fill_segments(seg_b, seg_p, column):
    total = column.shape[0]
    seg_b[...] = jnp.broadcast_to(column[...], seg_b.shape)
    if seg_p is not None:
        half = seg_p.shape[0]
        seg_p[:, 0:64] = seg_b[0:half, 0:64]
        seg_p[:, 64:128] = seg_b[total - half : total, 64:128]


def windows(source, index, start, way):
    for fine in range(8):
        if way < 0:
            window = source[index, pl.ds(start + HALO - 56 - fine, 120), :]
        else:
            window = source[index, pl.ds(start + fine, 120), :]
        for coarse in range(SHIFT // 8):
            at = 56 - 8 * coarse if way < 0 else 8 * coarse
            yield 8 * coarse + fine, window[at : at + 64]


def seg_windows(seg_b, start, way):
    for fine in range(8):
        if way < 0:
            window = seg_b[pl.ds(start + HALO - 56 - fine, 120), :]
        else:
            window = seg_b[pl.ds(start + HALO + fine, 120), :]
        for coarse in range(SHIFT // 8):
            at = 56 - 8 * coarse if way < 0 else 8 * coarse
            yield window[at : at + 64]


def filtered(source, index, start, taps_ref, seg, way, clear):
    def plain():
        total = jnp.zeros((64, 128), F32)
        for lag, part in windows(source, index, start, way):
            total = total + part * taps_ref[index, lag : lag + 1, :]
        return total

    def masked():
        total = jnp.zeros((64, 128), F32)
        now = seg[pl.ds(start + HALO, 64), :]
        pairs = zip(windows(source, index, start, way), seg_windows(seg, start, way))
        for (lag, part), there in pairs:
            total = total + jnp.where(there == now, part * taps_ref[index, lag : lag + 1, :], 0.0)
        return total

    return lax.cond(clear, plain, masked)


def all_same(seg_s, start, first, last, packed, span):
    same = seg_s[start + first] == seg_s[start + last]
    if packed:
        same = jnp.logical_and(same, seg_s[span + start + first] == seg_s[span + start + last])
    return same


def shift_fwd_kernel(seg_s, k_ref, halo_ref, taps_ref, segcol_ref, out_ref, ext, seg_b, seg_p):
    width = k_ref.shape[1]
    rows = k_ref.shape[0] * TILE
    fill_ext_t(ext, k_ref, halo_ref, width, True)
    fill_segments(seg_b, seg_p, segcol_ref)
    for index, (base, size, span, packed) in enumerate(cut_lanes(width, rows)):

        def body(tile, carry):
            start = pl.multiple_of(tile * 64, 64)
            clear = all_same(seg_s, start, 1, HALO + 63, packed, span)
            total = filtered(ext, index, start, taps_ref, seg_p if packed else seg_b, -1, clear)
            out_ref[pl.ds(start, 64), base : base + size] = total[:, 0:size].astype(BF)
            if packed:
                out_ref[pl.ds(start + span, 64), base : base + size] = total[:, size:].astype(BF)
            return carry

        lax.fori_loop(0, span // 64, body, 0)


def lane_taps(taps):
    tiles = []
    for base, size, _, packed in cut_lanes(taps.shape[1], 0):
        part = taps[:, base : base + size]
        tiles.append(jnp.concatenate([part, part], axis=1) if packed else part)
    return jnp.stack(tiles)


def shift_fwd(seg_full, k_own, k_halo, taps):
    count, width, _ = k_own.shape
    rows = count * TILE
    tiles = len(cut_lanes(width, rows))
    return pl.pallas_call(
        shift_fwd_kernel,
        out_shape=jax.ShapeDtypeStruct((rows, width), BF),
        in_specs=[smem(), vmem(), vmem(), vmem(), vmem()],
        out_specs=vmem(),
        scratch_shapes=[
            pltpu.VMEM((tiles, HALO + rows, 128), F32),
            pltpu.VMEM((2 * HALO + rows, 128), jnp.int32),
            pltpu.VMEM((2 * HALO + rows // 2, 128), jnp.int32),
        ],
        compiler_params=params(),
        cost_estimate=cost(10, 2 << 20),
        name="shift_fwd",
    )(seg_full, k_own, k_halo, taps, seg_full[:, None])


def shift_bwd_kernel(
    seg_s, k_ref, halo_ref, g_ref, ghalo_ref, taps_ref, segcol_ref, tg_ref, out_ref,
    ext, gext, seg_b, seg_p, acc, gk_rows,
):
    width = k_ref.shape[1]
    rows = k_ref.shape[0] * TILE
    fill_ext_t(ext, k_ref, halo_ref, width, True)
    fill_ext(gext, g_ref, ghalo_ref, width)
    fill_segments(seg_b, seg_p, segcol_ref)
    acc[...] = jnp.zeros_like(acc)

    def fold(part):
        total = part[0:8]
        for piece in range(1, 8):
            total = total + part[8 * piece : 8 * piece + 8]
        return total

    for index, (base, size, span, packed) in enumerate(cut_lanes(width, rows)):
        seg = seg_p if packed else seg_b

        def body(tile, carry):
            start = pl.multiple_of(tile * 64, 64)
            clear = all_same(seg_s, start, HALO, HALO + 126, packed, span)
            gk_rows[index, pl.ds(start, 64), :] = filtered(gext, index, start, taps_ref, seg, 1, clear)
            grad = gext[index, pl.ds(start, 64), :]
            clear = all_same(seg_s, start, 1, HALO + 63, packed, span)

            @pl.when(clear)
            def _():
                for lag, part in windows(ext, index, start, -1):
                    acc[index, lag] += fold(part * grad)

            @pl.when(jnp.logical_not(clear))
            def _():
                now = seg[pl.ds(start + HALO, 64), :]
                pairs = zip(windows(ext, index, start, -1), seg_windows(seg, start, -1))
                for (lag, part), there in pairs:
                    acc[index, lag] += fold(jnp.where(there == now, part * grad, 0.0))

            return carry

        lax.fori_loop(0, span // 64, body, 0)
        line = jnp.sum(acc[index], axis=1)
        if packed:
            line = line[:, 0:size] + line[:, size:]
        tg_ref[:, base : base + size] = line
        blocks = span // TILE
        for block in range(rows // TILE):
            at = (block % blocks) * TILE
            part = gk_rows[index, at : at + TILE, :].T
            lane = (block // blocks) * size
            out_ref[block, base : base + size, :] = part[lane : lane + size].astype(BF)


def shift_bwd(seg_full, k_own, k_halo, grad, grad_halo, taps):
    count, width, _ = k_own.shape
    rows = count * TILE
    tiles = len(cut_lanes(width, rows))
    return pl.pallas_call(
        shift_bwd_kernel,
        out_shape=(
            jax.ShapeDtypeStruct((SHIFT, width), F32),
            jax.ShapeDtypeStruct(k_own.shape, BF),
        ),
        in_specs=[smem()] + [vmem()] * 6,
        out_specs=(vmem(),) * 2,
        scratch_shapes=[
            pltpu.VMEM((tiles, HALO + rows, 128), F32),
            pltpu.VMEM((tiles, HALO + rows, 128), F32),
            pltpu.VMEM((2 * HALO + rows, 128), jnp.int32),
            pltpu.VMEM((2 * HALO + rows // 2, 128), jnp.int32),
            pltpu.VMEM((tiles, SHIFT, 8, 128), F32),
            pltpu.VMEM((tiles, rows, 128), F32),
        ],
        compiler_params=params(),
        cost_estimate=cost(20, 4 << 20),
        name="shift_bwd",
    )(seg_full, k_own, k_halo, grad, grad_halo, taps, seg_full[:, None])


def build_bands(bands, row):
    length = row.shape[1]
    skewed = pltpu.roll(jnp.broadcast_to(row, (8, length)), 0, 1, stride=1, stride_axis=0)
    for step in range(16):
        bands[step] = pltpu.roll(skewed, 8 * step, 1) if step else skewed


def band_parts(distance, first, count):
    parts = []
    for row in range(first, first + count, 128):
        high = min(128, first + count - row)
        lane = TILE * (1 + distance) - (row // 128) * 128
        parts.append((slice((row % 128) // 8, (row % 128 + high) // 8), slice(lane, lane + TILE), high))
    return parts


def read_band(bands, parts):
    pieces = [bands[steps, :, lanes].reshape(high, TILE) for steps, lanes, high in parts]
    return pieces[0] if len(pieces) == 1 else jnp.concatenate(pieces, axis=0)


def alike(seg_b, rows, seg_line):
    now = seg_b[rows, :]
    return jnp.concatenate([now, now], axis=1) == seg_line


def head_rows(dest, source, heads, size):
    for head in range(heads):
        dest[head] = source[:, head * size : (head + 1) * size]


def head_turn(dest, source, heads, size, base=0):
    for head in range(heads):
        for block in range(source.shape[0]):
            part = source[block, base + head * size : base + (head + 1) * size, :].astype(F32)
            dest[head, block * TILE : (block + 1) * TILE, :] = part.T.astype(dest.dtype)


STRIP = 64


def mix_fwd_kernel(v_base, q_ref, k_ref, v_ref, row_ref, segq_ref, segk_ref, y_ref, kh, bands, seg_b):
    heads = row_ref.shape[0]
    size = k_ref.shape[1] // heads
    query_blocks, key_blocks = q_ref.shape[0], v_ref.shape[0]
    offset = key_blocks - query_blocks
    head_rows(kh, k_ref, heads, size)
    seg_b[...] = jnp.broadcast_to(segk_ref[...], seg_b.shape)

    def head_body(head, carry):
        build_bands(bands, row_ref[head])
        own = pl.ds(pl.multiple_of(head * size, size), size)
        own_v = pl.ds(pl.multiple_of(v_base + head * size, size), size)
        for row in range(query_blocks):
            query = q_ref[row, own, :]
            total = jnp.zeros((size, TILE), F32)
            for col in range(max(0, row + offset - HOPS), row + offset + 1):
                for first in range(0, TILE, STRIP):
                    kern = read_band(bands, band_parts(row + offset - col, first, STRIP))
                    rows = slice(col * TILE + first, col * TILE + first + STRIP)
                    weight = mm(kh[head, rows, :], query) * kern
                    weight = jnp.where(alike(seg_b, rows, segq_ref[row]), weight, 0.0).astype(BF)
                    total = total + mm(v_ref[col, own_v, first : first + STRIP], weight)
            y_ref[row, own, :] = total.astype(BF)
        return carry

    lax.fori_loop(0, heads, head_body, 0)


def mix_fwd(q, k_win, v_win, kern_asc, seg_q, seg_k):
    blocks = q.shape[0]
    wide, width = k_win.shape
    shape = (blocks, width, TILE)
    heads, _, length = kern_asc.shape
    size = width // heads
    return pl.pallas_call(
        functools.partial(mix_fwd_kernel, v_win.shape[1] - width),
        out_shape=jax.ShapeDtypeStruct(shape, BF),
        in_specs=[vmem()] * 6,
        out_specs=vmem(),
        scratch_shapes=[
            pltpu.VMEM((heads, wide, size), BF),
            pltpu.VMEM((16, 8, length), F32),
            pltpu.VMEM((wide, 128), jnp.int32),
        ],
        compiler_params=params(),
        cost_estimate=cost(20, 4 << 20),
        name="mix_fwd",
    )(q, k_win, v_win, kern_asc, seg_q.reshape(blocks, 1, TILE), seg_k[:, None])


def mix_bwd_kernel(
    v_base, q_ref, k_ref, v_ref, g_ref, row_ref, segq_ref, segk_ref, gq_ref, gk_ref, gv_ref, gkern_ref,
    qh, kh, vh, gh, kt, gqt, gkacc, gvacc, bands, gbands, seg_b,
):
    heads, length = row_ref.shape[0], row_ref.shape[2]
    size = k_ref.shape[1] // heads
    query_blocks, key_blocks = q_ref.shape[0], v_ref.shape[0]
    offset = key_blocks - query_blocks
    head_turn(qh, q_ref, heads, size)
    head_rows(kh, k_ref, heads, size)
    head_turn(vh, v_ref, heads, size, v_base)
    head_turn(gh, g_ref, heads, size)
    for head in range(heads):
        for block in range(key_blocks):
            part = kh[head, block * TILE : (block + 1) * TILE, :].astype(F32)
            kt[block, head * size : (head + 1) * size, :] = part.T.astype(BF)
    seg_b[...] = jnp.broadcast_to(segk_ref[...], seg_b.shape)
    gqt[...] = jnp.zeros_like(gqt)

    def head_body(head, carry):
        build_bands(bands, row_ref[head])
        gbands[...] = jnp.zeros_like(gbands)
        own = pl.ds(pl.multiple_of(head * size, size), size)
        for col in range(key_blocks):
            rows = slice(col * TILE, (col + 1) * TILE)
            gk = jnp.zeros((TILE, size), F32)
            gv = jnp.zeros((TILE, size), F32)
            for row in range(max(0, col - offset), min(query_blocks, col - offset + HOPS + 1)):
                parts = band_parts(row + offset - col, 0, TILE)
                kern = read_band(bands, parts)
                score = mm(kh[head, rows, :], q_ref[row, own, :])
                grad = mm(vh[head, rows, :], g_ref[row, own, :])
                live = alike(seg_b, rows, segq_ref[row])
                grad = jnp.where(live, grad, 0.0)
                weight = jnp.where(live, score * kern, 0.0).astype(BF)
                gscore = (grad * kern).astype(BF)
                both = grad * score
                at = 0
                for steps, lanes, high in parts:
                    gbands[steps, :, lanes] += both[at : at + high].reshape(high // 8, 8, TILE)
                    at += high
                queries = slice(row * TILE, (row + 1) * TILE)
                gk = gk + mm(gscore, qh[head, queries, :])
                gv = gv + mm(weight, gh[head, queries, :])
                gqt[row, own, :] += mm(kt[col, own, :], gscore)
            gkacc[head, rows, :] = gk
            gvacc[head, rows, :] = gv
        total = gbands[0]
        for step in range(1, 16):
            total = total + pltpu.roll(gbands[step], length - 8 * step, 1)
        line = total[0:1]
        for sub in range(1, 8):
            line = line + pltpu.roll(total, length - sub, 1)[sub : sub + 1]
        gkern_ref[head] = line
        return carry

    lax.fori_loop(0, heads, head_body, 0)
    gq_ref[:, 0 : heads * size, :] = gqt[...].astype(BF)
    for head in range(heads):
        gk_ref[:, head * size : (head + 1) * size] = gkacc[head]
        for block in range(key_blocks):
            part = gvacc[head, block * TILE : (block + 1) * TILE, :].T
            gv_ref[block, v_base + head * size : v_base + (head + 1) * size, :] = part.astype(gv_ref.dtype)


def mix_bwd_merged(v_base, *refs):
    mix_bwd_kernel(v_base, *refs[:7], refs[7], refs[8], refs[7], *refs[9:])


def mix_bwd(q, k_win, v_win, grad, kern_asc, seg_q, seg_k):
    blocks = q.shape[0]
    wide, width = k_win.shape
    heads, _, length = kern_asc.shape
    size = width // heads
    rows = blocks * TILE
    shape = (blocks, width, TILE)
    v_base = v_win.shape[1] - width
    outs = [
        jax.ShapeDtypeStruct((blocks, v_win.shape[1], TILE), BF),
        jax.ShapeDtypeStruct((wide, width), F32),
        jax.ShapeDtypeStruct((heads, 1, length), F32),
    ]
    if not v_base:
        outs.insert(2, jax.ShapeDtypeStruct(v_win.shape, F32))
    return pl.pallas_call(
        functools.partial(mix_bwd_merged if v_base else mix_bwd_kernel, v_base),
        out_shape=tuple(outs),
        in_specs=[vmem()] * 7,
        out_specs=(vmem(),) * len(outs),
        scratch_shapes=[
            pltpu.VMEM((heads, rows, size), BF),
            pltpu.VMEM((heads, wide, size), BF),
            pltpu.VMEM((heads, wide, size), BF),
            pltpu.VMEM((heads, rows, size), BF),
            pltpu.VMEM((wide // TILE, width, TILE), BF),
            pltpu.VMEM(shape, F32),
            pltpu.VMEM((heads, wide, size), F32),
            pltpu.VMEM((heads, wide, size), F32),
            pltpu.VMEM((16, 8, length), F32),
            pltpu.VMEM((16, 8, length), F32),
            pltpu.VMEM((wide, 128), jnp.int32),
        ],
        compiler_params=params(),
        cost_estimate=cost(40, 8 << 20),
        name="mix_bwd",
    )(q, k_win, v_win, grad, kern_asc, seg_q.reshape(blocks, 1, TILE), seg_k[:, None])


def load_pieces(me, pieces, full, sem, base):
    rows = pieces[0].shape[0]
    copies = []
    for mask, piece in enumerate(pieces):
        place = pl.ds(pl.multiple_of((me ^ mask) * rows, 64), rows)
        copies.append(pltpu.make_async_copy(piece, full.at[place], sem.at[base + mask]))
    for copy in copies:
        copy.start()

    def wait():
        for copy in copies:
            copy.wait()

    return wait


def normal_stats(value):
    center = value - jnp.mean(value, axis=-1, keepdims=True)
    scale = lax.rsqrt(jnp.mean(center * center, axis=-1, keepdims=True) + EPS)
    return center * scale, scale


def normal_grad(grad, hat, scale, gain):
    lead = grad * gain
    first = jnp.mean(lead, axis=-1, keepdims=True)
    second = jnp.mean(lead * hat, axis=-1, keepdims=True)
    return scale * (lead - first - hat * second)


def to_blocks(dest, turned, seqs, groups, base=0):
    share = turned.shape[0] // groups
    for seq in range(seqs):
        for group in range(groups):
            dest[seq * groups + group, base : base + share, :] = turned[
                group * share : (group + 1) * share, seq * TILE : (seq + 1) * TILE
            ]


def from_blocks(dest, blocks, seqs, groups, base=0):
    share = dest.shape[1] // groups
    for seq in range(seqs):
        whole = jnp.concatenate(
            [blocks[seq * groups + group, base : base + share, :] for group in range(groups)], axis=0
        )
        dest[seq * TILE : (seq + 1) * TILE, :] = whole.astype(F32).T.astype(BF)


def turn(value):
    return value.astype(F32).T.astype(BF)


def key_kernel(me_ref, x_ref, n0, n1, n2, n3, w0, w1, w2, w3, act_ref, out_ref, norm_ref, full, sem):
    wait = load_pieces(me_ref[0], (w0, w1, w2, w3), full, sem, 0)
    width = full.shape[0]
    groups = width // out_ref.shape[1]
    seqs = x_ref.shape[0] // TILE
    share = n0.shape[1]
    for owner in range(width // share):
        mask = me_ref[0] ^ owner
        low = jnp.where(mask == 0, n0[...].astype(F32), n1[...].astype(F32))
        high = jnp.where(mask == 2, n2[...].astype(F32), n3[...].astype(F32))
        norm_ref[:, owner * share : (owner + 1) * share] = jnp.where(mask < 2, low, high)
    hat, _ = normal_stats(x_ref[...].astype(F32))
    act_ref[...] = (hat * norm_ref[0:1, :] + norm_ref[1:2, :]).astype(BF)
    wait()
    to_blocks(out_ref, mm(act_ref[...], full[...]).T.astype(BF), seqs, groups)


def key_call(me, x, norms, pieces, blocks):
    tokens, width = x.shape
    return pl.pallas_call(
        key_kernel,
        out_shape=(
            jax.ShapeDtypeStruct((tokens, width), BF),
            jax.ShapeDtypeStruct(blocks, BF),
            jax.ShapeDtypeStruct((2, width), F32),
        ),
        in_specs=[smem()] + [vmem()] * 5 + [hbm()] * 4,
        out_specs=(vmem(),) * 3,
        scratch_shapes=[pltpu.VMEM((width, width), BF), pltpu.SemaphoreType.DMA((4,))],
        compiler_params=params(),
        cost_estimate=cost(0.1, 1 << 16),
        name="key_call",
    )(me, x, *norms, *pieces)


def query_value_kernel(me_ref, act_ref, q0, q1, q2, q3, v0, v1, v2, v3, *rest):
    outs, (qfull, vfull, turned, sem) = rest[:-4], rest[-4:]
    wait_q = load_pieces(me_ref[0], (q0, q1, q2, q3), qfull, sem, 0)
    wait_v = load_pieces(me_ref[0], (v0, v1, v2, v3), vfull, sem, 4)
    share = outs[0].shape[0] // 2
    wait_q()
    turned[0] = mm(act_ref[...], qfull[...]).T.astype(BF)
    wait_v()
    turned[1] = mm(act_ref[...], vfull[...]).T.astype(BF)
    groups = qfull.shape[0] // share
    for mask, out in enumerate(outs):
        there = me_ref[1] ^ mask
        features = pl.ds(pl.multiple_of(lax.rem(there, groups) * share, 64), share)
        tokens = pl.ds(pl.multiple_of(lax.div(there, groups) * TILE, TILE), TILE)
        out[0:share, :] = turned[0, features, tokens]
        out[share : 2 * share, :] = turned[1, features, tokens]


def query_value_call(me, act, q_pieces, v_pieces, blocks):
    width = act.shape[1]
    return pl.pallas_call(
        query_value_kernel,
        out_shape=(jax.ShapeDtypeStruct((2 * blocks[1], blocks[2]), BF),) * blocks[0],
        in_specs=[smem(), vmem()] + [hbm()] * 8,
        out_specs=(vmem(),) * blocks[0],
        scratch_shapes=[
            pltpu.VMEM((width, width), BF),
            pltpu.VMEM((width, width), BF),
            pltpu.VMEM((2, width, act.shape[0]), BF),
            pltpu.SemaphoreType.DMA((8,)),
        ],
        compiler_params=params(),
        cost_estimate=cost(0.1, 1 << 16),
        name="query_value_call",
    )(me, act, *q_pieces, *v_pieces)


GELU_A = 0.7978845608028654
GELU_B = 0.044715


def middle_kernel(
    me_ref, y_ref, x_ref, gain_ref, bias_ref, cot_ref, o0, o1, o2, o3, u0, u1, u2, u3, d0, d1, d2, d3,
    resid_ref, act_ref, hidden_ref, gz_ref, gr_ref, gy_ref, gln_ref,
    ofull, ufull, dfull, mixed, hat, gb, sem,
):
    me = me_ref[0]
    wait_o = load_pieces(me, (o0, o1, o2, o3), ofull, sem, 0)
    wait_u = load_pieces(me, (u0, u1, u2, u3), ufull, sem, 4)
    wait_d = load_pieces(me, (d0, d1, d2, d3), dfull, sem, 8)
    tokens, width = x_ref.shape
    groups = width // y_ref.shape[1]
    seqs = tokens // TILE
    chunk = width
    chunks = ufull.shape[1] // chunk
    from_blocks(mixed, y_ref, seqs, groups)
    wait_o()
    resid_ref[...] = x_ref[...].astype(F32) + mm(mixed[...], ofull[...])
    normed, scale = normal_stats(resid_ref[...])
    hat[...] = normed
    act_ref[...] = (normed * gain_ref[...] + bias_ref[...]).astype(BF)
    gb[...] = jnp.zeros_like(gb)
    wait_u()
    wait_d()

    def body(step, carry):
        rows = pl.ds(pl.multiple_of(lax.rem(step, seqs) * TILE, TILE), TILE)
        cols = pl.ds(pl.multiple_of(lax.div(step, seqs) * chunk, chunk), chunk)
        z = mm(act_ref[rows, :], ufull[:, cols])
        dh = mm_nt(cot_ref[rows, :], dfull[cols, :])
        square = z * z
        t = jnp.tanh(GELU_A * z * (1.0 + GELU_B * square))
        half = 0.5 * (1.0 + t)
        hidden_ref[rows, cols] = (z * half).astype(BF)
        slope = half + 0.5 * z * (1.0 - t * t) * (GELU_A * (1.0 + 3.0 * GELU_B * square))
        gz = (slope * dh).astype(BF)
        gz_ref[rows, cols] = gz
        gb[rows, :] += mm_nt(gz, ufull[:, cols])
        return carry

    lax.fori_loop(0, seqs * chunks, body, 0)
    gln_ref[0:1, :] = jnp.sum(gb[...] * hat[...], axis=0, keepdims=True)
    gln_ref[1:2, :] = jnp.sum(gb[...], axis=0, keepdims=True)
    gr_ref[...] = cot_ref[...].astype(F32) + normal_grad(gb[...], hat[...], scale, gain_ref[...])
    to_blocks(gy_ref, mm_nt(ofull[...], gr_ref[...].astype(BF)).astype(BF), seqs, groups)


def middle_call(me, y, x, gain, bias, cot, o_pieces, u_pieces, d_pieces):
    tokens, width = x.shape
    hidden = u_pieces[0].shape[1]
    return pl.pallas_call(
        middle_kernel,
        out_shape=(
            jax.ShapeDtypeStruct((tokens, width), F32),
            jax.ShapeDtypeStruct((tokens, width), BF),
            jax.ShapeDtypeStruct((tokens, hidden), BF),
            jax.ShapeDtypeStruct((tokens, hidden), BF),
            jax.ShapeDtypeStruct((tokens, width), F32),
            jax.ShapeDtypeStruct(y.shape, BF),
            jax.ShapeDtypeStruct((2, width), F32),
        ),
        in_specs=[smem()] + [vmem()] * 5 + [hbm()] * 12,
        out_specs=(vmem(),) * 7,
        scratch_shapes=[
            pltpu.VMEM((width, width), BF),
            pltpu.VMEM((width, hidden), BF),
            pltpu.VMEM((hidden, width), BF),
            pltpu.VMEM((tokens, width), BF),
            pltpu.VMEM((tokens, width), F32),
            pltpu.VMEM((tokens, width), F32),
            pltpu.SemaphoreType.DMA((12,)),
        ],
        compiler_params=params(),
        cost_estimate=cost(15, 24 << 20),
        name="middle_call",
    )(me, y, x, gain, bias, cot, *o_pieces, *u_pieces, *d_pieces)


def ffn_grads_kernel(
    me_ref, y_ref, resid_ref, act_ref, hidden_ref, gz_ref, gr_ref, cot_ref, d0, d1, d2, d3,
    out_ref, down_keep, down_send, up_keep, up_send, dfull, act_t, low, sem,
):
    me = me_ref[0]
    wait_d = load_pieces(me, (d0, d1, d2, d3), dfull, sem, 0)
    tokens, width = resid_ref.shape
    hidden = hidden_ref.shape[1]
    groups = width // y_ref.shape[1]
    share = width // groups
    wide = hidden // groups
    seqs = tokens // TILE
    act_t[...] = turn(act_ref[...])
    low[...] = gr_ref[...].astype(BF)
    blocks = hidden // width

    def body(slot, carry):
        for down, up, side in ((down_keep, up_keep, 0), (down_send, up_send, 1)):
            owner = me ^ (2 * slot + side)
            part = hidden_ref[:, pl.ds(pl.multiple_of(owner * wide, wide), wide)]
            down[slot] = mm(turn(part), cot_ref[...]).astype(BF)
            part = act_t[pl.ds(pl.multiple_of(owner * share, share), share), :]
            for block in range(blocks):
                value = mm(part, gz_ref[:, block * width : (block + 1) * width])
                up[slot, block * share : (block + 1) * share, :] = value.astype(BF)
            value = mm(y_ref[owner], low[0:TILE, :])
            for seq in range(1, seqs):
                value = value + mm(y_ref[seq * groups + owner], low[seq * TILE : (seq + 1) * TILE, :])
            up[slot, blocks * share : (blocks + 1) * share, :] = value.astype(BF)
        return carry

    lax.fori_loop(0, 2, body, 0)
    wait_d()
    out_ref[...] = (resid_ref[...] + mm(hidden_ref[...], dfull[...])).astype(BF)


def ffn_grads_call(me, y, resid, act, hidden, gz, gr, cot, d_pieces):
    tokens, width = resid.shape
    wide = hidden.shape[1]
    groups = width // y.shape[1]
    down_rows = wide // groups
    up_rows = (wide // width + 1) * (width // groups)
    return pl.pallas_call(
        ffn_grads_kernel,
        out_shape=(
            jax.ShapeDtypeStruct((tokens, width), BF),
            jax.ShapeDtypeStruct((2, down_rows, width), BF),
            jax.ShapeDtypeStruct((2, down_rows, width), BF),
            jax.ShapeDtypeStruct((2, up_rows, width), BF),
            jax.ShapeDtypeStruct((2, up_rows, width), BF),
        ),
        in_specs=[smem()] + [vmem()] * 7 + [hbm()] * 4,
        out_specs=(vmem(),) * 5,
        scratch_shapes=[
            pltpu.VMEM((wide, width), BF),
            pltpu.VMEM((width, tokens), BF),
            pltpu.VMEM((tokens, width), BF),
            pltpu.SemaphoreType.DMA((4,)),
        ],
        compiler_params=params(),
        cost_estimate=cost(19, 24 << 20),
        name="ffn_grads_call",
    )(me, y, resid, act, hidden, gz, gr, cot, *d_pieces)


def input_grads(me, act_t, grad_ref, share, base, keep_ref, send_ref):
    def body(slot, carry):
        for dest, side in ((keep_ref, 0), (send_ref, 1)):
            owner = me ^ (2 * slot + side)
            part = act_t[pl.ds(pl.multiple_of(owner * share, share), share), :]
            dest[slot, base : base + share, :] = mm(part, grad_ref[...]).astype(dest.dtype)
        return carry

    lax.fori_loop(0, 2, body, 0)


def qv_grads_kernel(
    me_ref, gqv_ref, act_ref, q0, q1, q2, q3, v0, v1, v2, v3,
    keep_ref, send_ref, ga_ref, qfull, vfull, act_t, rows, sem,
):
    me = me_ref[0]
    wait_q = load_pieces(me, (q0, q1, q2, q3), qfull, sem, 0)
    wait_v = load_pieces(me, (v0, v1, v2, v3), vfull, sem, 4)
    tokens, width = act_ref.shape
    share = gqv_ref.shape[1] // 2
    groups = width // share
    seqs = tokens // TILE
    act_t[...] = turn(act_ref[...])
    from_blocks(rows, gqv_ref, seqs, groups)
    input_grads(me, act_t, rows, share, 0, keep_ref, send_ref)
    wait_q()
    ga_ref[...] = mm_nt(rows[...], qfull[...])
    from_blocks(rows, gqv_ref, seqs, groups, share)
    input_grads(me, act_t, rows, share, share, keep_ref, send_ref)
    wait_v()
    ga_ref[...] += mm_nt(rows[...], vfull[...])


def qv_grads_call(me, gqv, act, q_pieces, v_pieces):
    tokens, width = act.shape
    share = gqv.shape[1] // 2
    return pl.pallas_call(
        qv_grads_kernel,
        out_shape=(
            jax.ShapeDtypeStruct((2, 2 * share, width), BF),
            jax.ShapeDtypeStruct((2, 2 * share, width), BF),
            jax.ShapeDtypeStruct((tokens, width), F32),
        ),
        in_specs=[smem()] + [vmem()] * 2 + [hbm()] * 8,
        out_specs=(vmem(),) * 3,
        scratch_shapes=[
            pltpu.VMEM((width, width), BF),
            pltpu.VMEM((width, width), BF),
            pltpu.VMEM((width, tokens), BF),
            pltpu.VMEM((tokens, width), BF),
            pltpu.SemaphoreType.DMA((8,)),
        ],
        compiler_params=params(),
        cost_estimate=cost(8, 12 << 20),
        name="qv_grads_call",
    )(me, gqv, act, *q_pieces, *v_pieces)


def last_kernel(
    me_ref, gk_ref, act_ref, ga_ref, x_ref, gr_ref, norm_ref, extra_ref, k0, k1, k2, k3,
    keep_ref, send_ref, gx_ref, kfull, act_t, rows, sem,
):
    me = me_ref[0]
    wait_k = load_pieces(me, (k0, k1, k2, k3), kfull, sem, 0)
    tokens, width = act_ref.shape
    share = gk_ref.shape[1]
    act_t[...] = turn(act_ref[...])
    from_blocks(rows, gk_ref, tokens // TILE, width // share)
    input_grads(me, act_t, rows, share, 0, keep_ref, send_ref)
    wait_k()
    ga = ga_ref[...] + mm_nt(rows[...], kfull[...])
    hat, scale = normal_stats(x_ref[...].astype(F32))
    gain = jnp.sum(ga * hat, axis=0, keepdims=True)
    bias = jnp.sum(ga, axis=0, keepdims=True)
    lines = jnp.concatenate([gain, bias, jnp.zeros((6, width), F32)], axis=0).astype(BF)
    for slot in range(2):
        for dest, mask in ((keep_ref, 2 * slot), (send_ref, 2 * slot + 1)):
            dest[slot, share : share + 8, :] = lines
            dest[slot, share + 8 :, :] = extra_ref[mask]
    gx_ref[...] = (gr_ref[...] + normal_grad(ga, hat, scale, norm_ref[0:1, :])).astype(BF)


def last_call(me, gk, act, ga, x, gr, norm, extra, k_pieces):
    tokens, width = act.shape
    rows = gk.shape[1] + 8 + extra.shape[1]
    return pl.pallas_call(
        last_kernel,
        out_shape=(
            jax.ShapeDtypeStruct((2, rows, width), BF),
            jax.ShapeDtypeStruct((2, rows, width), BF),
            jax.ShapeDtypeStruct((tokens, width), BF),
        ),
        in_specs=[smem()] + [vmem()] * 7 + [hbm()] * 4,
        out_specs=(vmem(),) * 3,
        scratch_shapes=[
            pltpu.VMEM((width, width), BF),
            pltpu.VMEM((width, tokens), BF),
            pltpu.VMEM((tokens, width), BF),
            pltpu.SemaphoreType.DMA((4,)),
        ],
        compiler_params=params(),
        cost_estimate=cost(6, 8 << 20),
        name="last_call",
    )(me, gk, act, ga, x, gr, norm, extra, *k_pieces)


def xor_permute(value, axis, mask):
    count = lax.axis_size(axis)
    return lax.ppermute(value, axis, [(source, source ^ mask) for source in range(count)])


def collect_kernel(me_ref, *refs):
    parts, out = refs[:-1], refs[-1]
    for mask, part in enumerate(parts):
        out[me_ref[1] ^ mask] = part[...]


def swap_parts(me, parts, label, order):
    came = [order(parts[0])] + [xor_permute(part, "dp", mask) for mask, part in enumerate(parts) if mask]
    shape = (len(parts),) + parts[0].shape
    return pl.pallas_call(
        collect_kernel,
        out_shape=jax.ShapeDtypeStruct(shape, BF),
        in_specs=[smem()] + [vmem()] * len(parts),
        out_specs=vmem(),
        compiler_params=params(),
        cost_estimate=cost(0.5, 2 << 20),
        name=label,
    )(me, *came)


def gather_pieces(shard):
    across = xor_permute(shard, "fsdp", 2)
    beside = xor_permute(shard, "fsdp", 1)
    both = xor_permute(across, "fsdp", 1)
    return (shard, beside, across, both)


class Order:
    def __init__(self):
        self.last = None

    def __call__(self, value):
        if self.last is None:
            return value
        return lax.optimization_barrier((value, self.last))[0]

    def mark(self, value):
        self.last = value
        return value


def join_halves(own, other, bit):
    first = jnp.where(bit == 0, own, other)
    second = jnp.where(bit == 0, other, own)
    return jnp.concatenate([first, second], axis=0)


DP_MASKS = (1, 2, 4)


class Reduction:
    def __init__(self, order, keep, send, direct=False, near_first=False):
        self.order = order
        self.keep = keep
        self.move = send
        self.me = lax.axis_index("dp")
        self.steps = [self.core]
        self.near_first = near_first and lax.axis_size("dp") == 8
        if direct or lax.axis_size("dp") != 8:
            self.cuts = []
            self.steps += [self.high, self.scatter_all, self.gather_all]
        else:
            self.cuts = list(DP_MASKS)
            scatters = [functools.partial(self.scatter, mask) for mask in DP_MASKS]
            self.steps += scatters[:1] + [self.high] + scatters[1:] if near_first else [self.high] + scatters
            self.steps += [functools.partial(self.gather, mask) for mask in DP_MASKS[::-1]]

    def next(self):
        if self.steps:
            self.steps.pop(0)()
            self.order.mark(self.move)

    def add(self, came):
        return (self.order(self.keep).astype(F32) + came.astype(F32)).astype(BF)

    def core(self):
        came = xor_permute(self.move, "fsdp", 1)
        total = self.add(came)
        if self.near_first:
            self.cut(total, 1)
        else:
            self.keep, self.move = total[0], total[1]

    def high(self):
        self.cut(self.add(xor_permute(self.move, "fsdp", 2)))

    def cut(self, total, axis=0):
        self.move = total
        if self.cuts:
            bit = (self.me // self.cuts.pop(0)) % 2
            rows = total.shape[axis] // 2
            halves = total.reshape(total.shape[:axis] + (2, rows) + total.shape[axis + 1 :])
            self.keep = lax.dynamic_index_in_dim(halves, bit, axis, keepdims=False)
            self.move = lax.dynamic_index_in_dim(halves, 1 - bit, axis, keepdims=False)

    def scatter(self, mask):
        total = self.add(xor_permute(self.move, "dp", mask))
        if total.ndim == 3:
            self.keep, self.move = total[0], total[1]
        else:
            self.cut(total)

    def gather(self, mask):
        other = xor_permute(self.move, "dp", mask)
        self.move = join_halves(self.order(self.move), other, (self.me // mask) % 2)

    def scatter_all(self):
        rows, cols = self.move.shape
        count = lax.axis_size("dp")
        parts = lax.all_to_all(self.move.reshape(count, rows // count, cols), "dp", 0, 0)
        self.move = jnp.sum(self.order(parts).astype(F32), axis=0).astype(BF)

    def gather_all(self):
        rows, cols = self.move.shape
        count = lax.axis_size("dp")
        spread = jnp.broadcast_to(self.move[None], (count, rows, cols))
        self.move = lax.all_to_all(spread, "dp", 0, 0).reshape(count * rows, cols)

    def result(self):
        while self.steps:
            self.next()
        return self.move.astype(F32)


def kernel_rows(rate, freq, coef, skip, lags, reach):
    lag = lags.astype(F32)
    inside = (lags >= 0) & (lags < reach)
    clipped = jnp.where(inside, lag, 0.0)
    decay = jnp.exp(-rate[:, :, None] * clipped)
    angle = freq[:, :, None] * clipped
    wave = coef[0][:, :, None] * jnp.cos(angle) - coef[1][:, :, None] * jnp.sin(angle)
    first = (lags == 0).astype(F32)
    return jnp.where(inside, jnp.sum(decay * wave, axis=1) + skip[:, None] * first, 0.0)


def shards(
    tokens, segments, ln1_gain, ln1_bias, w_query, w_key, w_value, shift_taps, ssm_rate, ssm_freq,
    ssm_coef, ssm_skip, w_out, ln2_gain, ln2_bias, w_up, w_down, cotangent,
):
    seqs, rows, width = tokens.shape
    fsdp = lax.axis_size("fsdp")
    dp = lax.axis_size("dp")
    run = HOPS
    place = lax.axis_index("fsdp")
    me = lax.axis_index("dp")
    chunk, inner = me // run, me % run
    group_count = run // seqs
    share = width // group_count
    seq, group = inner // group_count, inner % group_count
    span = run * rows
    multi = dp > run
    groups = [list(range(base, base + run)) for base in range(0, dp, run)] if multi else None
    reach = HOPS * rows + rows
    assert dp % run == 0 and rows == TILE and fsdp == 4 and group_count == fsdp
    blocks = (run, share, rows)

    def exchange(value):
        return lax.all_to_all(value, "dp", 0, 0, axis_index_groups=groups)

    def from_prev(value):
        if not multi:
            return jnp.zeros_like(value)
        return lax.ppermute(value, "dp", [(src, src + run) for src in range(dp - run)])

    def from_next(value):
        return lax.ppermute(value, "dp", [(src + run, src) for src in range(dp - run)])

    key_w = gather_pieces(w_key)
    norm_one = gather_pieces(jnp.stack([ln1_gain, ln1_bias]))
    w_query, w_value, w_out, _ = lax.optimization_barrier((w_query, w_value, w_out, key_w[2]))
    query_w = gather_pieces(w_query)
    value_w = gather_pieces(w_value)
    out_w = gather_pieces(w_out)
    w_up, w_down, _ = lax.optimization_barrier((w_up, w_down, value_w[2]))
    up_w = gather_pieces(w_up)
    down_w = gather_pieces(w_down)
    small_parts = (shift_taps, ssm_rate, ssm_freq, ssm_coef, ssm_skip, ln2_gain, ln2_bias)
    flat = jnp.concatenate([part.reshape(-1) for part in small_parts])
    padded = -(-flat.shape[0] // 1024) * 1024
    flat = jnp.pad(flat, (0, padded - flat.shape[0])).reshape(padded // 128, 128)
    flat, _ = lax.optimization_barrier((flat, key_w[2]))
    in_order = jnp.stack(gather_pieces(flat)).reshape(fsdp, padded)
    small = in_order[jnp.arange(fsdp) ^ place]
    pieces, at = [], 0
    for part in small_parts:
        pieces.append(small[:, at : at + part.size])
        at += part.size
    gain_two, bias_two = (pieces[index].reshape(1, width).astype(F32) for index in (5, 6))

    def mine(piece, shape):
        return lax.dynamic_index_in_dim(piece, group, 0, keepdims=False).reshape(shape).astype(F32)

    taps = mine(pieces[0], shift_taps.shape)
    rate = mine(pieces[1], ssm_rate.shape)
    freq = mine(pieces[2], ssm_freq.shape)
    coef = mine(pieces[3], ssm_coef.shape)
    skip = mine(pieces[4], ssm_skip.shape)

    lags = jnp.arange(reach + TILE) - TILE
    kern, kern_pull = jax.vjp(lambda *leaves: kernel_rows(*leaves, lags, reach), rate, freq, coef, skip)
    kern = kern[:, None, :]

    seg_row = lax.dynamic_index_in_dim(segments, seq, 0, keepdims=False)
    seg_wide = jnp.concatenate(
        [jnp.full((span,), -1, jnp.int32), seg_row, jnp.full((HALO,), -2, jnp.int32)]
    )
    seg_full = lax.dynamic_slice_in_dim(seg_wide, chunk * span + span - HALO, span + 2 * HALO, 0)
    seg_q = seg_full[HALO : HALO + span]
    seg_k = lax.dynamic_slice_in_dim(seg_wide, chunk * span, 2 * span, 0) if multi else seg_q

    taps_tiles = lane_taps(taps)

    which = jnp.stack([place, inner]).astype(jnp.int32)
    x = tokens.reshape(seqs * rows, width)
    cot = cotangent.reshape(seqs * rows, width)
    act_one, k_mine, norm = key_call(which, x, norm_one, key_w, blocks)
    k_own = exchange(k_mine)
    qv_parts = query_value_call(which, act_one, query_w, value_w, blocks)
    k_halo = from_prev(k_own[-1, :, rows - HALO :].T)
    ks_own = shift_fwd(seg_full, k_own, k_halo, taps_tiles)
    forward = Order()
    forward.mark((ks_own, up_w[2]))
    qv_own = swap_parts(which, qv_parts, "collect_qv", forward)
    if multi:
        ks_win = jnp.concatenate([from_prev(ks_own), ks_own], axis=0)
        v_own = qv_own[:, share:]
        v_win = jnp.concatenate([from_prev(v_own), v_own], axis=0)
    else:
        ks_win, v_win = ks_own, qv_own
    y_own = mix_fwd(qv_own, ks_win, v_win, kern, seg_q, seg_k)
    forward.mark(down_w[2])
    y_mine = exchange(forward(y_own))
    resid, act_two, hidden, gz, gr, gy_mine, gln_two = middle_call(
        which, y_mine, x, gain_two, bias_two, cot, out_w, up_w, down_w
    )
    gy_own = exchange(gy_mine)
    order = Order()
    output, down_keep, down_send, up_keep, up_send = ffn_grads_call(
        which, y_mine, resid, act_two, hidden, gz, gr, cot, down_w
    )
    down_sum = Reduction(order, down_keep, down_send, near_first=True)
    up_sum = Reduction(order, up_keep, up_send)

    down_sum.move, up_sum.move, gy_own = lax.optimization_barrier((down_sum.move, up_sum.move, gy_own))
    down_sum.next()
    up_sum.next()
    gy_own = order(gy_own)
    if multi:
        gq_own, gks_win, gv_win, gkern = mix_bwd(qv_own, ks_win, v_win, gy_own, kern, seg_q, seg_k)
        gks_own = gks_win[span:] + from_next(gks_win[:span].astype(BF)).astype(F32)
        gv_own = (gv_win[run:] + from_next(gv_win[:run].astype(BF)).astype(F32)).astype(BF)
        gqv_own = jnp.concatenate([gq_own, gv_own], axis=1)
        gks_halo = from_next(gks_own[:HALO].astype(BF)).astype(F32)
    else:
        gqv_own, gks_own, gkern = mix_bwd(qv_own, ks_win, v_win, gy_own, kern, seg_q, seg_k)
        gks_halo = jnp.zeros((HALO, share), F32)
    order.mark(gkern)
    gqv_mine = exchange(gqv_own)
    down_sum.next()
    up_sum.next()
    gks_own = order(gks_own)
    taps_grad, gk_own = shift_bwd(seg_full, k_own, k_halo, gks_own, gks_halo, taps_tiles)
    order.mark(taps_grad)
    down_sum.next()
    rate_grad, freq_grad, coef_grad, skip_grad = kern_pull(order(gkern)[:, 0, :])

    ssm_line = jnp.concatenate([grad.reshape(-1) for grad in (rate_grad, freq_grad, coef_grad, skip_grad)])
    ssm_line = jnp.pad(ssm_line, (0, width - ssm_line.shape[0]))[None]
    by_group = jnp.concatenate([taps_grad.reshape(-1, width), ssm_line])
    slots = (jnp.arange(fsdp) ^ place) == group
    by_group = jnp.where(slots[:, None, None], by_group[None], 0.0)
    extra = jnp.concatenate([jnp.broadcast_to(gln_two, (fsdp, 2, width)), by_group], axis=1).astype(BF)
    extra = jnp.pad(extra, ((0, 0), (0, 56 - extra.shape[1]), (0, 0)))
    order.mark(extra)
    gk_own, gqv_mine = lax.optimization_barrier((gk_own, order(gqv_mine)))
    gk_mine = exchange(gk_own)
    *qv_grads, ga = qv_grads_call(which, gqv_mine, act_one, query_w, value_w)
    qv_sum = Reduction(order, *qv_grads)
    order.mark(qv_sum.move)
    chains = {"q": qv_sum, "u": up_sum, "d": down_sum}
    keep_c, send_c, input_grad = last_call(which, order(gk_mine), act_one, ga, x, gr, norm, extra, key_w)
    key_sum = Reduction(order, keep_c, send_c, direct=True)
    order.mark(send_c)

    shard = width // fsdp
    chains["k"] = key_sum
    for name in "uqdukdquqdukqdukqkqqq":
        chains[name].next()
    key_rows, query_value, up_out, down_grad = (
        chain.result() for chain in (key_sum, qv_sum, up_sum, down_sum)
    )
    key_grad = key_rows[:shard]
    up_grad = up_out[:-shard]
    up_grad = up_grad.reshape(-1, shard, width).transpose(1, 0, 2).reshape(w_up.shape)
    out_grad = up_out[-shard:]
    query_grad, value_grad = query_value[:shard], query_value[shard:]
    norms = jnp.concatenate([key_rows[shard : shard + 2], key_rows[shard + 8 : shard + 10]])
    norms = lax.dynamic_slice_in_dim(norms, place * shard, shard, 1)
    owned = jnp.concatenate([norms.reshape(-1), key_rows[shard + 10 :].reshape(-1)])
    shapes = [ln1_gain.shape, ln1_bias.shape, ln2_gain.shape, ln2_bias.shape, shift_taps.shape]
    shapes += [ssm_rate.shape, ssm_freq.shape, ssm_coef.shape, ssm_skip.shape]
    little, at = [], 0
    for shape in shapes:
        count = int(np.prod(shape))
        little.append(owned[at : at + count].reshape(shape))
        at += count
    return (
        output.reshape(seqs, rows, width),
        input_grad.reshape(seqs, rows, width),
        little[0],
        little[1],
        query_grad,
        key_grad,
        value_grad,
        little[4],
        little[5],
        little[6],
        little[7],
        little[8],
        out_grad,
        little[2],
        little[3],
        up_grad,
        down_grad,
    )


def solution(mesh):
    return jax.shard_map(
        shards,
        mesh=mesh,
        in_specs=(
            P("fsdp", "dp", None),
            P("fsdp", None),
            P("fsdp"),
            P("fsdp"),
            P("fsdp", None),
            P("fsdp", None),
            P("fsdp", None),
            P(None, "fsdp"),
            P("fsdp", None),
            P("fsdp", None),
            P(None, "fsdp", None),
            P("fsdp"),
            P("fsdp", None),
            P("fsdp"),
            P("fsdp"),
            P("fsdp", None),
            P("fsdp", None),
            P("fsdp", "dp", None),
        ),
        out_specs=(
            P("fsdp", "dp", None),
            P("fsdp", "dp", None),
            P("fsdp"),
            P("fsdp"),
            P("fsdp", None),
            P("fsdp", None),
            P("fsdp", None),
            P(None, "fsdp"),
            P("fsdp", None),
            P("fsdp", None),
            P(None, "fsdp", None),
            P("fsdp"),
            P("fsdp", None),
            P("fsdp"),
            P("fsdp"),
            P("fsdp", None),
            P("fsdp", None),
        ),
        check_vma=False,
    )
```

```python
import functools

import jax
import jax.numpy as jnp
import numpy as np
from jax import lax
from jax.experimental import pallas as pl
from jax.experimental.pallas import tpu as pltpu
from jax.sharding import PartitionSpec as P

SHIFT = 64
HOPS = 8
TILE = 256
HALO = 64
EPS = 1e-05
BF = jnp.bfloat16
F32 = jnp.float32
VMEM_BYTES = 56 * 1024 * 1024


def vmem():
    return pl.BlockSpec(memory_space=pltpu.VMEM)


def smem():
    return pl.BlockSpec(memory_space=pltpu.SMEM)


def hbm():
    return pl.BlockSpec(memory_space=pl.ANY)


def params():
    return pltpu.CompilerParams(vmem_limit_bytes=VMEM_BYTES)


SCALE = 1


def cost(micros, moved):
    return pl.CostEstimate(
        flops=int(micros * 1.0e9) // SCALE, bytes_accessed=int(moved) // (8 * SCALE), transcendentals=0
    )


def mm(left, right):
    return lax.dot_general(left, right, (((1,), (0,)), ((), ())), preferred_element_type=F32)


def mm_nt(left, right):
    return lax.dot_general(left, right, (((1,), (1,)), ((), ())), preferred_element_type=F32)


def tn(left, right):
    return lax.dot_general(left, right, (((0,), (0,)), ((), ())), preferred_element_type=F32)


def cut_lanes(width, rows):
    tiles = [(base, 128, rows, False) for base in range(0, width - 127, 128)]
    if width % 128:
        assert width % 128 == 64
        tiles.append((width - 64, 64, rows // 2, True))
    return tiles


def fill_ext_t(ext, source, halo, width, lead):
    rows = source.shape[0] * TILE
    first = HALO if lead else 0
    for index, (base, size, span, packed) in enumerate(cut_lanes(width, rows)):
        halo_at = 0 if lead else span
        blocks = span // TILE
        sides = [(0, 0)] + ([(64, span)] if packed else [])
        for lane, token in sides:
            lanes = slice(lane, lane + size)
            for block in range(blocks):
                part = source[token // TILE + block, base : base + size, :].astype(F32).T
                ext[index, first + block * TILE : first + (block + 1) * TILE, lanes] = part
            if lead and token:
                part = source[token // TILE - 1, base : base + size, TILE - 128 :].astype(F32).T[128 - HALO :]
            else:
                part = halo[:, base : base + size].astype(F32)
            ext[index, halo_at : halo_at + HALO, lanes] = part


def fill_ext(ext, source, halo, width):
    rows = source.shape[0]
    for index, (base, size, span, packed) in enumerate(cut_lanes(width, rows)):
        features = slice(base, base + size)
        if packed:
            ext[index, 0 : span + HALO, 0:size] = source[0 : span + HALO, features]
            ext[index, 0:span, size : 2 * size] = source[span:rows, features]
            ext[index, span : span + HALO, size : 2 * size] = halo[:, features]
        else:
            ext[index, 0:span, :] = source[:, features]
            ext[index, span : span + HALO, :] = halo[:, features]


def fill_segments(seg_b, seg_p, column):
    total = column.shape[0]
    seg_b[...] = jnp.broadcast_to(column[...], seg_b.shape)
    if seg_p is not None:
        half = seg_p.shape[0]
        seg_p[:, 0:64] = seg_b[0:half, 0:64]
        seg_p[:, 64:128] = seg_b[total - half : total, 64:128]


def windows(source, index, start, way):
    for fine in range(8):
        if way < 0:
            window = source[index, pl.ds(start + HALO - 56 - fine, 120), :]
        else:
            window = source[index, pl.ds(start + fine, 120), :]
        for coarse in range(SHIFT // 8):
            at = 56 - 8 * coarse if way < 0 else 8 * coarse
            yield 8 * coarse + fine, window[at : at + 64]


def seg_windows(seg_b, start, way):
    for fine in range(8):
        if way < 0:
            window = seg_b[pl.ds(start + HALO - 56 - fine, 120), :]
        else:
            window = seg_b[pl.ds(start + HALO + fine, 120), :]
        for coarse in range(SHIFT // 8):
            at = 56 - 8 * coarse if way < 0 else 8 * coarse
            yield window[at : at + 64]


def filtered(source, index, start, taps_ref, seg, way, clear):
    def plain():
        total = jnp.zeros((64, 128), F32)
        for lag, part in windows(source, index, start, way):
            total = total + part * taps_ref[index, lag : lag + 1, :]
        return total

    def masked():
        total = jnp.zeros((64, 128), F32)
        now = seg[pl.ds(start + HALO, 64), :]
        pairs = zip(windows(source, index, start, way), seg_windows(seg, start, way))
        for (lag, part), there in pairs:
            total = total + jnp.where(there == now, part * taps_ref[index, lag : lag + 1, :], 0.0)
        return total

    return lax.cond(clear, plain, masked)


def all_same(seg_s, start, first, last, packed, span):
    same = seg_s[start + first] == seg_s[start + last]
    if packed:
        same = jnp.logical_and(same, seg_s[span + start + first] == seg_s[span + start + last])
    return same


def shift_fwd_kernel(seg_s, k_ref, halo_ref, taps_ref, segcol_ref, out_ref, ext, seg_b, seg_p):
    width = k_ref.shape[1]
    rows = k_ref.shape[0] * TILE
    fill_ext_t(ext, k_ref, halo_ref, width, True)
    fill_segments(seg_b, seg_p, segcol_ref)
    for index, (base, size, span, packed) in enumerate(cut_lanes(width, rows)):

        def body(tile, carry):
            start = pl.multiple_of(tile * 64, 64)
            clear = all_same(seg_s, start, 1, HALO + 63, packed, span)
            total = filtered(ext, index, start, taps_ref, seg_p if packed else seg_b, -1, clear)
            out_ref[pl.ds(start, 64), base : base + size] = total[:, 0:size].astype(BF)
            if packed:
                out_ref[pl.ds(start + span, 64), base : base + size] = total[:, size:].astype(BF)
            return carry

        lax.fori_loop(0, span // 64, body, 0)


def lane_taps(taps):
    tiles = []
    for base, size, _, packed in cut_lanes(taps.shape[1], 0):
        part = taps[:, base : base + size]
        tiles.append(jnp.concatenate([part, part], axis=1) if packed else part)
    return jnp.stack(tiles)


def shift_fwd(seg_full, k_own, k_halo, taps):
    count, width, _ = k_own.shape
    rows = count * TILE
    tiles = len(cut_lanes(width, rows))
    return pl.pallas_call(
        shift_fwd_kernel,
        out_shape=jax.ShapeDtypeStruct((rows, width), BF),
        in_specs=[smem(), vmem(), vmem(), vmem(), vmem()],
        out_specs=vmem(),
        scratch_shapes=[
            pltpu.VMEM((tiles, HALO + rows, 128), F32),
            pltpu.VMEM((2 * HALO + rows, 128), jnp.int32),
            pltpu.VMEM((2 * HALO + rows // 2, 128), jnp.int32),
        ],
        compiler_params=params(),
        cost_estimate=cost(10, 2 << 20),
        name="shift_fwd",
    )(seg_full, k_own, k_halo, taps, seg_full[:, None])


def shift_bwd_kernel(
    seg_s, k_ref, halo_ref, g_ref, ghalo_ref, taps_ref, segcol_ref, tg_ref, out_ref,
    ext, gext, seg_b, seg_p, acc, gk_rows,
):
    width = k_ref.shape[1]
    rows = k_ref.shape[0] * TILE
    fill_ext_t(ext, k_ref, halo_ref, width, True)
    fill_ext(gext, g_ref, ghalo_ref, width)
    fill_segments(seg_b, seg_p, segcol_ref)
    acc[...] = jnp.zeros_like(acc)

    def fold(part):
        total = part[0:8]
        for piece in range(1, 8):
            total = total + part[8 * piece : 8 * piece + 8]
        return total

    for index, (base, size, span, packed) in enumerate(cut_lanes(width, rows)):
        seg = seg_p if packed else seg_b

        def body(tile, carry):
            start = pl.multiple_of(tile * 64, 64)
            clear = all_same(seg_s, start, HALO, HALO + 126, packed, span)
            gk_rows[index, pl.ds(start, 64), :] = filtered(gext, index, start, taps_ref, seg, 1, clear)
            grad = gext[index, pl.ds(start, 64), :]
            clear = all_same(seg_s, start, 1, HALO + 63, packed, span)

            @pl.when(clear)
            def _():
                for lag, part in windows(ext, index, start, -1):
                    acc[index, lag] += fold(part * grad)

            @pl.when(jnp.logical_not(clear))
            def _():
                now = seg[pl.ds(start + HALO, 64), :]
                pairs = zip(windows(ext, index, start, -1), seg_windows(seg, start, -1))
                for (lag, part), there in pairs:
                    acc[index, lag] += fold(jnp.where(there == now, part * grad, 0.0))

            return carry

        lax.fori_loop(0, span // 64, body, 0)
        line = jnp.sum(acc[index], axis=1)
        if packed:
            line = line[:, 0:size] + line[:, size:]
        tg_ref[:, base : base + size] = line
        blocks = span // TILE
        for block in range(rows // TILE):
            at = (block % blocks) * TILE
            part = gk_rows[index, at : at + TILE, :].T
            lane = (block // blocks) * size
            out_ref[block, base : base + size, :] = part[lane : lane + size].astype(BF)


def shift_bwd(seg_full, k_own, k_halo, grad, grad_halo, taps):
    count, width, _ = k_own.shape
    rows = count * TILE
    tiles = len(cut_lanes(width, rows))
    return pl.pallas_call(
        shift_bwd_kernel,
        out_shape=(
            jax.ShapeDtypeStruct((SHIFT, width), F32),
            jax.ShapeDtypeStruct(k_own.shape, BF),
        ),
        in_specs=[smem()] + [vmem()] * 6,
        out_specs=(vmem(),) * 2,
        scratch_shapes=[
            pltpu.VMEM((tiles, HALO + rows, 128), F32),
            pltpu.VMEM((tiles, HALO + rows, 128), F32),
            pltpu.VMEM((2 * HALO + rows, 128), jnp.int32),
            pltpu.VMEM((2 * HALO + rows // 2, 128), jnp.int32),
            pltpu.VMEM((tiles, SHIFT, 8, 128), F32),
            pltpu.VMEM((tiles, rows, 128), F32),
        ],
        compiler_params=params(),
        cost_estimate=cost(20, 4 << 20),
        name="shift_bwd",
    )(seg_full, k_own, k_halo, grad, grad_halo, taps, seg_full[:, None])


def build_bands(bands, row):
    length = row.shape[1]
    skewed = pltpu.roll(jnp.broadcast_to(row, (8, length)), 0, 1, stride=1, stride_axis=0)
    for step in range(16):
        bands[step] = pltpu.roll(skewed, 8 * step, 1) if step else skewed


def band_parts(distance, first, count):
    parts = []
    for row in range(first, first + count, 128):
        high = min(128, first + count - row)
        lane = TILE * (1 + distance) - (row // 128) * 128
        parts.append((slice((row % 128) // 8, (row % 128 + high) // 8), slice(lane, lane + TILE), high))
    return parts


def read_band(bands, parts):
    pieces = [bands[steps, :, lanes].reshape(high, TILE) for steps, lanes, high in parts]
    return pieces[0] if len(pieces) == 1 else jnp.concatenate(pieces, axis=0)


def alike(seg_b, rows, seg_line):
    now = seg_b[rows, :]
    return jnp.concatenate([now, now], axis=1) == seg_line


def head_rows(dest, source, heads, size):
    for head in range(heads):
        dest[head] = source[:, head * size : (head + 1) * size]


def head_turn(dest, source, heads, size, base=0):
    for head in range(heads):
        for block in range(source.shape[0]):
            part = source[block, base + head * size : base + (head + 1) * size, :].astype(F32)
            dest[head, block * TILE : (block + 1) * TILE, :] = part.T.astype(dest.dtype)


STRIP = 64


def mix_fwd_kernel(v_base, q_ref, k_ref, v_ref, row_ref, segq_ref, segk_ref, y_ref, kh, bands, seg_b):
    heads = row_ref.shape[0]
    size = k_ref.shape[1] // heads
    query_blocks, key_blocks = q_ref.shape[0], v_ref.shape[0]
    offset = key_blocks - query_blocks
    head_rows(kh, k_ref, heads, size)
    seg_b[...] = jnp.broadcast_to(segk_ref[...], seg_b.shape)

    def head_body(head, carry):
        build_bands(bands, row_ref[head])
        own = pl.ds(pl.multiple_of(head * size, size), size)
        own_v = pl.ds(pl.multiple_of(v_base + head * size, size), size)
        for row in range(query_blocks):
            query = q_ref[row, own, :]
            total = jnp.zeros((size, TILE), F32)
            for col in range(max(0, row + offset - HOPS), row + offset + 1):
                for first in range(0, TILE, STRIP):
                    kern = read_band(bands, band_parts(row + offset - col, first, STRIP))
                    rows = slice(col * TILE + first, col * TILE + first + STRIP)
                    weight = mm(kh[head, rows, :], query) * kern
                    weight = jnp.where(alike(seg_b, rows, segq_ref[row]), weight, 0.0).astype(BF)
                    total = total + mm(v_ref[col, own_v, first : first + STRIP], weight)
            y_ref[row, own, :] = total.astype(BF)
        return carry

    lax.fori_loop(0, heads, head_body, 0)


def mix_fwd(q, k_win, v_win, kern_asc, seg_q, seg_k):
    blocks = q.shape[0]
    wide, width = k_win.shape
    shape = (blocks, width, TILE)
    heads, _, length = kern_asc.shape
    size = width // heads
    return pl.pallas_call(
        functools.partial(mix_fwd_kernel, v_win.shape[1] - width),
        out_shape=jax.ShapeDtypeStruct(shape, BF),
        in_specs=[vmem()] * 6,
        out_specs=vmem(),
        scratch_shapes=[
            pltpu.VMEM((heads, wide, size), BF),
            pltpu.VMEM((16, 8, length), F32),
            pltpu.VMEM((wide, 128), jnp.int32),
        ],
        compiler_params=params(),
        cost_estimate=cost(20, 4 << 20),
        name="mix_fwd",
    )(q, k_win, v_win, kern_asc, seg_q.reshape(blocks, 1, TILE), seg_k[:, None])


def mix_bwd_kernel(
    v_base, q_ref, k_ref, v_ref, g_ref, row_ref, segq_ref, segk_ref, gq_ref, gk_ref, gv_ref, gkern_ref,
    qh, kh, vh, gh, kt, gqt, gkacc, gvacc, bands, gbands, seg_b,
):
    heads, length = row_ref.shape[0], row_ref.shape[2]
    size = k_ref.shape[1] // heads
    query_blocks, key_blocks = q_ref.shape[0], v_ref.shape[0]
    offset = key_blocks - query_blocks
    head_turn(qh, q_ref, heads, size)
    head_rows(kh, k_ref, heads, size)
    head_turn(vh, v_ref, heads, size, v_base)
    head_turn(gh, g_ref, heads, size)
    for head in range(heads):
        for block in range(key_blocks):
            part = kh[head, block * TILE : (block + 1) * TILE, :].astype(F32)
            kt[block, head * size : (head + 1) * size, :] = part.T.astype(BF)
    seg_b[...] = jnp.broadcast_to(segk_ref[...], seg_b.shape)
    gqt[...] = jnp.zeros_like(gqt)

    def head_body(head, carry):
        build_bands(bands, row_ref[head])
        gbands[...] = jnp.zeros_like(gbands)
        own = pl.ds(pl.multiple_of(head * size, size), size)
        for col in range(key_blocks):
            rows = slice(col * TILE, (col + 1) * TILE)
            gk = jnp.zeros((TILE, size), F32)
            gv = jnp.zeros((TILE, size), F32)
            for row in range(max(0, col - offset), min(query_blocks, col - offset + HOPS + 1)):
                parts = band_parts(row + offset - col, 0, TILE)
                kern = read_band(bands, parts)
                score = mm(kh[head, rows, :], q_ref[row, own, :])
                grad = mm(vh[head, rows, :], g_ref[row, own, :])
                live = alike(seg_b, rows, segq_ref[row])
                grad = jnp.where(live, grad, 0.0)
                weight = jnp.where(live, score * kern, 0.0).astype(BF)
                gscore = (grad * kern).astype(BF)
                both = grad * score
                at = 0
                for steps, lanes, high in parts:
                    gbands[steps, :, lanes] += both[at : at + high].reshape(high // 8, 8, TILE)
                    at += high
                queries = slice(row * TILE, (row + 1) * TILE)
                gk = gk + mm(gscore, qh[head, queries, :])
                gv = gv + mm(weight, gh[head, queries, :])
                gqt[row, own, :] += mm(kt[col, own, :], gscore)
            gkacc[head, rows, :] = gk
            gvacc[head, rows, :] = gv
        total = gbands[0]
        for step in range(1, 16):
            total = total + pltpu.roll(gbands[step], length - 8 * step, 1)
        line = total[0:1]
        for sub in range(1, 8):
            line = line + pltpu.roll(total, length - sub, 1)[sub : sub + 1]
        gkern_ref[head] = line
        return carry

    lax.fori_loop(0, heads, head_body, 0)
    gq_ref[:, 0 : heads * size, :] = gqt[...].astype(BF)
    for head in range(heads):
        gk_ref[:, head * size : (head + 1) * size] = gkacc[head]
        for block in range(key_blocks):
            part = gvacc[head, block * TILE : (block + 1) * TILE, :].T
            gv_ref[block, v_base + head * size : v_base + (head + 1) * size, :] = part.astype(gv_ref.dtype)


def mix_bwd_merged(v_base, *refs):
    mix_bwd_kernel(v_base, *refs[:7], refs[7], refs[8], refs[7], *refs[9:])


def mix_bwd(q, k_win, v_win, grad, kern_asc, seg_q, seg_k):
    blocks = q.shape[0]
    wide, width = k_win.shape
    heads, _, length = kern_asc.shape
    size = width // heads
    rows = blocks * TILE
    shape = (blocks, width, TILE)
    v_base = v_win.shape[1] - width
    outs = [
        jax.ShapeDtypeStruct((blocks, v_win.shape[1], TILE), BF),
        jax.ShapeDtypeStruct((wide, width), F32),
        jax.ShapeDtypeStruct((heads, 1, length), F32),
    ]
    if not v_base:
        outs.insert(2, jax.ShapeDtypeStruct(v_win.shape, F32))
    return pl.pallas_call(
        functools.partial(mix_bwd_merged if v_base else mix_bwd_kernel, v_base),
        out_shape=tuple(outs),
        in_specs=[vmem()] * 7,
        out_specs=(vmem(),) * len(outs),
        scratch_shapes=[
            pltpu.VMEM((heads, rows, size), BF),
            pltpu.VMEM((heads, wide, size), BF),
            pltpu.VMEM((heads, wide, size), BF),
            pltpu.VMEM((heads, rows, size), BF),
            pltpu.VMEM((wide // TILE, width, TILE), BF),
            pltpu.VMEM(shape, F32),
            pltpu.VMEM((heads, wide, size), F32),
            pltpu.VMEM((heads, wide, size), F32),
            pltpu.VMEM((16, 8, length), F32),
            pltpu.VMEM((16, 8, length), F32),
            pltpu.VMEM((wide, 128), jnp.int32),
        ],
        compiler_params=params(),
        cost_estimate=cost(40, 8 << 20),
        name="mix_bwd",
    )(q, k_win, v_win, grad, kern_asc, seg_q.reshape(blocks, 1, TILE), seg_k[:, None])


def load_pieces(me, pieces, full, sem, base):
    rows = pieces[0].shape[0]
    copies = []
    for mask, piece in enumerate(pieces):
        place = pl.ds(pl.multiple_of((me ^ mask) * rows, 64), rows)
        copies.append(pltpu.make_async_copy(piece, full.at[place], sem.at[base + mask]))
    for copy in copies:
        copy.start()

    def wait():
        for copy in copies:
            copy.wait()

    return wait


def normal_stats(value):
    center = value - jnp.mean(value, axis=-1, keepdims=True)
    scale = lax.rsqrt(jnp.mean(center * center, axis=-1, keepdims=True) + EPS)
    return center * scale, scale


def normal_grad(grad, hat, scale, gain):
    lead = grad * gain
    first = jnp.mean(lead, axis=-1, keepdims=True)
    second = jnp.mean(lead * hat, axis=-1, keepdims=True)
    return scale * (lead - first - hat * second)


def to_blocks(dest, turned, seqs, groups, base=0):
    share = turned.shape[0] // groups
    for seq in range(seqs):
        for group in range(groups):
            dest[seq * groups + group, base : base + share, :] = turned[
                group * share : (group + 1) * share, seq * TILE : (seq + 1) * TILE
            ]


def from_blocks(dest, blocks, seqs, groups, base=0):
    share = dest.shape[1] // groups
    for seq in range(seqs):
        whole = jnp.concatenate(
            [blocks[seq * groups + group, base : base + share, :] for group in range(groups)], axis=0
        )
        dest[seq * TILE : (seq + 1) * TILE, :] = whole.astype(F32).T.astype(BF)


def turn(value):
    return value.astype(F32).T.astype(BF)


def key_kernel(me_ref, x_ref, n0, n1, n2, n3, w0, w1, w2, w3, act_ref, out_ref, norm_ref, full, sem):
    wait = load_pieces(me_ref[0], (w0, w1, w2, w3), full, sem, 0)
    width = full.shape[0]
    groups = width // out_ref.shape[1]
    seqs = x_ref.shape[0] // TILE
    share = n0.shape[1]
    for owner in range(width // share):
        mask = me_ref[0] ^ owner
        low = jnp.where(mask == 0, n0[...].astype(F32), n1[...].astype(F32))
        high = jnp.where(mask == 2, n2[...].astype(F32), n3[...].astype(F32))
        norm_ref[:, owner * share : (owner + 1) * share] = jnp.where(mask < 2, low, high)
    hat, _ = normal_stats(x_ref[...].astype(F32))
    act_ref[...] = (hat * norm_ref[0:1, :] + norm_ref[1:2, :]).astype(BF)
    wait()
    to_blocks(out_ref, mm(act_ref[...], full[...]).T.astype(BF), seqs, groups)


def key_call(me, x, norms, pieces, blocks):
    tokens, width = x.shape
    return pl.pallas_call(
        key_kernel,
        out_shape=(
            jax.ShapeDtypeStruct((tokens, width), BF),
            jax.ShapeDtypeStruct(blocks, BF),
            jax.ShapeDtypeStruct((2, width), F32),
        ),
        in_specs=[smem()] + [vmem()] * 5 + [hbm()] * 4,
        out_specs=(vmem(),) * 3,
        scratch_shapes=[pltpu.VMEM((width, width), BF), pltpu.SemaphoreType.DMA((4,))],
        compiler_params=params(),
        cost_estimate=cost(0.1, 1 << 16),
        name="key_call",
    )(me, x, *norms, *pieces)


def query_value_kernel(me_ref, act_ref, q0, q1, q2, q3, v0, v1, v2, v3, *rest):
    outs, (qfull, vfull, turned, sem) = rest[:-4], rest[-4:]
    wait_q = load_pieces(me_ref[0], (q0, q1, q2, q3), qfull, sem, 0)
    wait_v = load_pieces(me_ref[0], (v0, v1, v2, v3), vfull, sem, 4)
    share = outs[0].shape[0] // 2
    wait_q()
    turned[0] = mm(act_ref[...], qfull[...]).T.astype(BF)
    wait_v()
    turned[1] = mm(act_ref[...], vfull[...]).T.astype(BF)
    groups = qfull.shape[0] // share
    for mask, out in enumerate(outs):
        there = me_ref[1] ^ mask
        features = pl.ds(pl.multiple_of(lax.rem(there, groups) * share, 64), share)
        tokens = pl.ds(pl.multiple_of(lax.div(there, groups) * TILE, TILE), TILE)
        out[0:share, :] = turned[0, features, tokens]
        out[share : 2 * share, :] = turned[1, features, tokens]


def query_value_call(me, act, q_pieces, v_pieces, blocks):
    width = act.shape[1]
    return pl.pallas_call(
        query_value_kernel,
        out_shape=(jax.ShapeDtypeStruct((2 * blocks[1], blocks[2]), BF),) * blocks[0],
        in_specs=[smem(), vmem()] + [hbm()] * 8,
        out_specs=(vmem(),) * blocks[0],
        scratch_shapes=[
            pltpu.VMEM((width, width), BF),
            pltpu.VMEM((width, width), BF),
            pltpu.VMEM((2, width, act.shape[0]), BF),
            pltpu.SemaphoreType.DMA((8,)),
        ],
        compiler_params=params(),
        cost_estimate=cost(0.1, 1 << 16),
        name="query_value_call",
    )(me, act, *q_pieces, *v_pieces)


GELU_A = 0.7978845608028654
GELU_B = 0.044715


def middle_kernel(
    me_ref, y_ref, x_ref, gain_ref, bias_ref, cot_ref, o0, o1, o2, o3, u0, u1, u2, u3, d0, d1, d2, d3,
    resid_ref, act_ref, hidden_ref, gz_ref, gr_ref, gy_ref, gln_ref,
    ofull, ufull, dfull, mixed, hat, gb, sem,
):
    me = me_ref[0]
    wait_o = load_pieces(me, (o0, o1, o2, o3), ofull, sem, 0)
    wait_u = load_pieces(me, (u0, u1, u2, u3), ufull, sem, 4)
    wait_d = load_pieces(me, (d0, d1, d2, d3), dfull, sem, 8)
    tokens, width = x_ref.shape
    groups = width // y_ref.shape[1]
    seqs = tokens // TILE
    chunk = width
    chunks = ufull.shape[1] // chunk
    from_blocks(mixed, y_ref, seqs, groups)
    wait_o()
    resid_ref[...] = x_ref[...].astype(F32) + mm(mixed[...], ofull[...])
    normed, scale = normal_stats(resid_ref[...])
    hat[...] = normed
    act_ref[...] = (normed * gain_ref[...] + bias_ref[...]).astype(BF)
    gb[...] = jnp.zeros_like(gb)
    wait_u()
    wait_d()

    def body(step, carry):
        rows = pl.ds(pl.multiple_of(lax.rem(step, seqs) * TILE, TILE), TILE)
        cols = pl.ds(pl.multiple_of(lax.div(step, seqs) * chunk, chunk), chunk)
        z = mm(act_ref[rows, :], ufull[:, cols])
        dh = mm_nt(cot_ref[rows, :], dfull[cols, :])
        square = z * z
        t = jnp.tanh(GELU_A * z * (1.0 + GELU_B * square))
        half = 0.5 * (1.0 + t)
        hidden_ref[rows, cols] = (z * half).astype(BF)
        slope = half + 0.5 * z * (1.0 - t * t) * (GELU_A * (1.0 + 3.0 * GELU_B * square))
        gz = (slope * dh).astype(BF)
        gz_ref[rows, cols] = gz
        gb[rows, :] += mm_nt(gz, ufull[:, cols])
        return carry

    lax.fori_loop(0, seqs * chunks, body, 0)
    gln_ref[0:1, :] = jnp.sum(gb[...] * hat[...], axis=0, keepdims=True)
    gln_ref[1:2, :] = jnp.sum(gb[...], axis=0, keepdims=True)
    gr_ref[...] = cot_ref[...].astype(F32) + normal_grad(gb[...], hat[...], scale, gain_ref[...])
    to_blocks(gy_ref, mm_nt(ofull[...], gr_ref[...].astype(BF)).astype(BF), seqs, groups)


def middle_call(me, y, x, gain, bias, cot, o_pieces, u_pieces, d_pieces):
    tokens, width = x.shape
    hidden = u_pieces[0].shape[1]
    return pl.pallas_call(
        middle_kernel,
        out_shape=(
            jax.ShapeDtypeStruct((tokens, width), F32),
            jax.ShapeDtypeStruct((tokens, width), BF),
            jax.ShapeDtypeStruct((tokens, hidden), BF),
            jax.ShapeDtypeStruct((tokens, hidden), BF),
            jax.ShapeDtypeStruct((tokens, width), F32),
            jax.ShapeDtypeStruct(y.shape, BF),
            jax.ShapeDtypeStruct((2, width), F32),
        ),
        in_specs=[smem()] + [vmem()] * 5 + [hbm()] * 12,
        out_specs=(vmem(),) * 7,
        scratch_shapes=[
            pltpu.VMEM((width, width), BF),
            pltpu.VMEM((width, hidden), BF),
            pltpu.VMEM((hidden, width), BF),
            pltpu.VMEM((tokens, width), BF),
            pltpu.VMEM((tokens, width), F32),
            pltpu.VMEM((tokens, width), F32),
            pltpu.SemaphoreType.DMA((12,)),
        ],
        compiler_params=params(),
        cost_estimate=cost(15, 24 << 20),
        name="middle_call",
    )(me, y, x, gain, bias, cot, *o_pieces, *u_pieces, *d_pieces)


def ffn_grads_kernel(
    me_ref, y_ref, resid_ref, act_ref, hidden_ref, gz_ref, gr_ref, cot_ref, d0, d1, d2, d3,
    out_ref, down_keep, down_send, up_keep, up_send, dfull, act_t, low, sem,
):
    me = me_ref[0]
    wait_d = load_pieces(me, (d0, d1, d2, d3), dfull, sem, 0)
    tokens, width = resid_ref.shape
    hidden = hidden_ref.shape[1]
    groups = width // y_ref.shape[1]
    share = width // groups
    wide = hidden // groups
    seqs = tokens // TILE
    act_t[...] = turn(act_ref[...])
    low[...] = gr_ref[...].astype(BF)
    blocks = hidden // width

    def body(slot, carry):
        for down, up, side in ((down_keep, up_keep, 0), (down_send, up_send, 1)):
            owner = me ^ (2 * slot + side)
            part = hidden_ref[:, pl.ds(pl.multiple_of(owner * wide, wide), wide)]
            down[slot] = mm(turn(part), cot_ref[...]).astype(BF)
            part = act_t[pl.ds(pl.multiple_of(owner * share, share), share), :]
            for block in range(blocks):
                value = mm(part, gz_ref[:, block * width : (block + 1) * width])
                up[slot, block * share : (block + 1) * share, :] = value.astype(BF)
            value = mm(y_ref[owner], low[0:TILE, :])
            for seq in range(1, seqs):
                value = value + mm(y_ref[seq * groups + owner], low[seq * TILE : (seq + 1) * TILE, :])
            up[slot, blocks * share : (blocks + 1) * share, :] = value.astype(BF)
        return carry

    lax.fori_loop(0, 2, body, 0)
    wait_d()
    out_ref[...] = (resid_ref[...] + mm(hidden_ref[...], dfull[...])).astype(BF)


def ffn_grads_call(me, y, resid, act, hidden, gz, gr, cot, d_pieces):
    tokens, width = resid.shape
    wide = hidden.shape[1]
    groups = width // y.shape[1]
    down_rows = wide // groups
    up_rows = (wide // width + 1) * (width // groups)
    return pl.pallas_call(
        ffn_grads_kernel,
        out_shape=(
            jax.ShapeDtypeStruct((tokens, width), BF),
            jax.ShapeDtypeStruct((2, down_rows, width), BF),
            jax.ShapeDtypeStruct((2, down_rows, width), BF),
            jax.ShapeDtypeStruct((2, up_rows, width), BF),
            jax.ShapeDtypeStruct((2, up_rows, width), BF),
        ),
        in_specs=[smem()] + [vmem()] * 7 + [hbm()] * 4,
        out_specs=(vmem(),) * 5,
        scratch_shapes=[
            pltpu.VMEM((wide, width), BF),
            pltpu.VMEM((width, tokens), BF),
            pltpu.VMEM((tokens, width), BF),
            pltpu.SemaphoreType.DMA((4,)),
        ],
        compiler_params=params(),
        cost_estimate=cost(19, 24 << 20),
        name="ffn_grads_call",
    )(me, y, resid, act, hidden, gz, gr, cot, *d_pieces)


def input_grads(me, act_t, grad_ref, share, base, keep_ref, send_ref):
    def body(slot, carry):
        for dest, side in ((keep_ref, 0), (send_ref, 1)):
            owner = me ^ (2 * slot + side)
            part = act_t[pl.ds(pl.multiple_of(owner * share, share), share), :]
            dest[slot, base : base + share, :] = mm(part, grad_ref[...]).astype(dest.dtype)
        return carry

    lax.fori_loop(0, 2, body, 0)


def qv_grads_kernel(
    me_ref, gqv_ref, act_ref, q0, q1, q2, q3, v0, v1, v2, v3,
    keep_ref, send_ref, ga_ref, qfull, vfull, act_t, rows, sem,
):
    me = me_ref[0]
    wait_q = load_pieces(me, (q0, q1, q2, q3), qfull, sem, 0)
    wait_v = load_pieces(me, (v0, v1, v2, v3), vfull, sem, 4)
    tokens, width = act_ref.shape
    share = gqv_ref.shape[1] // 2
    groups = width // share
    seqs = tokens // TILE
    act_t[...] = turn(act_ref[...])
    from_blocks(rows, gqv_ref, seqs, groups)
    input_grads(me, act_t, rows, share, 0, keep_ref, send_ref)
    wait_q()
    ga_ref[...] = mm_nt(rows[...], qfull[...])
    from_blocks(rows, gqv_ref, seqs, groups, share)
    input_grads(me, act_t, rows, share, share, keep_ref, send_ref)
    wait_v()
    ga_ref[...] += mm_nt(rows[...], vfull[...])


def qv_grads_call(me, gqv, act, q_pieces, v_pieces):
    tokens, width = act.shape
    share = gqv.shape[1] // 2
    return pl.pallas_call(
        qv_grads_kernel,
        out_shape=(
            jax.ShapeDtypeStruct((2, 2 * share, width), BF),
            jax.ShapeDtypeStruct((2, 2 * share, width), BF),
            jax.ShapeDtypeStruct((tokens, width), F32),
        ),
        in_specs=[smem()] + [vmem()] * 2 + [hbm()] * 8,
        out_specs=(vmem(),) * 3,
        scratch_shapes=[
            pltpu.VMEM((width, width), BF),
            pltpu.VMEM((width, width), BF),
            pltpu.VMEM((width, tokens), BF),
            pltpu.VMEM((tokens, width), BF),
            pltpu.SemaphoreType.DMA((8,)),
        ],
        compiler_params=params(),
        cost_estimate=cost(8, 12 << 20),
        name="qv_grads_call",
    )(me, gqv, act, *q_pieces, *v_pieces)


def last_kernel(
    me_ref, gk_ref, act_ref, ga_ref, x_ref, gr_ref, norm_ref, extra_ref, k0, k1, k2, k3,
    keep_ref, send_ref, gx_ref, kfull, act_t, rows, sem,
):
    me = me_ref[0]
    wait_k = load_pieces(me, (k0, k1, k2, k3), kfull, sem, 0)
    tokens, width = act_ref.shape
    share = gk_ref.shape[1]
    act_t[...] = turn(act_ref[...])
    from_blocks(rows, gk_ref, tokens // TILE, width // share)
    input_grads(me, act_t, rows, share, 0, keep_ref, send_ref)
    wait_k()
    ga = ga_ref[...] + mm_nt(rows[...], kfull[...])
    hat, scale = normal_stats(x_ref[...].astype(F32))
    gain = jnp.sum(ga * hat, axis=0, keepdims=True)
    bias = jnp.sum(ga, axis=0, keepdims=True)
    lines = jnp.concatenate([gain, bias, jnp.zeros((6, width), F32)], axis=0).astype(BF)
    for slot in range(2):
        for dest, mask in ((keep_ref, 2 * slot), (send_ref, 2 * slot + 1)):
            dest[slot, share : share + 8, :] = lines
            dest[slot, share + 8 :, :] = extra_ref[mask]
    gx_ref[...] = (gr_ref[...] + normal_grad(ga, hat, scale, norm_ref[0:1, :])).astype(BF)


def last_call(me, gk, act, ga, x, gr, norm, extra, k_pieces):
    tokens, width = act.shape
    rows = gk.shape[1] + 8 + extra.shape[1]
    return pl.pallas_call(
        last_kernel,
        out_shape=(
            jax.ShapeDtypeStruct((2, rows, width), BF),
            jax.ShapeDtypeStruct((2, rows, width), BF),
            jax.ShapeDtypeStruct((tokens, width), BF),
        ),
        in_specs=[smem()] + [vmem()] * 7 + [hbm()] * 4,
        out_specs=(vmem(),) * 3,
        scratch_shapes=[
            pltpu.VMEM((width, width), BF),
            pltpu.VMEM((width, tokens), BF),
            pltpu.VMEM((tokens, width), BF),
            pltpu.SemaphoreType.DMA((4,)),
        ],
        compiler_params=params(),
        cost_estimate=cost(6, 8 << 20),
        name="last_call",
    )(me, gk, act, ga, x, gr, norm, extra, *k_pieces)


def xor_permute(value, axis, mask):
    count = lax.axis_size(axis)
    return lax.ppermute(value, axis, [(source, source ^ mask) for source in range(count)])


def collect_kernel(me_ref, *refs):
    parts, out = refs[:-1], refs[-1]
    for mask, part in enumerate(parts):
        out[me_ref[1] ^ mask] = part[...]


def swap_parts(me, parts, label, order):
    came = [order(parts[0])] + [xor_permute(part, "dp", mask) for mask, part in enumerate(parts) if mask]
    shape = (len(parts),) + parts[0].shape
    return pl.pallas_call(
        collect_kernel,
        out_shape=jax.ShapeDtypeStruct(shape, BF),
        in_specs=[smem()] + [vmem()] * len(parts),
        out_specs=vmem(),
        compiler_params=params(),
        cost_estimate=cost(0.5, 2 << 20),
        name=label,
    )(me, *came)


def gather_pieces(shard):
    across = xor_permute(shard, "fsdp", 2)
    beside = xor_permute(shard, "fsdp", 1)
    both = xor_permute(across, "fsdp", 1)
    return (shard, beside, across, both)


class Order:
    def __init__(self):
        self.last = None

    def __call__(self, value):
        if self.last is None:
            return value
        return lax.optimization_barrier((value, self.last))[0]

    def mark(self, value):
        self.last = value
        return value


def join_halves(own, other, bit):
    first = jnp.where(bit == 0, own, other)
    second = jnp.where(bit == 0, other, own)
    return jnp.concatenate([first, second], axis=0)


DP_MASKS = (1, 2, 4)


class Reduction:
    def __init__(self, order, keep, send, direct=False, near_first=False):
        self.order = order
        self.keep = keep
        self.move = send
        self.me = lax.axis_index("dp")
        self.steps = [self.core]
        self.near_first = near_first and lax.axis_size("dp") == 8
        if direct or lax.axis_size("dp") != 8:
            self.cuts = []
            self.steps += [self.high, self.scatter_all, self.gather_all]
        else:
            self.cuts = list(DP_MASKS)
            scatters = [functools.partial(self.scatter, mask) for mask in DP_MASKS]
            self.steps += scatters[:1] + [self.high] + scatters[1:] if near_first else [self.high] + scatters
            self.steps += [functools.partial(self.gather, mask) for mask in DP_MASKS[::-1]]

    def next(self):
        if self.steps:
            self.steps.pop(0)()
            self.order.mark(self.move)

    def add(self, came):
        return (self.order(self.keep).astype(F32) + came.astype(F32)).astype(BF)

    def core(self):
        came = xor_permute(self.move, "fsdp", 1)
        total = self.add(came)
        if self.near_first:
            self.cut(total, 1)
        else:
            self.keep, self.move = total[0], total[1]

    def high(self):
        self.cut(self.add(xor_permute(self.move, "fsdp", 2)))

    def cut(self, total, axis=0):
        self.move = total
        if self.cuts:
            bit = (self.me // self.cuts.pop(0)) % 2
            rows = total.shape[axis] // 2
            halves = total.reshape(total.shape[:axis] + (2, rows) + total.shape[axis + 1 :])
            self.keep = lax.dynamic_index_in_dim(halves, bit, axis, keepdims=False)
            self.move = lax.dynamic_index_in_dim(halves, 1 - bit, axis, keepdims=False)

    def scatter(self, mask):
        total = self.add(xor_permute(self.move, "dp", mask))
        if total.ndim == 3:
            self.keep, self.move = total[0], total[1]
        else:
            self.cut(total)

    def gather(self, mask):
        other = xor_permute(self.move, "dp", mask)
        self.move = join_halves(self.order(self.move), other, (self.me // mask) % 2)

    def scatter_all(self):
        rows, cols = self.move.shape
        count = lax.axis_size("dp")
        parts = lax.all_to_all(self.move.reshape(count, rows // count, cols), "dp", 0, 0)
        self.move = jnp.sum(self.order(parts).astype(F32), axis=0).astype(BF)

    def gather_all(self):
        rows, cols = self.move.shape
        count = lax.axis_size("dp")
        spread = jnp.broadcast_to(self.move[None], (count, rows, cols))
        self.move = lax.all_to_all(spread, "dp", 0, 0).reshape(count * rows, cols)

    def result(self):
        while self.steps:
            self.next()
        return self.move.astype(F32)


def kernel_rows(rate, freq, coef, skip, lags, reach):
    lag = lags.astype(F32)
    inside = (lags >= 0) & (lags < reach)
    clipped = jnp.where(inside, lag, 0.0)
    decay = jnp.exp(-rate[:, :, None] * clipped)
    angle = freq[:, :, None] * clipped
    wave = coef[0][:, :, None] * jnp.cos(angle) - coef[1][:, :, None] * jnp.sin(angle)
    first = (lags == 0).astype(F32)
    return jnp.where(inside, jnp.sum(decay * wave, axis=1) + skip[:, None] * first, 0.0)


def shards(
    tokens, segments, ln1_gain, ln1_bias, w_query, w_key, w_value, shift_taps, ssm_rate, ssm_freq,
    ssm_coef, ssm_skip, w_out, ln2_gain, ln2_bias, w_up, w_down, cotangent,
):
    seqs, rows, width = tokens.shape
    fsdp = lax.axis_size("fsdp")
    dp = lax.axis_size("dp")
    run = HOPS
    place = lax.axis_index("fsdp")
    me = lax.axis_index("dp")
    chunk, inner = me // run, me % run
    group_count = run // seqs
    share = width // group_count
    seq, group = inner // group_count, inner % group_count
    span = run * rows
    multi = dp > run
    groups = [list(range(base, base + run)) for base in range(0, dp, run)] if multi else None
    reach = HOPS * rows + rows
    assert dp % run == 0 and rows == TILE and fsdp == 4 and group_count == fsdp
    blocks = (run, share, rows)

    def exchange(value):
        return lax.all_to_all(value, "dp", 0, 0, axis_index_groups=groups)

    def from_prev(value):
        if not multi:
            return jnp.zeros_like(value)
        return lax.ppermute(value, "dp", [(src, src + run) for src in range(dp - run)])

    def from_next(value):
        return lax.ppermute(value, "dp", [(src + run, src) for src in range(dp - run)])

    key_w = gather_pieces(w_key)
    norm_one = gather_pieces(jnp.stack([ln1_gain, ln1_bias]))
    w_query, w_value, w_out, _ = lax.optimization_barrier((w_query, w_value, w_out, key_w[2]))
    query_w = gather_pieces(w_query)
    value_w = gather_pieces(w_value)
    out_w = gather_pieces(w_out)
    w_up, w_down, _ = lax.optimization_barrier((w_up, w_down, value_w[2]))
    up_w = gather_pieces(w_up)
    down_w = gather_pieces(w_down)
    small_parts = (shift_taps, ssm_rate, ssm_freq, ssm_coef, ssm_skip, ln2_gain, ln2_bias)
    flat = jnp.concatenate([part.reshape(-1) for part in small_parts])
    padded = -(-flat.shape[0] // 1024) * 1024
    flat = jnp.pad(flat, (0, padded - flat.shape[0])).reshape(padded // 128, 128)
    flat, _ = lax.optimization_barrier((flat, key_w[2]))
    in_order = jnp.stack(gather_pieces(flat)).reshape(fsdp, padded)
    small = in_order[jnp.arange(fsdp) ^ place]
    pieces, at = [], 0
    for part in small_parts:
        pieces.append(small[:, at : at + part.size])
        at += part.size
    gain_two, bias_two = (pieces[index].reshape(1, width).astype(F32) for index in (5, 6))

    def mine(piece, shape):
        return lax.dynamic_index_in_dim(piece, group, 0, keepdims=False).reshape(shape).astype(F32)

    taps = mine(pieces[0], shift_taps.shape)
    rate = mine(pieces[1], ssm_rate.shape)
    freq = mine(pieces[2], ssm_freq.shape)
    coef = mine(pieces[3], ssm_coef.shape)
    skip = mine(pieces[4], ssm_skip.shape)

    lags = jnp.arange(reach + TILE) - TILE
    kern, kern_pull = jax.vjp(lambda *leaves: kernel_rows(*leaves, lags, reach), rate, freq, coef, skip)
    kern = kern[:, None, :]

    seg_row = lax.dynamic_index_in_dim(segments, seq, 0, keepdims=False)
    seg_wide = jnp.concatenate(
        [jnp.full((span,), -1, jnp.int32), seg_row, jnp.full((HALO,), -2, jnp.int32)]
    )
    seg_full = lax.dynamic_slice_in_dim(seg_wide, chunk * span + span - HALO, span + 2 * HALO, 0)
    seg_q = seg_full[HALO : HALO + span]
    seg_k = lax.dynamic_slice_in_dim(seg_wide, chunk * span, 2 * span, 0) if multi else seg_q

    taps_tiles = lane_taps(taps)

    which = jnp.stack([place, inner]).astype(jnp.int32)
    x = tokens.reshape(seqs * rows, width)
    cot = cotangent.reshape(seqs * rows, width)
    act_one, k_mine, norm = key_call(which, x, norm_one, key_w, blocks)
    k_own = exchange(k_mine)
    qv_parts = query_value_call(which, act_one, query_w, value_w, blocks)
    k_halo = from_prev(k_own[-1, :, rows - HALO :].T)
    ks_own = shift_fwd(seg_full, k_own, k_halo, taps_tiles)
    forward = Order()
    forward.mark((ks_own, up_w[2]))
    qv_own = swap_parts(which, qv_parts, "collect_qv", forward)
    if multi:
        ks_win = jnp.concatenate([from_prev(ks_own), ks_own], axis=0)
        v_own = qv_own[:, share:]
        v_win = jnp.concatenate([from_prev(v_own), v_own], axis=0)
    else:
        ks_win, v_win = ks_own, qv_own
    y_own = mix_fwd(qv_own, ks_win, v_win, kern, seg_q, seg_k)
    forward.mark(down_w[2])
    y_mine = exchange(forward(y_own))
    resid, act_two, hidden, gz, gr, gy_mine, gln_two = middle_call(
        which, y_mine, x, gain_two, bias_two, cot, out_w, up_w, down_w
    )
    gy_own = exchange(gy_mine)
    order = Order()
    output, down_keep, down_send, up_keep, up_send = ffn_grads_call(
        which, y_mine, resid, act_two, hidden, gz, gr, cot, down_w
    )
    down_sum = Reduction(order, down_keep, down_send, near_first=True)
    up_sum = Reduction(order, up_keep, up_send)

    down_sum.move, up_sum.move, gy_own = lax.optimization_barrier((down_sum.move, up_sum.move, gy_own))
    down_sum.next()
    up_sum.next()
    gy_own = order(gy_own)
    if multi:
        gq_own, gks_win, gv_win, gkern = mix_bwd(qv_own, ks_win, v_win, gy_own, kern, seg_q, seg_k)
        gks_own = gks_win[span:] + from_next(gks_win[:span].astype(BF)).astype(F32)
        gv_own = (gv_win[run:] + from_next(gv_win[:run].astype(BF)).astype(F32)).astype(BF)
        gqv_own = jnp.concatenate([gq_own, gv_own], axis=1)
        gks_halo = from_next(gks_own[:HALO].astype(BF)).astype(F32)
    else:
        gqv_own, gks_own, gkern = mix_bwd(qv_own, ks_win, v_win, gy_own, kern, seg_q, seg_k)
        gks_halo = jnp.zeros((HALO, share), F32)
    order.mark(gkern)
    gqv_mine = exchange(gqv_own)
    down_sum.next()
    up_sum.next()
    gks_own = order(gks_own)
    taps_grad, gk_own = shift_bwd(seg_full, k_own, k_halo, gks_own, gks_halo, taps_tiles)
    order.mark(taps_grad)
    down_sum.next()
    rate_grad, freq_grad, coef_grad, skip_grad = kern_pull(order(gkern)[:, 0, :])

    ssm_line = jnp.concatenate([grad.reshape(-1) for grad in (rate_grad, freq_grad, coef_grad, skip_grad)])
    ssm_line = jnp.pad(ssm_line, (0, width - ssm_line.shape[0]))[None]
    by_group = jnp.concatenate([taps_grad.reshape(-1, width), ssm_line])
    slots = (jnp.arange(fsdp) ^ place) == group
    by_group = jnp.where(slots[:, None, None], by_group[None], 0.0)
    extra = jnp.concatenate([jnp.broadcast_to(gln_two, (fsdp, 2, width)), by_group], axis=1).astype(BF)
    extra = jnp.pad(extra, ((0, 0), (0, 56 - extra.shape[1]), (0, 0)))
    order.mark(extra)
    gk_own, gqv_mine = lax.optimization_barrier((gk_own, order(gqv_mine)))
    gk_mine = exchange(gk_own)
    *qv_grads, ga = qv_grads_call(which, gqv_mine, act_one, query_w, value_w)
    qv_sum = Reduction(order, *qv_grads)
    order.mark(qv_sum.move)
    chains = {"q": qv_sum, "u": up_sum, "d": down_sum}
    keep_c, send_c, input_grad = last_call(which, order(gk_mine), act_one, ga, x, gr, norm, extra, key_w)
    key_sum = Reduction(order, keep_c, send_c, direct=True)
    order.mark(send_c)

    shard = width // fsdp
    chains["k"] = key_sum
    for name in "uqdukdquqdukqdukqkqqq":
        chains[name].next()
    key_rows, query_value, up_out, down_grad = (
        chain.result() for chain in (key_sum, qv_sum, up_sum, down_sum)
    )
    key_grad = key_rows[:shard]
    up_grad = up_out[:-shard]
    up_grad = up_grad.reshape(-1, shard, width).transpose(1, 0, 2).reshape(w_up.shape)
    out_grad = up_out[-shard:]
    query_grad, value_grad = query_value[:shard], query_value[shard:]
    norms = jnp.concatenate([key_rows[shard : shard + 2], key_rows[shard + 8 : shard + 10]])
    norms = lax.dynamic_slice_in_dim(norms, place * shard, shard, 1)
    taps_rows = shift_taps.size // width
    modes = key_rows[shard + 10 + taps_rows]
    little, at = [norms[row] for row in range(4)], 0
    little.append(key_rows[shard + 10 : shard + 10 + taps_rows].reshape(shift_taps.shape))
    for shape in (ssm_rate.shape, ssm_freq.shape, ssm_coef.shape, ssm_skip.shape):
        count = int(np.prod(shape))
        little.append(modes[at : at + count].reshape(shape))
        at += count
    return (
        output.reshape(seqs, rows, width),
        input_grad.reshape(seqs, rows, width),
        little[0],
        little[1],
        query_grad,
        key_grad,
        value_grad,
        little[4],
        little[5],
        little[6],
        little[7],
        little[8],
        out_grad,
        little[2],
        little[3],
        up_grad,
        down_grad,
    )


def solution(mesh):
    return jax.shard_map(
        shards,
        mesh=mesh,
        in_specs=(
            P("fsdp", "dp", None),
            P("fsdp", None),
            P("fsdp"),
            P("fsdp"),
            P("fsdp", None),
            P("fsdp", None),
            P("fsdp", None),
            P(None, "fsdp"),
            P("fsdp", None),
            P("fsdp", None),
            P(None, "fsdp", None),
            P("fsdp"),
            P("fsdp", None),
            P("fsdp"),
            P("fsdp"),
            P("fsdp", None),
            P("fsdp", None),
            P("fsdp", "dp", None),
        ),
        out_specs=(
            P("fsdp", "dp", None),
            P("fsdp", "dp", None),
            P("fsdp"),
            P("fsdp"),
            P("fsdp", None),
            P("fsdp", None),
            P("fsdp", None),
            P(None, "fsdp"),
            P("fsdp", None),
            P("fsdp", None),
            P(None, "fsdp", None),
            P("fsdp"),
            P("fsdp", None),
            P("fsdp"),
            P("fsdp"),
            P("fsdp", None),
            P("fsdp", None),
        ),
        check_vma=False,
    )
```
